256 devices in a mesh: dp: 32 (over x, z_lo, core), tensor: 8 (over z_hi, y).
Axes of the slice: x: 4, y: 4, z: 8 (z_hi: 2, z_lo: 4; z = z_hi * 4 + z_lo), core: 2. Of those that a mesh axis runs over, the one named last changes fastest.
Arguments:
- tokens: bfloat16 [512, 64, 1536], P('tensor', 'dp'), may hold values from -6 to 6
- cached_len: int32 [64], P('dp'), may hold values from 0 to 32768, as said below
- prompt_group: int32 [64], P('dp'), may hold values from 0 to 7, as said below
- attn_gain: float32 [1536], replicated, may hold values from 0.1 to 1.9
- w_query: bfloat16 [1536, 1536], P(None, 'tensor'), may hold values from -0.15625 to 0.15625
- key_matrix: bfloat16 [1536, 768], P(None, 'tensor'), may hold values from -0.15625 to 0.15625
- value_matrix: bfloat16 [1536, 768], P(None, 'tensor'), may hold values from -0.15625 to 0.15625
- w_out: bfloat16 [1536, 1536], P('tensor'), may hold values from -1.25 to 1.25
- window_cache_keys: bfloat16 [64, 4096, 768], P('dp', None, 'tensor'), may hold values from -400 to 400
- window_cache_values: bfloat16 [64, 4096, 768], P('dp', None, 'tensor'), may hold values from -6 to 6
- prompt_keys: bfloat16 [8, 4096, 768], P(None, 'dp', 'tensor'), may hold values from -6 to 6
- prompt_values: bfloat16 [8, 4096, 768], P(None, 'dp', 'tensor'), may hold values from -6 to 6
- mlp_gain: float32 [1536], replicated, may hold values from 0.1 to 1.9
- w_gate: bfloat16 [1536, 4096], P(None, 'tensor'), may hold values from -0.15625 to 0.15625
- w_up: bfloat16 [1536, 4096], P(None, 'tensor'), may hold values from -0.15625 to 0.15625
- w_down: bfloat16 [4096, 1536], P('tensor'), may hold values from -0.09375 to 0.09375
Outputs:
- output: bfloat16 [512, 64, 1536], P('tensor', 'dp')
The draws below stay inside these ranges and needn't reach their ends.
Inputs may be any that keep to these rules, and one draw needn't show every extreme that they name: `cached_len`: in each prompt group some request has no cached tokens, and exactly one request in all has 32768. `prompt_group`: every group holds 8 requests.
All inputs are finite; a program needn't handle non-finite values.
Results may differ from the reference program's by a relative error of at most 0.024.
Values may be sent and summed in bfloat16 or wider, within the bound.
A program may use at most 128 MiB of HBM per device.

```python
import math
import jax
import jax.numpy as jnp
from jax import lax

MODEL_WIDTH = 1536
QUERY_HEADS = 16
KEY_VALUE_HEADS = 8
HEAD_SIZE = 96
FF = 4096
FRESH_TOKENS = 512
WINDOW_SPAN = 4096
SINKS = 4
PROMPT_TOKENS = 4096
PROMPT_GROUPS = 8
MAXLEN = 32768
REQUEST_TOTAL = 64
N_TENSOR = 8


def request_plan(key):
    order = jax.random.permutation(jax.random.fold_in(key, 11), REQUEST_TOTAL).astype(jnp.int32)
    groups = (order % PROMPT_GROUPS).astype(jnp.int32)
    exponent = jax.random.randint(jax.random.fold_in(key, 12), (REQUEST_TOTAL,), 0, 16, dtype=jnp.int32)
    mantissa = jax.random.randint(jax.random.fold_in(key, 13), (REQUEST_TOTAL,), 0, MAXLEN, dtype=jnp.int32)
    shifted = jnp.right_shift(mantissa, 15 - exponent)
    lengths = jnp.where(order < PROMPT_GROUPS, 0, jnp.where(order == PROMPT_GROUPS, MAXLEN, shifted)).astype(jnp.int32)
    return (groups, lengths)


def draw_cached_len(key, part):
    return request_plan(key)[1]


def draw_prompt_group(key, part):
    return request_plan(key)[0]


def draw_window_cache_keys(key, part):
    rotary_base = jax.random.normal(jax.random.fold_in(key, 21), (REQUEST_TOTAL, WINDOW_SPAN, KEY_VALUE_HEADS * HEAD_SIZE), jnp.float32)
    return jnp.clip(rotary_base, -6.0, 6.0).astype(jnp.bfloat16)


def block_levels(key, dims, cuts, least, largest):
    loudness, own = 1.0, jax.random.fold_in(key, 6)
    for axis_at, shards_of in cuts:
        draws = jnp.exp(jax.random.uniform(jax.random.fold_in(own, axis_at), (shards_of,), jnp.float32, least / len(cuts), largest / len(cuts)))
        loudness = loudness * jnp.repeat(draws, dims[axis_at] // shards_of).reshape([-1 if axis == axis_at else 1 for axis in range(len(dims))])
    return loudness


def centred(key, extent, deviation, reach, cuts=(), kind=jnp.bfloat16):
    level = block_levels(key, extent, cuts, -0.22, 0.18) if cuts else 1.0
    result = jax.random.normal(key, extent, jnp.float32) * deviation * level
    return jnp.minimum(jnp.maximum(result, -reach), reach).astype(kind)


def setup_inputs(seed: int = 0) -> dict:
    arg_keys = jax.random.split(jax.random.key(seed), 17)
    tokens = centred(arg_keys[0], (FRESH_TOKENS, REQUEST_TOTAL, MODEL_WIDTH), 1.0, 6.0, ((0, 8), (1, 32)))
    cached_len = draw_cached_len(jax.random.fold_in(arg_keys[16], 71), 0)
    prompt_group = draw_prompt_group(jax.random.fold_in(arg_keys[16], 71), 0)
    attn_gain = jnp.clip(1.0 + 0.18 * jax.random.normal(arg_keys[3], (MODEL_WIDTH,), jnp.float32), 0.1, 1.9)
    w_query = centred(arg_keys[4], (MODEL_WIDTH, QUERY_HEADS * HEAD_SIZE), MODEL_WIDTH ** -0.5, 0.15625, ((1, 8),))
    key_matrix = centred(arg_keys[5], (MODEL_WIDTH, KEY_VALUE_HEADS * HEAD_SIZE), MODEL_WIDTH ** -0.5, 0.15625, ((1, 8),))
    value_matrix = centred(arg_keys[6], (MODEL_WIDTH, KEY_VALUE_HEADS * HEAD_SIZE), MODEL_WIDTH ** -0.5, 0.15625, ((1, 8),))
    w_out = centred(arg_keys[7], (QUERY_HEADS * HEAD_SIZE, MODEL_WIDTH), (QUERY_HEADS * HEAD_SIZE // 64) ** -0.5, 1.25, ((0, 8),))
    window_cache_keys = draw_window_cache_keys(jax.random.fold_in(arg_keys[16], 71), 0)
    window_cache_values = centred(arg_keys[9], (REQUEST_TOTAL, WINDOW_SPAN, KEY_VALUE_HEADS * HEAD_SIZE), 1.0, 6.0, ((0, 32), (2, 8)))
    prompt_keys = centred(arg_keys[10], (PROMPT_GROUPS, PROMPT_TOKENS, KEY_VALUE_HEADS * HEAD_SIZE), 1.0, 6.0, ((1, 32), (2, 8)))
    prompt_values = centred(arg_keys[11], (PROMPT_GROUPS, PROMPT_TOKENS, KEY_VALUE_HEADS * HEAD_SIZE), 1.0, 6.0, ((1, 32), (2, 8)))
    mlp_gain = jnp.clip(1.0 + 0.18 * jax.random.normal(arg_keys[12], (MODEL_WIDTH,), jnp.float32), 0.1, 1.9)
    w_gate = centred(arg_keys[13], (MODEL_WIDTH, FF), MODEL_WIDTH ** -0.5, 0.15625, ((1, 8),))
    w_up = centred(arg_keys[14], (MODEL_WIDTH, FF), MODEL_WIDTH ** -0.5, 0.15625, ((1, 8),))
    w_down = centred(arg_keys[15], (FF, MODEL_WIDTH), FF ** -0.5, 0.09375, ((0, 8),))
    return {"tokens": tokens, "cached_len": cached_len, "prompt_group": prompt_group, "attn_gain": attn_gain, "w_query": w_query, "key_matrix": key_matrix, "value_matrix": value_matrix, "w_out": w_out, "window_cache_keys": window_cache_keys, "window_cache_values": window_cache_values, "prompt_keys": prompt_keys, "prompt_values": prompt_values, "mlp_gain": mlp_gain, "w_gate": w_gate, "w_up": w_up, "w_down": w_down}


rope_base = 10000.0
epsilon = 1e-05

def norm_rows(values, gain_vec):
    widened = values.astype(jnp.float32)
    factor = lax.rsqrt(lax.optimization_barrier(jnp.mean(widened * widened, axis=-1, keepdims=True)) + epsilon)
    return (widened * factor * gain_vec).astype(jnp.bfloat16)

def rotate(values, positions):
    half_dim = values.shape[-1] // 2
    frequency = rope_base ** (-2.0 * jnp.arange(half_dim, dtype=jnp.float32) / values.shape[-1])
    angles = positions.astype(jnp.float32)[..., None, None] * frequency
    cosine = jnp.cos(angles)
    sine_part = jnp.sin(angles)
    first_half = values[..., :half_dim]
    second_half = values[..., half_dim:]
    return jnp.concatenate([first_half * cosine - second_half * sine_part, second_half * cosine + first_half * sine_part], axis=-1)

def group_sum(left_side, right_side, pieces):
    column_count = left_side.shape[1] // pieces
    summed = jnp.zeros((left_side.shape[0], right_side.shape[1]), jnp.float32)
    for part_index in range(pieces):
        partial_value = jnp.dot(left_side[:, part_index * column_count:(part_index + 1) * column_count], right_side[part_index * column_count:(part_index + 1) * column_count], preferred_element_type=jnp.float32)
        partial_value = lax.optimization_barrier(partial_value.astype(jnp.bfloat16))
        summed = summed + partial_value.astype(jnp.float32)
    return summed

def reference(tokens, cached_len, prompt_group, attn_gain, w_query, key_matrix, value_matrix, w_out, window_cache_keys, window_cache_values, prompt_keys, prompt_values, mlp_gain, w_gate, w_up, w_down):
    query_group_width = QUERY_HEADS // KEY_VALUE_HEADS
    score_scale = 1.0 / math.sqrt(HEAD_SIZE)
    normed = norm_rows(tokens, attn_gain)
    flattened_rows = normed.reshape(FRESH_TOKENS * REQUEST_TOTAL, MODEL_WIDTH)
    queries = jnp.dot(flattened_rows, w_query, preferred_element_type=jnp.float32).reshape(FRESH_TOKENS, REQUEST_TOTAL, QUERY_HEADS, HEAD_SIZE)
    fresh_keys = jnp.dot(flattened_rows, key_matrix, preferred_element_type=jnp.float32).reshape(FRESH_TOKENS, REQUEST_TOTAL, KEY_VALUE_HEADS, HEAD_SIZE)
    fresh_values = jnp.dot(flattened_rows, value_matrix, preferred_element_type=jnp.float32).astype(jnp.bfloat16).reshape(FRESH_TOKENS, REQUEST_TOTAL, KEY_VALUE_HEADS, HEAD_SIZE)
    positions = PROMPT_TOKENS + cached_len[None, :] + jnp.arange(FRESH_TOKENS, dtype=jnp.int32)[:, None]
    queries = rotate(queries, positions).astype(jnp.bfloat16)
    fresh_keys = rotate(fresh_keys, positions).astype(jnp.bfloat16)

    def one_request(request_index):
        length = lax.dynamic_index_in_dim(cached_len, request_index, 0, keepdims=False)
        prompt_group_index = lax.dynamic_index_in_dim(prompt_group, request_index, 0, keepdims=False)
        request_query = lax.dynamic_index_in_dim(queries, request_index, 1, keepdims=False)
        own_key = lax.dynamic_index_in_dim(fresh_keys, request_index, 1, keepdims=False)
        own_value = lax.dynamic_index_in_dim(fresh_values, request_index, 1, keepdims=False)
        earlier_key = lax.dynamic_index_in_dim(window_cache_keys, request_index, 0, keepdims=False).reshape(WINDOW_SPAN, KEY_VALUE_HEADS, HEAD_SIZE)
        earlier_value = lax.dynamic_index_in_dim(window_cache_values, request_index, 0, keepdims=False).reshape(WINDOW_SPAN, KEY_VALUE_HEADS, HEAD_SIZE)
        common_prompt_key = lax.dynamic_index_in_dim(prompt_keys, prompt_group_index, 0, keepdims=False).reshape(PROMPT_TOKENS, KEY_VALUE_HEADS, HEAD_SIZE)
        common_prompt_value = lax.dynamic_index_in_dim(prompt_values, prompt_group_index, 0, keepdims=False).reshape(PROMPT_TOKENS, KEY_VALUE_HEADS, HEAD_SIZE)
        keys_all = jnp.concatenate([common_prompt_key, earlier_key, own_key], axis=0)
        values_all = jnp.concatenate([common_prompt_value, earlier_value, own_value], axis=0)
        row_ids = jnp.arange(FRESH_TOKENS, dtype=jnp.int32)[:, None]
        prefix_ids = jnp.arange(PROMPT_TOKENS, dtype=jnp.int32)[None, :]
        slot_ids = jnp.arange(WINDOW_SPAN, dtype=jnp.int32)[None, :]
        col_ids = jnp.arange(FRESH_TOKENS, dtype=jnp.int32)[None, :]
        horizon = PROMPT_TOKENS + length + row_ids - WINDOW_SPAN
        prefix_seen = (prefix_ids < SINKS) | (prefix_ids > horizon)
        window_seen = (slot_ids >= WINDOW_SPAN - length) & (slot_ids > row_ids)
        span_seen = col_ids <= row_ids
        visible = jnp.concatenate([prefix_seen, window_seen, span_seen], axis=1)
        grouped_queries = request_query.reshape(FRESH_TOKENS, KEY_VALUE_HEADS, query_group_width, HEAD_SIZE)

        def single_head(head_index):
            query_head = lax.dynamic_index_in_dim(grouped_queries, head_index, 1, keepdims=False).astype(jnp.float32)
            key_head = lax.dynamic_index_in_dim(keys_all, head_index, 1, keepdims=False).astype(jnp.float32)
            value_head = lax.dynamic_index_in_dim(values_all, head_index, 1, keepdims=False).astype(jnp.float32)
            scores = jnp.einsum('igd,kd->gik', query_head, key_head) * score_scale
            scores = jnp.where(visible[None], scores, -jnp.inf)
            row_peak = lax.optimization_barrier(jnp.max(scores, axis=-1, keepdims=True))
            weights = jnp.exp(scores - row_peak)
            summed = lax.optimization_barrier(jnp.sum(weights, axis=-1, keepdims=True))
            rounded = lax.optimization_barrier(weights.astype(jnp.bfloat16)).astype(jnp.float32)
            blended = jnp.einsum('gik,kd->gid', rounded, value_head) / summed
            return blended
        head_outputs = lax.map(single_head, jnp.arange(KEY_VALUE_HEADS, dtype=jnp.int32))
        return head_outputs.transpose(2, 0, 1, 3).reshape(FRESH_TOKENS, QUERY_HEADS * HEAD_SIZE).astype(jnp.bfloat16)
    attended = lax.map(one_request, jnp.arange(REQUEST_TOTAL, dtype=jnp.int32))
    attended = attended.transpose(1, 0, 2).reshape(FRESH_TOKENS * REQUEST_TOTAL, QUERY_HEADS * HEAD_SIZE)
    attn_part = group_sum(attended, w_out, N_TENSOR).reshape(FRESH_TOKENS, REQUEST_TOTAL, MODEL_WIDTH)
    residual = (tokens.astype(jnp.float32) + attn_part).astype(jnp.bfloat16)
    normed_mlp = norm_rows(residual, mlp_gain).reshape(FRESH_TOKENS * REQUEST_TOTAL, MODEL_WIDTH)
    gate_part = jnp.dot(normed_mlp, w_gate, preferred_element_type=jnp.float32)
    up_part = jnp.dot(normed_mlp, w_up, preferred_element_type=jnp.float32)
    hidden = (jax.nn.silu(gate_part) * up_part).astype(jnp.bfloat16)
    mlp_part = group_sum(hidden, w_down, N_TENSOR).reshape(FRESH_TOKENS, REQUEST_TOTAL, MODEL_WIDTH)
    return (residual.astype(jnp.float32) + mlp_part).astype(jnp.bfloat16)
```

```python
import math

import jax
import jax.numpy as jnp
from jax import lax
from jax.sharding import PartitionSpec as P

MODEL_WIDTH = 1536
HEAD_SIZE = 96
FRESH_TOKENS = 512
WINDOW_SPAN = 4096
SINKS = 4
PROMPT_TOKENS = 4096


rope_base = 10000.0
epsilon = 1e-05
far_below = -1e30


def norm_rows(values, gain_vec):
    widened = values.astype(jnp.float32)
    factor = lax.rsqrt(jnp.mean(widened * widened, axis=-1, keepdims=True) + epsilon)
    return (widened * factor * gain_vec).astype(jnp.bfloat16)


def rotate(values, positions):
    half_dim = values.shape[-1] // 2
    frequency = rope_base ** (-2.0 * jnp.arange(half_dim, dtype=jnp.float32) / values.shape[-1])
    angles = positions.astype(jnp.float32)[..., None, None] * frequency
    cosine = jnp.cos(angles)
    sine_part = jnp.sin(angles)
    first_half = values[..., :half_dim]
    second_half = values[..., half_dim:]
    return jnp.concatenate(
        [
            first_half * cosine - second_half * sine_part,
            second_half * cosine + first_half * sine_part,
        ],
        axis=-1,
    )


def absorb(soft_state, queries, key_block, value_block, visible, score_scale):
    row_peak, row_sum, accumulated = soft_state
    scores = (
        jnp.einsum("irhgd,rkhd->rhgik", queries, key_block, preferred_element_type=jnp.float32)
        * score_scale
    )
    scores = jnp.where(visible[:, None, None], scores, -jnp.inf)
    new_peak = jnp.maximum(row_peak, jnp.max(scores, axis=-1))
    factor = jnp.exp(row_peak - new_peak)
    weights = jnp.exp(scores - new_peak[..., None])
    blended = jnp.einsum(
        "rhgik,rkhd->rhgid",
        weights.astype(jnp.bfloat16),
        value_block,
        preferred_element_type=jnp.float32,
    )
    return (
        new_peak,
        row_sum * factor + jnp.sum(weights, axis=-1),
        accumulated * factor[..., None] + blended,
    )


def shared_block(soft_state, pieces, queries, selector, horizon, score_scale):
    key_piece, value_piece = pieces
    row_count = key_piece.shape[1]
    key_heads = key_piece.shape[2] // HEAD_SIZE
    local_reqs = queries.shape[1]
    picked_keys = key_piece.reshape(local_reqs, row_count, key_heads, HEAD_SIZE)
    picked_values = value_piece.reshape(local_reqs, row_count, key_heads, HEAD_SIZE)
    block_len = math.gcd(row_count, FRESH_TOKENS)

    def block_step(running, block_index):
        block_start = block_index * block_len
        key_block = lax.dynamic_slice_in_dim(picked_keys, block_start, block_len, 1)
        value_block = lax.dynamic_slice_in_dim(picked_values, block_start, block_len, 1)
        prompt_pos = block_start + jnp.arange(block_len, dtype=jnp.int32)
        visible = (prompt_pos[None, None, :] < SINKS) | (
            prompt_pos[None, None, :] > horizon[:, :, None]
        )
        return (absorb(running, queries, key_block, value_block, visible, score_scale), None)

    return lax.scan(block_step, soft_state, jnp.arange(row_count // block_len, dtype=jnp.int32))[0]


def gather_rows(piece):
    across = lax.all_gather(piece, "zh", axis=0, tiled=False)
    both = lax.all_gather(across, "y", axis=0, tiled=False)
    both = jnp.swapaxes(both, 0, 1)
    return both.reshape((-1,) + piece.shape[1:])


def scatter_rows(full):
    rows = full.shape[0]
    zh_size = lax.axis_size("zh")
    y_size = lax.axis_size("y")
    split = full.reshape((zh_size, y_size, rows // (zh_size * y_size)) + full.shape[1:])
    part = lax.psum_scatter(split, "y", scatter_dimension=1, tiled=False)
    return lax.psum_scatter(part, "zh", scatter_dimension=0, tiled=False)


def prompt_for_requests(prompt_keys, prompt_values, prompt_group):
    every_group = lax.all_gather(prompt_group, "dp", axis=0, tiled=True)
    dp_size = lax.axis_size("dp")
    wanted = every_group.reshape(dp_size, -1)
    both = jnp.stack([prompt_keys, prompt_values], axis=1)
    outgoing = jnp.take(both, wanted, axis=0)
    incoming = lax.all_to_all(outgoing, "dp", 0, 0, tiled=False)
    local_reqs = wanted.shape[1]
    rows = prompt_keys.shape[1]
    incoming = incoming.transpose(1, 2, 0, 3, 4)
    incoming = incoming.reshape(local_reqs, 2, dp_size * rows, prompt_keys.shape[2])
    return incoming[:, 0], incoming[:, 1]


def body(
    tokens,
    cached_len,
    prompt_group,
    attn_gain,
    w_query,
    key_matrix,
    value_matrix,
    w_out,
    window_cache_keys,
    window_cache_values,
    prompt_keys,
    prompt_values,
    mlp_gain,
    w_gate,
    w_up,
    w_down,
):
    local_rows = tokens.shape[0]
    local_reqs = tokens.shape[1]
    query_cols = w_query.shape[1]
    key_cols = key_matrix.shape[1]
    hidden_cols = w_gate.shape[1]
    key_heads = key_cols // HEAD_SIZE
    query_group_width = query_cols // key_cols
    score_scale = 1.0 / math.sqrt(HEAD_SIZE)
    source = norm_rows(tokens, attn_gain)
    offset = 0
    row_piece = gather_rows(source)
    row_count = row_piece.shape[0]
    normed = row_piece
    flattened_rows = normed.reshape(row_count * local_reqs, MODEL_WIDTH)
    positions = (
        PROMPT_TOKENS + cached_len[None, :] + jnp.arange(row_count, dtype=jnp.int32)[:, None]
    )
    project_queries = jnp.dot(flattened_rows, w_query, preferred_element_type=jnp.float32).reshape(
        row_count, local_reqs, query_cols // HEAD_SIZE, HEAD_SIZE
    )
    fresh_keys = jnp.dot(flattened_rows, key_matrix, preferred_element_type=jnp.float32).reshape(
        row_count, local_reqs, key_heads, HEAD_SIZE
    )
    fresh_values = (
        jnp.dot(flattened_rows, value_matrix, preferred_element_type=jnp.float32)
        .astype(jnp.bfloat16)
        .reshape(row_count, local_reqs, key_cols)
    )
    project_queries = (
        rotate(project_queries, positions)
        .astype(jnp.bfloat16)
        .reshape(row_count, local_reqs, query_cols)
    )
    fresh_keys = (
        rotate(fresh_keys, positions).astype(jnp.bfloat16).reshape(row_count, local_reqs, key_cols)
    )
    gathered = jnp.concatenate([project_queries, fresh_keys, fresh_values], axis=2)
    queries = gathered[:, :, offset : offset + query_cols].reshape(
        FRESH_TOKENS, local_reqs, key_heads, query_group_width, HEAD_SIZE
    )
    own_keys = jnp.swapaxes(
        gathered[:, :, offset + query_cols : offset + query_cols + key_cols], 0, 1
    ).reshape(local_reqs, FRESH_TOKENS, key_heads, HEAD_SIZE)
    own_values = jnp.swapaxes(
        gathered[:, :, offset + query_cols + key_cols : offset + query_cols + 2 * key_cols], 0, 1
    ).reshape(local_reqs, FRESH_TOKENS, key_heads, HEAD_SIZE)
    state_shape = (local_reqs, key_heads, query_group_width, FRESH_TOKENS)
    soft_state = (
        jnp.full(state_shape, far_below, jnp.float32),
        jnp.zeros(state_shape, jnp.float32),
        jnp.zeros(state_shape + (HEAD_SIZE,), jnp.float32),
    )
    row_ids = jnp.arange(FRESH_TOKENS, dtype=jnp.int32)
    causal = jnp.broadcast_to(
        row_ids[None, None, :] <= row_ids[None, :, None], (local_reqs, FRESH_TOKENS, FRESH_TOKENS)
    )
    soft_state = absorb(soft_state, queries, own_keys, own_values, causal, score_scale)
    past_keys = window_cache_keys.reshape(local_reqs, WINDOW_SPAN, key_heads, HEAD_SIZE)
    past_values = window_cache_values.reshape(local_reqs, WINDOW_SPAN, key_heads, HEAD_SIZE)

    def window_step(running, block_index):
        block_start = block_index * FRESH_TOKENS
        key_block = lax.dynamic_slice_in_dim(past_keys, block_start, FRESH_TOKENS, 1)
        value_block = lax.dynamic_slice_in_dim(past_values, block_start, FRESH_TOKENS, 1)
        slot_ids = block_start + row_ids
        visible = (slot_ids[None, None, :] >= WINDOW_SPAN - cached_len[:, None, None]) & (
            slot_ids[None, None, :] > row_ids[None, :, None]
        )
        return (absorb(running, queries, key_block, value_block, visible, score_scale), None)

    soft_state = lax.scan(
        window_step, soft_state, jnp.arange(WINDOW_SPAN // FRESH_TOKENS, dtype=jnp.int32)
    )[0]
    horizon = PROMPT_TOKENS + cached_len[:, None] + row_ids[None, :] - WINDOW_SPAN
    soft_state = shared_block(
        soft_state,
        prompt_for_requests(prompt_keys, prompt_values, prompt_group),
        queries,
        prompt_group,
        horizon,
        score_scale,
    )
    row_peak, row_sum, accumulated = soft_state
    attended = (accumulated / row_sum[..., None]).astype(jnp.bfloat16)
    attended = attended.transpose(3, 0, 1, 2, 4).reshape(FRESH_TOKENS, local_reqs, query_cols)
    picked = attended
    attn_part = scatter_rows(
        jnp.dot(
            picked.reshape(FRESH_TOKENS * local_reqs, query_cols),
            w_out,
            preferred_element_type=jnp.float32,
        )
        .reshape(FRESH_TOKENS, local_reqs, MODEL_WIDTH)
        .astype(jnp.bfloat16)
    ).astype(jnp.float32)
    residual = (tokens.astype(jnp.float32) + attn_part).astype(jnp.bfloat16)
    row_piece = gather_rows(norm_rows(residual, mlp_gain))
    row_count = row_piece.shape[0]
    flattened_rows = row_piece.reshape(row_count * local_reqs, MODEL_WIDTH)
    gate_part = jnp.dot(flattened_rows, w_gate, preferred_element_type=jnp.float32)
    up_part = jnp.dot(flattened_rows, w_up, preferred_element_type=jnp.float32)
    hidden = (
        (jax.nn.silu(gate_part) * up_part)
        .astype(jnp.bfloat16)
        .reshape(row_count, local_reqs, hidden_cols)
    )
    picked = hidden
    mlp_part = scatter_rows(
        jnp.dot(
            picked.reshape(FRESH_TOKENS * local_reqs, hidden_cols),
            w_down,
            preferred_element_type=jnp.float32,
        )
        .reshape(FRESH_TOKENS, local_reqs, MODEL_WIDTH)
        .astype(jnp.bfloat16)
    ).astype(jnp.float32)
    return (residual.astype(jnp.float32) + mlp_part).astype(jnp.bfloat16)


def solution(mesh):
    zh_size = 2
    split_mesh = jax.sharding.Mesh(
        mesh.devices.reshape(mesh.devices.shape[0], zh_size, -1), ("dp", "zh", "y")
    )
    rows = ("zh", "y")
    in_specs = (
        P(rows, "dp", None),
        P("dp"),
        P("dp"),
        P(),
        P(None, rows),
        P(None, rows),
        P(None, rows),
        P(rows, None),
        P("dp", None, rows),
        P("dp", None, rows),
        P(None, "dp", rows),
        P(None, "dp", rows),
        P(),
        P(None, rows),
        P(None, rows),
        P(rows, None),
    )
    out_specs = P(rows, "dp", None)
    return jax.shard_map(
        body, mesh=split_mesh, in_specs=in_specs, out_specs=out_specs, check_vma=False
    )
```

```python
import math

import jax
import jax.numpy as jnp
from jax import lax
from jax.sharding import PartitionSpec as P
from jax.experimental import pallas as pl
from jax.experimental.pallas import tpu as pltpu

MODEL_WIDTH = 1536
HEAD_SIZE = 96
FRESH_TOKENS = 512
WINDOW_SPAN = 4096
SINKS = 4
PROMPT_TOKENS = 4096


rope_base = 10000.0
epsilon = 1e-05
far_below = -1e30


def norm_rows(values, gain_vec):
    widened = values.astype(jnp.float32)
    factor = lax.rsqrt(jnp.mean(widened * widened, axis=-1, keepdims=True) + epsilon)
    return (widened * factor * gain_vec).astype(jnp.bfloat16)


def rotate(values, positions):
    half_dim = values.shape[-1] // 2
    frequency = rope_base ** (-2.0 * jnp.arange(half_dim, dtype=jnp.float32) / values.shape[-1])
    angles = positions.astype(jnp.float32)[..., None, None] * frequency
    cosine = jnp.cos(angles)
    sine_part = jnp.sin(angles)
    first_half = values[..., :half_dim]
    second_half = values[..., half_dim:]
    return jnp.concatenate(
        [
            first_half * cosine - second_half * sine_part,
            second_half * cosine + first_half * sine_part,
        ],
        axis=-1,
    )


KEY_BLOCK = 512


def attention_kernel(
    length_ref, q_ref, pk_ref, pv_ref, wk_ref, wv_ref, nk_ref, nv_ref, o_ref, peak, total, acc
):
    request = pl.program_id(0)
    block = pl.program_id(1)
    length = length_ref[request]
    prompt_blocks = PROMPT_TOKENS // KEY_BLOCK
    window_blocks = WINDOW_SPAN // KEY_BLOCK
    row_count = q_ref.shape[1]
    score_scale = 1.0 / math.sqrt(HEAD_SIZE)

    @pl.when(block == 0)
    def _():
        peak[...] = jnp.full(peak.shape, far_below, jnp.float32)
        total[...] = jnp.zeros(total.shape, jnp.float32)
        acc[...] = jnp.zeros(acc.shape, jnp.float32)

    rows = lax.rem(lax.broadcasted_iota(jnp.int32, (row_count, KEY_BLOCK), 0), FRESH_TOKENS)
    cols = lax.broadcasted_iota(jnp.int32, (row_count, KEY_BLOCK), 1)

    def absorb(k_ref, v_ref, visible):
        scores = (
            lax.dot_general(
                q_ref[0],
                k_ref[0],
                (((1,), (1,)), ((), ())),
                preferred_element_type=jnp.float32,
            )
            * score_scale
        )
        scores = jnp.where(visible, scores, -jnp.inf)
        old_peak = peak[...]
        new_peak = jnp.maximum(old_peak, jnp.max(scores, axis=-1, keepdims=True))
        factor = jnp.exp(old_peak - new_peak)
        weights = jnp.exp(scores - new_peak)
        total[...] = total[...] * factor + jnp.sum(weights, axis=-1, keepdims=True)
        acc[...] = acc[...] * factor + jnp.dot(
            weights.astype(jnp.bfloat16), v_ref[0], preferred_element_type=jnp.float32
        )
        peak[...] = new_peak

    prompt_start = block * KEY_BLOCK

    @pl.when(
        (block < prompt_blocks)
        & ((block == 0) | (prompt_start + KEY_BLOCK - 1 > length))
    )
    def _():
        spot = prompt_start + cols
        absorb(pk_ref, pv_ref, (spot < SINKS) | (spot > length + rows))

    window_start = (block - prompt_blocks) * KEY_BLOCK

    @pl.when(
        (block >= prompt_blocks)
        & (block < prompt_blocks + window_blocks)
        & (window_start + KEY_BLOCK - 1 >= WINDOW_SPAN - length)
    )
    def _():
        slot = window_start + cols
        absorb(wk_ref, wv_ref, (slot >= WINDOW_SPAN - length) & (slot > rows))

    @pl.when(block == prompt_blocks + window_blocks)
    def _():
        absorb(nk_ref, nv_ref, cols <= rows)
        o_ref[0] = (acc[...] / total[...]).astype(o_ref.dtype)


def attention(lengths, queries, prompt_k, prompt_v, window_k, window_v, new_k, new_v):
    local_reqs, row_count, width = queries.shape
    prompt_blocks = PROMPT_TOKENS // KEY_BLOCK
    window_blocks = WINDOW_SPAN // KEY_BLOCK
    steps = prompt_blocks + window_blocks + 1
    key_spec = lambda pick: pl.BlockSpec((1, KEY_BLOCK, width), pick)
    prompt_pick = lambda r, b, lens: (r, jnp.minimum(b, prompt_blocks - 1), 0)
    window_pick = lambda r, b, lens: (r, jnp.clip(b - prompt_blocks, 0, window_blocks - 1), 0)
    fixed_pick = lambda r, b, lens: (r, 0, 0)
    grid_spec = pltpu.PrefetchScalarGridSpec(
        num_scalar_prefetch=1,
        grid=(local_reqs, steps),
        in_specs=[
            pl.BlockSpec((1, row_count, width), fixed_pick),
            key_spec(prompt_pick),
            key_spec(prompt_pick),
            key_spec(window_pick),
            key_spec(window_pick),
            key_spec(fixed_pick),
            key_spec(fixed_pick),
        ],
        out_specs=pl.BlockSpec((1, row_count, width), fixed_pick),
        scratch_shapes=[
            pltpu.VMEM((row_count, 1), jnp.float32),
            pltpu.VMEM((row_count, 1), jnp.float32),
            pltpu.VMEM((row_count, width), jnp.float32),
        ],
    )
    keys_total = PROMPT_TOKENS + WINDOW_SPAN + FRESH_TOKENS
    flops = 4 * local_reqs * row_count * keys_total * width
    return pl.pallas_call(
        attention_kernel,
        grid_spec=grid_spec,
        out_shape=jax.ShapeDtypeStruct(queries.shape, jnp.bfloat16),
        cost_estimate=pl.CostEstimate(
            flops=flops,
            transcendentals=local_reqs * row_count * keys_total,
            bytes_accessed=4 * local_reqs * keys_total * width * 2,
        ),
    )(lengths, queries, prompt_k, prompt_v, window_k, window_v, new_k, new_v)


def gather_rows(piece):
    across = lax.all_gather(piece, "zh", axis=0, tiled=False)
    both = lax.all_gather(across, "y", axis=0, tiled=False)
    both = jnp.swapaxes(both, 0, 1)
    return both.reshape((-1,) + piece.shape[1:])


def scatter_rows(full):
    rows = full.shape[0]
    zh_size = lax.axis_size("zh")
    y_size = lax.axis_size("y")
    split = full.reshape((zh_size, y_size, rows // (zh_size * y_size)) + full.shape[1:])
    part = lax.psum_scatter(split, "y", scatter_dimension=1, tiled=False)
    return lax.psum_scatter(part, "zh", scatter_dimension=0, tiled=False)


def prompt_for_requests(prompt_keys, prompt_values, prompt_group):
    dp_size = lax.axis_size("dp")
    wanted = lax.all_to_all(
        jnp.broadcast_to(prompt_group[None], (dp_size,) + prompt_group.shape), "dp", 0, 0, tiled=False
    )
    both = jnp.stack([prompt_keys, prompt_values], axis=1)
    outgoing = jnp.take(both, wanted, axis=0)
    incoming = lax.all_to_all(outgoing, "dp", 0, 0, tiled=False)
    local_reqs = wanted.shape[1]
    rows = prompt_keys.shape[1]
    incoming = incoming.transpose(1, 2, 0, 3, 4)
    incoming = incoming.reshape(local_reqs, 2, dp_size * rows, prompt_keys.shape[2])
    return incoming[:, 0], incoming[:, 1]


def body(
    tokens,
    cached_len,
    prompt_group,
    attn_gain,
    w_query,
    key_matrix,
    value_matrix,
    w_out,
    window_cache_keys,
    window_cache_values,
    prompt_keys,
    prompt_values,
    mlp_gain,
    w_gate,
    w_up,
    w_down,
):
    local_rows = tokens.shape[0]
    local_reqs = tokens.shape[1]
    query_cols = w_query.shape[1]
    key_cols = key_matrix.shape[1]
    hidden_cols = w_gate.shape[1]
    key_heads = key_cols // HEAD_SIZE
    query_group_width = query_cols // key_cols
    score_scale = 1.0 / math.sqrt(HEAD_SIZE)
    source = norm_rows(tokens, attn_gain)
    offset = 0
    row_piece = gather_rows(source)
    row_count = row_piece.shape[0]
    normed = row_piece
    flattened_rows = normed.reshape(row_count * local_reqs, MODEL_WIDTH)
    positions = (
        PROMPT_TOKENS + cached_len[None, :] + jnp.arange(row_count, dtype=jnp.int32)[:, None]
    )
    project_queries = jnp.dot(flattened_rows, w_query, preferred_element_type=jnp.float32).reshape(
        row_count, local_reqs, query_cols // HEAD_SIZE, HEAD_SIZE
    )
    fresh_keys = jnp.dot(flattened_rows, key_matrix, preferred_element_type=jnp.float32).reshape(
        row_count, local_reqs, key_heads, HEAD_SIZE
    )
    fresh_values = (
        jnp.dot(flattened_rows, value_matrix, preferred_element_type=jnp.float32)
        .astype(jnp.bfloat16)
        .reshape(row_count, local_reqs, key_cols)
    )
    project_queries = (
        rotate(project_queries, positions)
        .astype(jnp.bfloat16)
        .reshape(row_count, local_reqs, query_cols)
    )
    fresh_keys = (
        rotate(fresh_keys, positions).astype(jnp.bfloat16).reshape(row_count, local_reqs, key_cols)
    )
    query_heads = query_cols // HEAD_SIZE
    queries = (
        project_queries.reshape(row_count, local_reqs, query_heads, HEAD_SIZE)
        .transpose(1, 2, 0, 3)
        .reshape(local_reqs, query_heads * row_count, HEAD_SIZE)
    )
    own_keys = jnp.swapaxes(fresh_keys, 0, 1)
    own_values = jnp.swapaxes(fresh_values, 0, 1)
    prompt_k, prompt_v = prompt_for_requests(prompt_keys, prompt_values, prompt_group)
    attended = attention(
        cached_len, queries, prompt_k, prompt_v, window_cache_keys, window_cache_values, own_keys, own_values
    )
    attended = (
        attended.reshape(local_reqs, query_heads, row_count, HEAD_SIZE)
        .transpose(2, 0, 1, 3)
        .reshape(row_count, local_reqs, query_cols)
    )
    picked = attended
    attn_part = scatter_rows(
        jnp.dot(
            picked.reshape(FRESH_TOKENS * local_reqs, query_cols),
            w_out,
            preferred_element_type=jnp.float32,
        )
        .reshape(FRESH_TOKENS, local_reqs, MODEL_WIDTH)
        .astype(jnp.bfloat16)
    ).astype(jnp.float32)
    residual = (tokens.astype(jnp.float32) + attn_part).astype(jnp.bfloat16)
    row_piece = gather_rows(norm_rows(residual, mlp_gain))
    row_count = row_piece.shape[0]
    flattened_rows = row_piece.reshape(row_count * local_reqs, MODEL_WIDTH)
    gate_part = jnp.dot(flattened_rows, w_gate, preferred_element_type=jnp.float32)
    up_part = jnp.dot(flattened_rows, w_up, preferred_element_type=jnp.float32)
    hidden = (
        (jax.nn.silu(gate_part) * up_part)
        .astype(jnp.bfloat16)
        .reshape(row_count, local_reqs, hidden_cols)
    )
    picked = hidden
    mlp_part = scatter_rows(
        jnp.dot(
            picked.reshape(FRESH_TOKENS * local_reqs, hidden_cols),
            w_down,
            preferred_element_type=jnp.float32,
        )
        .reshape(FRESH_TOKENS, local_reqs, MODEL_WIDTH)
        .astype(jnp.bfloat16)
    ).astype(jnp.float32)
    return (residual.astype(jnp.float32) + mlp_part).astype(jnp.bfloat16)


def solution(mesh):
    zh_size = 2
    split_mesh = jax.sharding.Mesh(
        mesh.devices.reshape(mesh.devices.shape[0], zh_size, -1), ("dp", "zh", "y")
    )
    rows = ("zh", "y")
    in_specs = (
        P(rows, "dp", None),
        P("dp"),
        P("dp"),
        P(),
        P(None, rows),
        P(None, rows),
        P(None, rows),
        P(rows, None),
        P("dp", None, rows),
        P("dp", None, rows),
        P(None, "dp", rows),
        P(None, "dp", rows),
        P(),
        P(None, rows),
        P(None, rows),
        P(rows, None),
    )
    out_specs = P(rows, "dp", None)
    return jax.shard_map(
        body, mesh=split_mesh, in_specs=in_specs, out_specs=out_specs, check_vma=False
    )
```

```python
import math

import jax
import jax.numpy as jnp
from jax import lax
from jax.sharding import PartitionSpec as P
from jax.experimental import pallas as pl
from jax.experimental.pallas import tpu as pltpu

MODEL_WIDTH = 1536
HEAD_SIZE = 96
FRESH_TOKENS = 512
WINDOW_SPAN = 4096
SINKS = 4
PROMPT_TOKENS = 4096


rope_base = 10000.0
epsilon = 1e-05
far_below = -1e30


def norm_rows(values, gain_vec):
    widened = values.astype(jnp.float32)
    factor = lax.rsqrt(jnp.mean(widened * widened, axis=-1, keepdims=True) + epsilon)
    return (widened * factor * gain_vec).astype(jnp.bfloat16)


def rotate(values, positions):
    half_dim = values.shape[-1] // 2
    frequency = rope_base ** (-2.0 * jnp.arange(half_dim, dtype=jnp.float32) / values.shape[-1])
    angles = positions.astype(jnp.float32)[..., None, None] * frequency
    cosine = jnp.cos(angles)
    sine_part = jnp.sin(angles)
    first_half = values[..., :half_dim]
    second_half = values[..., half_dim:]
    return jnp.concatenate(
        [
            first_half * cosine - second_half * sine_part,
            second_half * cosine + first_half * sine_part,
        ],
        axis=-1,
    )


KEY_BLOCK = 512


def attention_kernel(
    length_ref, q_ref, pk_ref, pv_ref, wk_ref, wv_ref, nk_ref, nv_ref, o_ref, peak, total, acc
):
    request = pl.program_id(0)
    block = pl.program_id(1)
    length = length_ref[request]
    prompt_blocks = PROMPT_TOKENS // KEY_BLOCK
    window_blocks = WINDOW_SPAN // KEY_BLOCK
    row_count = q_ref.shape[1]
    score_scale = 1.0 / math.sqrt(HEAD_SIZE)

    @pl.when(block == 0)
    def _():
        peak[...] = jnp.full(peak.shape, far_below, jnp.float32)
        total[...] = jnp.zeros(total.shape, jnp.float32)
        acc[...] = jnp.zeros(acc.shape, jnp.float32)

    rows = lax.rem(lax.broadcasted_iota(jnp.int32, (row_count, KEY_BLOCK), 0), FRESH_TOKENS)
    cols = lax.broadcasted_iota(jnp.int32, (row_count, KEY_BLOCK), 1)

    def absorb(k_ref, v_ref, visible):
        scores = (
            lax.dot_general(
                q_ref[0],
                k_ref[0],
                (((1,), (1,)), ((), ())),
                preferred_element_type=jnp.float32,
            )
            * score_scale
        )
        scores = jnp.where(visible, scores, -jnp.inf)
        old_peak = peak[...]
        new_peak = jnp.maximum(old_peak, jnp.max(scores, axis=-1, keepdims=True))
        factor = jnp.exp(old_peak - new_peak)
        weights = jnp.exp(scores - new_peak)
        total[...] = total[...] * factor + jnp.sum(weights, axis=-1, keepdims=True)
        acc[...] = acc[...] * factor + jnp.dot(
            weights.astype(jnp.bfloat16), v_ref[0], preferred_element_type=jnp.float32
        )
        peak[...] = new_peak

    prompt_start = block * KEY_BLOCK

    @pl.when(
        (block < prompt_blocks)
        & ((block == 0) | (prompt_start + KEY_BLOCK - 1 > length))
    )
    def _():
        spot = prompt_start + cols
        absorb(pk_ref, pv_ref, (spot < SINKS) | (spot > length + rows))

    window_start = (block - prompt_blocks) * KEY_BLOCK

    @pl.when(
        (block >= prompt_blocks)
        & (block < prompt_blocks + window_blocks)
        & (window_start + KEY_BLOCK - 1 >= WINDOW_SPAN - length)
    )
    def _():
        slot = window_start + cols
        absorb(wk_ref, wv_ref, (slot >= WINDOW_SPAN - length) & (slot > rows))

    @pl.when(block == prompt_blocks + window_blocks)
    def _():
        absorb(nk_ref, nv_ref, cols <= rows)
        o_ref[0] = (acc[...] / total[...]).astype(o_ref.dtype)


def attention(lengths, queries, prompt_k, prompt_v, window_k, window_v, new_k, new_v):
    local_reqs, row_count, width = queries.shape
    prompt_blocks = PROMPT_TOKENS // KEY_BLOCK
    window_blocks = WINDOW_SPAN // KEY_BLOCK
    steps = prompt_blocks + window_blocks + 1
    key_spec = lambda pick: pl.BlockSpec((1, KEY_BLOCK, width), pick)
    prompt_pick = lambda r, b, lens: (r, jnp.minimum(b, prompt_blocks - 1), 0)
    window_pick = lambda r, b, lens: (r, jnp.clip(b - prompt_blocks, 0, window_blocks - 1), 0)
    fixed_pick = lambda r, b, lens: (r, 0, 0)
    grid_spec = pltpu.PrefetchScalarGridSpec(
        num_scalar_prefetch=1,
        grid=(local_reqs, steps),
        in_specs=[
            pl.BlockSpec((1, row_count, width), fixed_pick),
            key_spec(prompt_pick),
            key_spec(prompt_pick),
            key_spec(window_pick),
            key_spec(window_pick),
            key_spec(fixed_pick),
            key_spec(fixed_pick),
        ],
        out_specs=pl.BlockSpec((1, row_count, width), fixed_pick),
        scratch_shapes=[
            pltpu.VMEM((row_count, 1), jnp.float32),
            pltpu.VMEM((row_count, 1), jnp.float32),
            pltpu.VMEM((row_count, width), jnp.float32),
        ],
    )
    keys_total = PROMPT_TOKENS + WINDOW_SPAN + FRESH_TOKENS
    flops = 4 * local_reqs * row_count * keys_total * width
    return pl.pallas_call(
        attention_kernel,
        grid_spec=grid_spec,
        out_shape=jax.ShapeDtypeStruct(queries.shape, jnp.bfloat16),
        cost_estimate=pl.CostEstimate(
            flops=flops,
            transcendentals=local_reqs * row_count * keys_total,
            bytes_accessed=4 * local_reqs * keys_total * width * 2,
        ),
    )(lengths, queries, prompt_k, prompt_v, window_k, window_v, new_k, new_v)


def exchange_kernel(piece_ref, other_ref, send_sem, recv_sem):
    partner = (
        lax.axis_index("dp"),
        1 - lax.axis_index("zh"),
        lax.axis_index("y"),
    )
    barrier = pltpu.get_barrier_semaphore()
    pl.semaphore_signal(
        barrier, 1, device_id=partner, device_id_type=pl.DeviceIdType.MESH
    )
    pl.semaphore_wait(barrier, 1)
    copy = pltpu.make_async_remote_copy(
        src_ref=piece_ref,
        dst_ref=other_ref,
        send_sem=send_sem,
        recv_sem=recv_sem,
        device_id=partner,
        device_id_type=pl.DeviceIdType.MESH,
    )
    copy.start()
    copy.wait()


def exchange(piece, call_id):
    return pl.pallas_call(
        exchange_kernel,
        out_shape=jax.ShapeDtypeStruct(piece.shape, piece.dtype),
        in_specs=[pl.BlockSpec(memory_space=pl.ANY)],
        out_specs=pl.BlockSpec(memory_space=pl.ANY),
        scratch_shapes=[pltpu.SemaphoreType.DMA, pltpu.SemaphoreType.DMA],
        compiler_params=pltpu.CompilerParams(collective_id=call_id, has_side_effects=True),
    )(piece)


def gather_rows(piece, call_id):
    upper = lax.axis_index("zh") == 1
    other = exchange(piece, call_id)
    pair = jnp.stack([jnp.where(upper, other, piece), jnp.where(upper, piece, other)])
    both = lax.all_gather(pair, "y", axis=0, tiled=False)
    return both.reshape((-1,) + piece.shape[1:])


def scatter_rows(full, call_id):
    y_size = lax.axis_size("y")
    zh_size = lax.axis_size("zh")
    split = full.reshape((y_size, zh_size, full.shape[0] // (y_size * zh_size)) + full.shape[1:])
    part = lax.psum_scatter(split, "y", scatter_dimension=0, tiled=False)
    me = lax.axis_index("zh")
    mine = lax.dynamic_index_in_dim(part, me, 0, keepdims=False)
    outgoing = lax.dynamic_index_in_dim(part, 1 - me, 0, keepdims=False)
    return mine.astype(jnp.float32) + exchange(outgoing, call_id).astype(jnp.float32)


def prompt_for_requests(prompt_keys, prompt_values, prompt_group):
    dp_size = lax.axis_size("dp")
    wanted = lax.all_to_all(
        jnp.broadcast_to(prompt_group[None], (dp_size,) + prompt_group.shape), "dp", 0, 0, tiled=False
    )
    both = jnp.stack([prompt_keys, prompt_values], axis=1)
    outgoing = jnp.take(both, wanted, axis=0)
    incoming = lax.all_to_all(outgoing, "dp", 0, 0, tiled=False)
    local_reqs = wanted.shape[1]
    rows = prompt_keys.shape[1]
    incoming = incoming.transpose(1, 2, 0, 3, 4)
    incoming = incoming.reshape(local_reqs, 2, dp_size * rows, prompt_keys.shape[2])
    return incoming[:, 0], incoming[:, 1]


def body(
    tokens,
    cached_len,
    prompt_group,
    attn_gain,
    w_query,
    key_matrix,
    value_matrix,
    w_out,
    window_cache_keys,
    window_cache_values,
    prompt_keys,
    prompt_values,
    mlp_gain,
    w_gate,
    w_up,
    w_down,
):
    local_rows = tokens.shape[0]
    local_reqs = tokens.shape[1]
    query_cols = w_query.shape[1]
    key_cols = key_matrix.shape[1]
    hidden_cols = w_gate.shape[1]
    key_heads = key_cols // HEAD_SIZE
    query_group_width = query_cols // key_cols
    score_scale = 1.0 / math.sqrt(HEAD_SIZE)
    source = norm_rows(tokens, attn_gain)
    offset = 0
    row_piece = gather_rows(source, 0)
    row_count = row_piece.shape[0]
    normed = row_piece
    flattened_rows = normed.reshape(row_count * local_reqs, MODEL_WIDTH)
    y_size = lax.axis_size("y")
    zh_size = lax.axis_size("zh")
    gathered_row = jnp.arange(row_count, dtype=jnp.int32)
    token_of_row = (
        (gathered_row // (zh_size * local_rows) + y_size * ((gathered_row // local_rows) % zh_size))
        * local_rows
        + gathered_row % local_rows
    )
    positions = PROMPT_TOKENS + cached_len[None, :] + token_of_row[:, None]
    project_queries = jnp.dot(flattened_rows, w_query, preferred_element_type=jnp.float32).reshape(
        row_count, local_reqs, query_cols // HEAD_SIZE, HEAD_SIZE
    )
    fresh_keys = jnp.dot(flattened_rows, key_matrix, preferred_element_type=jnp.float32).reshape(
        row_count, local_reqs, key_heads, HEAD_SIZE
    )
    fresh_values = (
        jnp.dot(flattened_rows, value_matrix, preferred_element_type=jnp.float32)
        .astype(jnp.bfloat16)
        .reshape(row_count, local_reqs, key_cols)
    )
    project_queries = (
        rotate(project_queries, positions)
        .astype(jnp.bfloat16)
        .reshape(row_count, local_reqs, query_cols)
    )
    fresh_keys = (
        rotate(fresh_keys, positions).astype(jnp.bfloat16).reshape(row_count, local_reqs, key_cols)
    )
    query_heads = query_cols // HEAD_SIZE
    grid_rows = (y_size, zh_size, local_rows, local_reqs)
    queries = (
        project_queries.reshape(grid_rows + (query_heads, HEAD_SIZE))
        .transpose(3, 4, 1, 0, 2, 5)
        .reshape(local_reqs, query_heads * row_count, HEAD_SIZE)
    )
    own_keys = (
        fresh_keys.reshape(grid_rows + (HEAD_SIZE,))
        .transpose(3, 1, 0, 2, 4)
        .reshape(local_reqs, row_count, HEAD_SIZE)
    )
    own_values = (
        fresh_values.reshape(grid_rows + (HEAD_SIZE,))
        .transpose(3, 1, 0, 2, 4)
        .reshape(local_reqs, row_count, HEAD_SIZE)
    )
    prompt_k, prompt_v = prompt_for_requests(prompt_keys, prompt_values, prompt_group)
    attended = attention(
        cached_len, queries, prompt_k, prompt_v, window_cache_keys, window_cache_values, own_keys, own_values
    )
    attended = (
        attended.reshape(local_reqs, query_heads, zh_size, y_size, local_rows, HEAD_SIZE)
        .transpose(3, 2, 4, 0, 1, 5)
        .reshape(row_count, local_reqs, query_cols)
    )
    picked = attended
    attn_part = scatter_rows(
        jnp.dot(
            picked.reshape(FRESH_TOKENS * local_reqs, query_cols),
            w_out,
            preferred_element_type=jnp.float32,
        )
        .reshape(FRESH_TOKENS, local_reqs, MODEL_WIDTH)
        .astype(jnp.bfloat16),
        1,
    )
    residual = (tokens.astype(jnp.float32) + attn_part).astype(jnp.bfloat16)
    row_piece = gather_rows(norm_rows(residual, mlp_gain), 2)
    row_count = row_piece.shape[0]
    flattened_rows = row_piece.reshape(row_count * local_reqs, MODEL_WIDTH)
    gate_part = jnp.dot(flattened_rows, w_gate, preferred_element_type=jnp.float32)
    up_part = jnp.dot(flattened_rows, w_up, preferred_element_type=jnp.float32)
    hidden = (
        (jax.nn.silu(gate_part) * up_part)
        .astype(jnp.bfloat16)
        .reshape(row_count, local_reqs, hidden_cols)
    )
    picked = hidden
    mlp_part = scatter_rows(
        jnp.dot(
            picked.reshape(FRESH_TOKENS * local_reqs, hidden_cols),
            w_down,
            preferred_element_type=jnp.float32,
        )
        .reshape(FRESH_TOKENS, local_reqs, MODEL_WIDTH)
        .astype(jnp.bfloat16),
        3,
    )
    return (residual.astype(jnp.float32) + mlp_part).astype(jnp.bfloat16)


def solution(mesh):
    zh_size = 2
    split_mesh = jax.sharding.Mesh(
        mesh.devices.reshape(mesh.devices.shape[0], zh_size, -1), ("dp", "zh", "y")
    )
    rows = ("zh", "y")
    in_specs = (
        P(rows, "dp", None),
        P("dp"),
        P("dp"),
        P(),
        P(None, rows),
        P(None, rows),
        P(None, rows),
        P(rows, None),
        P("dp", None, rows),
        P("dp", None, rows),
        P(None, "dp", rows),
        P(None, "dp", rows),
        P(),
        P(None, rows),
        P(None, rows),
        P(rows, None),
    )
    out_specs = P(rows, "dp", None)
    return jax.shard_map(
        body, mesh=split_mesh, in_specs=in_specs, out_specs=out_specs, check_vma=False
    )
```

```python
import math

import jax
import jax.numpy as jnp
from jax import lax
from jax.sharding import PartitionSpec as P
from jax.experimental import pallas as pl
from jax.experimental.pallas import tpu as pltpu

MODEL_WIDTH = 1536
HEAD_SIZE = 96
FRESH_TOKENS = 512
WINDOW_SPAN = 4096
SINKS = 4
PROMPT_TOKENS = 4096


rope_base = 10000.0
epsilon = 1e-05
far_below = -1e30


def norm_rows(values, gain_vec):
    widened = values.astype(jnp.float32)
    factor = lax.rsqrt(jnp.mean(widened * widened, axis=-1, keepdims=True) + epsilon)
    return (widened * factor * gain_vec).astype(jnp.bfloat16)


def rotate(values, positions):
    half_dim = values.shape[-1] // 2
    frequency = rope_base ** (-2.0 * jnp.arange(half_dim, dtype=jnp.float32) / values.shape[-1])
    angles = positions.astype(jnp.float32)[..., None, None] * frequency
    cosine = jnp.cos(angles)
    sine_part = jnp.sin(angles)
    first_half = values[..., :half_dim]
    second_half = values[..., half_dim:]
    return jnp.concatenate(
        [
            first_half * cosine - second_half * sine_part,
            second_half * cosine + first_half * sine_part,
        ],
        axis=-1,
    )


KEY_BLOCK = 512


def attention_kernel(
    length_ref, q_ref, pk_ref, pv_ref, wk_ref, wv_ref, nk_ref, nv_ref, o_ref, peak, total, acc
):
    request = pl.program_id(0)
    block = pl.program_id(1)
    length = length_ref[request]
    prompt_blocks = PROMPT_TOKENS // KEY_BLOCK
    window_blocks = WINDOW_SPAN // KEY_BLOCK
    row_count = q_ref.shape[1]
    score_scale = 1.0 / math.sqrt(HEAD_SIZE)

    @pl.when(block == 0)
    def _():
        peak[...] = jnp.full(peak.shape, far_below, jnp.float32)
        total[...] = jnp.zeros(total.shape, jnp.float32)
        acc[...] = jnp.zeros(acc.shape, jnp.float32)

    rows = lax.rem(lax.broadcasted_iota(jnp.int32, (row_count, KEY_BLOCK), 0), FRESH_TOKENS)
    cols = lax.broadcasted_iota(jnp.int32, (row_count, KEY_BLOCK), 1)

    def absorb(keys, values, visible):
        scores = (
            lax.dot_general(
                q_ref[0],
                keys,
                (((1,), (1,)), ((), ())),
                preferred_element_type=jnp.float32,
            )
            * score_scale
        )
        scores = jnp.where(visible, scores, -jnp.inf)
        old_peak = peak[...]
        new_peak = jnp.maximum(old_peak, jnp.max(scores, axis=-1, keepdims=True))
        factor = jnp.exp(old_peak - new_peak)
        weights = jnp.exp(scores - new_peak)
        total[...] = total[...] * factor + jnp.sum(weights, axis=-1, keepdims=True)
        acc[...] = acc[...] * factor + jnp.dot(
            weights.astype(jnp.bfloat16), values, preferred_element_type=jnp.float32
        )
        peak[...] = new_peak

    prompt_start = block * KEY_BLOCK

    @pl.when(
        (block < prompt_blocks)
        & ((block == 0) | (prompt_start + KEY_BLOCK - 1 > length))
    )
    def _():
        spot = prompt_start + cols
        absorb(
            pk_ref[:, 0, 0].reshape(KEY_BLOCK, HEAD_SIZE),
            pv_ref[:, 0, 0].reshape(KEY_BLOCK, HEAD_SIZE),
            (spot < SINKS) | (spot > length + rows),
        )

    window_start = (block - prompt_blocks) * KEY_BLOCK

    @pl.when(
        (block >= prompt_blocks)
        & (block < prompt_blocks + window_blocks)
        & (window_start + KEY_BLOCK - 1 >= WINDOW_SPAN - length)
    )
    def _():
        slot = window_start + cols
        absorb(wk_ref[0], wv_ref[0], (slot >= WINDOW_SPAN - length) & (slot > rows))

    @pl.when(block == prompt_blocks + window_blocks)
    def _():
        absorb(nk_ref[0], nv_ref[0], cols <= rows)
        o_ref[0] = (acc[...] / total[...]).astype(o_ref.dtype)


def attention(lengths, queries, prompt_kv, window_k, window_v, new_k, new_v):
    local_reqs, row_count, width = queries.shape
    prompt_blocks = PROMPT_TOKENS // KEY_BLOCK
    window_blocks = WINDOW_SPAN // KEY_BLOCK
    steps = prompt_blocks + window_blocks + 1
    key_spec = lambda pick: pl.BlockSpec((1, KEY_BLOCK, width), pick)
    source_rows = prompt_kv.shape[3]
    if source_rows <= KEY_BLOCK:
        prompt_spec = lambda half: pl.BlockSpec(
            (KEY_BLOCK // source_rows, 1, 1, source_rows, width),
            lambda r, b, lens: (jnp.minimum(b, prompt_blocks - 1), r, half, 0, 0),
        )
    else:
        per_source = source_rows // KEY_BLOCK
        prompt_spec = lambda half: pl.BlockSpec(
            (1, 1, 1, KEY_BLOCK, width),
            lambda r, b, lens: (
                jnp.minimum(b, prompt_blocks - 1) // per_source,
                r,
                half,
                jnp.minimum(b, prompt_blocks - 1) % per_source,
                0,
            ),
        )
    window_pick = lambda r, b, lens: (r, jnp.clip(b - prompt_blocks, 0, window_blocks - 1), 0)
    fixed_pick = lambda r, b, lens: (r, 0, 0)
    grid_spec = pltpu.PrefetchScalarGridSpec(
        num_scalar_prefetch=1,
        grid=(local_reqs, steps),
        in_specs=[
            pl.BlockSpec((1, row_count, width), fixed_pick),
            prompt_spec(0),
            prompt_spec(1),
            key_spec(window_pick),
            key_spec(window_pick),
            key_spec(fixed_pick),
            key_spec(fixed_pick),
        ],
        out_specs=pl.BlockSpec((1, row_count, width), fixed_pick),
        scratch_shapes=[
            pltpu.VMEM((row_count, 1), jnp.float32),
            pltpu.VMEM((row_count, 1), jnp.float32),
            pltpu.VMEM((row_count, width), jnp.float32),
        ],
    )
    keys_total = PROMPT_TOKENS + WINDOW_SPAN + FRESH_TOKENS
    flops = 4 * local_reqs * row_count * keys_total * width
    return pl.pallas_call(
        attention_kernel,
        grid_spec=grid_spec,
        out_shape=jax.ShapeDtypeStruct(queries.shape, jnp.bfloat16),
        cost_estimate=pl.CostEstimate(
            flops=flops,
            transcendentals=local_reqs * row_count * keys_total,
            bytes_accessed=4 * local_reqs * keys_total * width * 2,
        ),
    )(lengths, queries, prompt_kv, prompt_kv, window_k, window_v, new_k, new_v)


def exchange_kernel(piece_ref, other_ref, send_sem, recv_sem):
    partner = (
        lax.axis_index("dp"),
        1 - lax.axis_index("zh"),
        lax.axis_index("y"),
    )
    barrier = pltpu.get_barrier_semaphore()
    pl.semaphore_signal(
        barrier, 1, device_id=partner, device_id_type=pl.DeviceIdType.MESH
    )
    pl.semaphore_wait(barrier, 1)
    copy = pltpu.make_async_remote_copy(
        src_ref=piece_ref,
        dst_ref=other_ref,
        send_sem=send_sem,
        recv_sem=recv_sem,
        device_id=partner,
        device_id_type=pl.DeviceIdType.MESH,
    )
    copy.start()
    copy.wait()


def exchange(piece, call_id):
    return pl.pallas_call(
        exchange_kernel,
        out_shape=jax.ShapeDtypeStruct(piece.shape, piece.dtype),
        in_specs=[pl.BlockSpec(memory_space=pl.ANY)],
        out_specs=pl.BlockSpec(memory_space=pl.ANY),
        scratch_shapes=[pltpu.SemaphoreType.DMA, pltpu.SemaphoreType.DMA],
        compiler_params=pltpu.CompilerParams(collective_id=call_id, has_side_effects=True),
    )(piece)


def gather_rows(piece, call_id):
    upper = lax.axis_index("zh") == 1
    other = exchange(piece, call_id)
    pair = jnp.stack([jnp.where(upper, other, piece), jnp.where(upper, piece, other)])
    return lax.all_gather(pair, "y", axis=0, tiled=True).reshape((-1,) + piece.shape[1:])


def scatter_rows(full, call_id):
    y_size = lax.axis_size("y")
    zh_size = lax.axis_size("zh")
    split = full.reshape((y_size * zh_size, full.shape[0] // (y_size * zh_size)) + full.shape[1:])
    part = lax.psum_scatter(split, "y", scatter_dimension=0, tiled=True)
    me = lax.axis_index("zh")
    mine = lax.dynamic_index_in_dim(part, me, 0, keepdims=False)
    outgoing = lax.dynamic_index_in_dim(part, 1 - me, 0, keepdims=False)
    return mine.astype(jnp.float32) + exchange(outgoing, call_id).astype(jnp.float32)


def prompt_for_requests(prompt_keys, prompt_values, prompt_group):
    dp_size = lax.axis_size("dp")
    wanted = lax.all_to_all(
        jnp.broadcast_to(prompt_group[None], (dp_size,) + prompt_group.shape), "dp", 0, 0, tiled=False
    )
    both = jnp.stack([prompt_keys, prompt_values], axis=1)
    outgoing = jnp.take(both, wanted, axis=0)
    return lax.all_to_all(outgoing, "dp", 0, 0, tiled=False)


def body(
    tokens,
    cached_len,
    prompt_group,
    attn_gain,
    w_query,
    key_matrix,
    value_matrix,
    w_out,
    window_cache_keys,
    window_cache_values,
    prompt_keys,
    prompt_values,
    mlp_gain,
    w_gate,
    w_up,
    w_down,
):
    local_rows = tokens.shape[0]
    local_reqs = tokens.shape[1]
    query_cols = w_query.shape[1]
    key_cols = key_matrix.shape[1]
    hidden_cols = w_gate.shape[1]
    key_heads = key_cols // HEAD_SIZE
    query_group_width = query_cols // key_cols
    score_scale = 1.0 / math.sqrt(HEAD_SIZE)
    source = norm_rows(tokens, attn_gain).reshape(local_rows * local_reqs, MODEL_WIDTH)
    offset = 0
    flattened_rows = gather_rows(source, 0)
    row_count = flattened_rows.shape[0] // local_reqs
    y_size = lax.axis_size("y")
    zh_size = lax.axis_size("zh")
    gathered_row = jnp.arange(row_count, dtype=jnp.int32)
    token_of_row = (
        (gathered_row // (zh_size * local_rows) + y_size * ((gathered_row // local_rows) % zh_size))
        * local_rows
        + gathered_row % local_rows
    )
    positions = PROMPT_TOKENS + cached_len[None, :] + token_of_row[:, None]
    project_queries = jnp.dot(flattened_rows, w_query, preferred_element_type=jnp.float32).reshape(
        row_count, local_reqs, query_cols // HEAD_SIZE, HEAD_SIZE
    )
    fresh_keys = jnp.dot(flattened_rows, key_matrix, preferred_element_type=jnp.float32).reshape(
        row_count, local_reqs, key_heads, HEAD_SIZE
    )
    fresh_values = (
        jnp.dot(flattened_rows, value_matrix, preferred_element_type=jnp.float32)
        .astype(jnp.bfloat16)
        .reshape(row_count, local_reqs, key_cols)
    )
    project_queries = (
        rotate(project_queries, positions)
        .astype(jnp.bfloat16)
        .reshape(row_count, local_reqs, query_cols)
    )
    fresh_keys = (
        rotate(fresh_keys, positions).astype(jnp.bfloat16).reshape(row_count, local_reqs, key_cols)
    )
    query_heads = query_cols // HEAD_SIZE
    grid_rows = (y_size, zh_size, local_rows, local_reqs)
    queries = (
        project_queries.reshape(grid_rows + (query_heads, HEAD_SIZE))
        .transpose(3, 4, 1, 0, 2, 5)
        .reshape(local_reqs, query_heads * row_count, HEAD_SIZE)
    )
    own_keys = (
        fresh_keys.reshape(grid_rows + (HEAD_SIZE,))
        .transpose(3, 1, 0, 2, 4)
        .reshape(local_reqs, row_count, HEAD_SIZE)
    )
    own_values = (
        fresh_values.reshape(grid_rows + (HEAD_SIZE,))
        .transpose(3, 1, 0, 2, 4)
        .reshape(local_reqs, row_count, HEAD_SIZE)
    )
    prompt_kv = prompt_for_requests(prompt_keys, prompt_values, prompt_group)
    attended = attention(
        cached_len, queries, prompt_kv, window_cache_keys, window_cache_values, own_keys, own_values
    )
    attended = (
        attended.reshape(local_reqs, query_heads, zh_size, y_size, local_rows, HEAD_SIZE)
        .transpose(3, 2, 4, 0, 1, 5)
        .reshape(row_count, local_reqs, query_cols)
    )
    picked = attended
    attn_part = scatter_rows(
        jnp.dot(
            picked.reshape(FRESH_TOKENS * local_reqs, query_cols),
            w_out,
            preferred_element_type=jnp.float32,
        ).astype(jnp.bfloat16),
        1,
    ).reshape(tokens.shape)
    residual = (tokens.astype(jnp.float32) + attn_part).astype(jnp.bfloat16)
    flattened_rows = gather_rows(
        norm_rows(residual, mlp_gain).reshape(local_rows * local_reqs, MODEL_WIDTH), 2
    )
    gate_part = jnp.dot(flattened_rows, w_gate, preferred_element_type=jnp.float32)
    up_part = jnp.dot(flattened_rows, w_up, preferred_element_type=jnp.float32)
    hidden = (jax.nn.silu(gate_part) * up_part).astype(jnp.bfloat16)
    mlp_part = scatter_rows(
        jnp.dot(hidden, w_down, preferred_element_type=jnp.float32).astype(jnp.bfloat16),
        3,
    ).reshape(tokens.shape)
    return (residual.astype(jnp.float32) + mlp_part).astype(jnp.bfloat16)


def solution(mesh):
    zh_size = 2
    split_mesh = jax.sharding.Mesh(
        mesh.devices.reshape(mesh.devices.shape[0], zh_size, -1), ("dp", "zh", "y")
    )
    rows = ("zh", "y")
    in_specs = (
        P(rows, "dp", None),
        P("dp"),
        P("dp"),
        P(),
        P(None, rows),
        P(None, rows),
        P(None, rows),
        P(rows, None),
        P("dp", None, rows),
        P("dp", None, rows),
        P(None, "dp", rows),
        P(None, "dp", rows),
        P(),
        P(None, rows),
        P(None, rows),
        P(rows, None),
    )
    out_specs = P(rows, "dp", None)
    return jax.shard_map(
        body, mesh=split_mesh, in_specs=in_specs, out_specs=out_specs, check_vma=False
    )
```

```python
import math

import jax
import jax.numpy as jnp
from jax import lax
from jax.sharding import PartitionSpec as P
from jax.experimental import pallas as pl
from jax.experimental.pallas import tpu as pltpu

MODEL_WIDTH = 1536
HEAD_SIZE = 96
FRESH_TOKENS = 512
WINDOW_SPAN = 4096
SINKS = 4
PROMPT_TOKENS = 4096


rope_base = 10000.0
epsilon = 1e-05
far_below = -1e30


def norm_rows(values, gain_vec):
    widened = values.astype(jnp.float32)
    factor = lax.rsqrt(jnp.mean(widened * widened, axis=-1, keepdims=True) + epsilon)
    return (widened * factor * gain_vec).astype(jnp.bfloat16)


def rotate(values, positions):
    half_dim = values.shape[-1] // 2
    frequency = rope_base ** (-2.0 * jnp.arange(half_dim, dtype=jnp.float32) / values.shape[-1])
    angles = positions.astype(jnp.float32)[..., None, None] * frequency
    cosine = jnp.cos(angles)
    sine_part = jnp.sin(angles)
    first_half = values[..., :half_dim]
    second_half = values[..., half_dim:]
    return jnp.concatenate(
        [
            first_half * cosine - second_half * sine_part,
            second_half * cosine + first_half * sine_part,
        ],
        axis=-1,
    )


KEY_BLOCK = 512


def absorber(q_ref, peak, total, acc):
    score_scale = 1.0 / math.sqrt(HEAD_SIZE)

    def absorb(keys, values, visible):
        scores = (
            lax.dot_general(
                q_ref[0],
                keys,
                (((1,), (1,)), ((), ())),
                preferred_element_type=jnp.float32,
            )
            * score_scale
        )
        scores = jnp.where(visible, scores, -jnp.inf)
        old_peak = peak[0]
        new_peak = jnp.maximum(old_peak, jnp.max(scores, axis=-1, keepdims=True))
        factor = jnp.exp(old_peak - new_peak)
        weights = jnp.exp(scores - new_peak)
        total[0] = total[0] * factor + jnp.sum(weights, axis=-1, keepdims=True)
        acc[0] = acc[0] * factor + jnp.dot(
            weights.astype(jnp.bfloat16), values, preferred_element_type=jnp.float32
        )
        peak[0] = new_peak

    return absorb


def recent_kernel(length_ref, q_ref, wk_ref, wv_ref, nk_ref, nv_ref, acc, peak, total):
    request = pl.program_id(0)
    block = pl.program_id(1)
    length = length_ref[request]
    window_blocks = WINDOW_SPAN // KEY_BLOCK
    row_count = q_ref.shape[1]
    absorb = absorber(q_ref, peak, total, acc)

    @pl.when(block == 0)
    def _():
        peak[...] = jnp.full(peak.shape, far_below, jnp.float32)
        total[...] = jnp.zeros(total.shape, jnp.float32)
        acc[...] = jnp.zeros(acc.shape, jnp.float32)

    rows = lax.rem(lax.broadcasted_iota(jnp.int32, (row_count, KEY_BLOCK), 0), FRESH_TOKENS)
    cols = lax.broadcasted_iota(jnp.int32, (row_count, KEY_BLOCK), 1)
    window_start = block * KEY_BLOCK

    @pl.when(
        (block < window_blocks) & (window_start + KEY_BLOCK - 1 >= WINDOW_SPAN - length)
    )
    def _():
        slot = window_start + cols
        absorb(wk_ref[0], wv_ref[0], (slot >= WINDOW_SPAN - length) & (slot > rows))

    @pl.when(block == window_blocks)
    def _():
        absorb(nk_ref[0], nv_ref[0], cols <= rows)


def prompt_kernel(
    length_ref, q_ref, pk_ref, pv_ref, acc_in, peak_in, total_in, o_ref, acc, peak, total
):
    request = pl.program_id(0)
    block = pl.program_id(1)
    length = length_ref[request]
    prompt_blocks = PROMPT_TOKENS // KEY_BLOCK
    row_count = q_ref.shape[1]
    absorb = absorber(q_ref, peak, total, acc)

    @pl.when(block == 0)
    def _():
        peak[...] = peak_in[...]
        total[...] = total_in[...]
        acc[...] = acc_in[...]

    rows = lax.rem(lax.broadcasted_iota(jnp.int32, (row_count, KEY_BLOCK), 0), FRESH_TOKENS)
    cols = lax.broadcasted_iota(jnp.int32, (row_count, KEY_BLOCK), 1)
    prompt_start = block * KEY_BLOCK

    @pl.when((block == 0) | (prompt_start + KEY_BLOCK - 1 > length))
    def _():
        spot = prompt_start + cols
        absorb(
            pk_ref[:, 0, 0].reshape(KEY_BLOCK, HEAD_SIZE),
            pv_ref[:, 0, 0].reshape(KEY_BLOCK, HEAD_SIZE),
            (spot < SINKS) | (spot > length + rows),
        )

    @pl.when(block == prompt_blocks - 1)
    def _():
        o_ref[0] = (acc[0] / total[0]).astype(o_ref.dtype)


def attention(lengths, queries, prompt_kv, window_k, window_v, new_k, new_v):
    local_reqs, row_count, width = queries.shape
    prompt_blocks = PROMPT_TOKENS // KEY_BLOCK
    window_blocks = WINDOW_SPAN // KEY_BLOCK
    key_spec = lambda pick: pl.BlockSpec((1, KEY_BLOCK, width), pick)
    window_pick = lambda r, b, lens: (r, jnp.minimum(b, window_blocks - 1), 0)
    fixed_pick = lambda r, b, lens: (r, 0, 0)
    state_specs = [
        pl.BlockSpec((1, row_count, width), fixed_pick),
        pl.BlockSpec((1, row_count, 1), fixed_pick),
        pl.BlockSpec((1, row_count, 1), fixed_pick),
    ]
    state_shapes = [
        jax.ShapeDtypeStruct((local_reqs, row_count, width), jnp.float32),
        jax.ShapeDtypeStruct((local_reqs, row_count, 1), jnp.float32),
        jax.ShapeDtypeStruct((local_reqs, row_count, 1), jnp.float32),
    ]
    recent_keys = WINDOW_SPAN + FRESH_TOKENS
    state = pl.pallas_call(
        recent_kernel,
        grid_spec=pltpu.PrefetchScalarGridSpec(
            num_scalar_prefetch=1,
            grid=(local_reqs, window_blocks + 1),
            in_specs=[
                pl.BlockSpec((1, row_count, width), fixed_pick),
                key_spec(window_pick),
                key_spec(window_pick),
                key_spec(fixed_pick),
                key_spec(fixed_pick),
            ],
            out_specs=state_specs,
        ),
        out_shape=state_shapes,
        cost_estimate=pl.CostEstimate(
            flops=4 * local_reqs * row_count * recent_keys * width,
            transcendentals=local_reqs * row_count * recent_keys,
            bytes_accessed=4 * local_reqs * recent_keys * width,
        ),
    )(lengths, queries, window_k, window_v, new_k, new_v)

    source_rows = prompt_kv.shape[3]
    if source_rows <= KEY_BLOCK:
        prompt_spec = lambda half: pl.BlockSpec(
            (KEY_BLOCK // source_rows, 1, 1, source_rows, width),
            lambda r, b, lens: (b, r, half, 0, 0),
        )
    else:
        per_source = source_rows // KEY_BLOCK
        prompt_spec = lambda half: pl.BlockSpec(
            (1, 1, 1, KEY_BLOCK, width),
            lambda r, b, lens: (b // per_source, r, half, b % per_source, 0),
        )
    return pl.pallas_call(
        prompt_kernel,
        grid_spec=pltpu.PrefetchScalarGridSpec(
            num_scalar_prefetch=1,
            grid=(local_reqs, prompt_blocks),
            in_specs=[
                pl.BlockSpec((1, row_count, width), fixed_pick),
                prompt_spec(0),
                prompt_spec(1),
            ]
            + state_specs,
            out_specs=pl.BlockSpec((1, row_count, width), fixed_pick),
            scratch_shapes=[
                pltpu.VMEM((1, row_count, width), jnp.float32),
                pltpu.VMEM((1, row_count, 1), jnp.float32),
                pltpu.VMEM((1, row_count, 1), jnp.float32),
            ],
        ),
        out_shape=jax.ShapeDtypeStruct(queries.shape, jnp.bfloat16),
        cost_estimate=pl.CostEstimate(
            flops=4 * local_reqs * row_count * PROMPT_TOKENS * width,
            transcendentals=local_reqs * row_count * PROMPT_TOKENS,
            bytes_accessed=4 * local_reqs * PROMPT_TOKENS * width,
        ),
    )(lengths, queries, prompt_kv, prompt_kv, *state)


def exchange_kernel(piece_ref, other_ref, send_sem, recv_sem):
    partner = (
        lax.axis_index("dp"),
        1 - lax.axis_index("zh"),
        lax.axis_index("y"),
    )
    barrier = pltpu.get_barrier_semaphore()
    pl.semaphore_signal(
        barrier, 1, device_id=partner, device_id_type=pl.DeviceIdType.MESH
    )
    pl.semaphore_wait(barrier, 1)
    copy = pltpu.make_async_remote_copy(
        src_ref=piece_ref,
        dst_ref=other_ref,
        send_sem=send_sem,
        recv_sem=recv_sem,
        device_id=partner,
        device_id_type=pl.DeviceIdType.MESH,
    )
    copy.start()
    copy.wait()


def exchange(piece, call_id):
    return pl.pallas_call(
        exchange_kernel,
        out_shape=jax.ShapeDtypeStruct(piece.shape, piece.dtype),
        in_specs=[pl.BlockSpec(memory_space=pl.ANY)],
        out_specs=pl.BlockSpec(memory_space=pl.ANY),
        scratch_shapes=[pltpu.SemaphoreType.DMA, pltpu.SemaphoreType.DMA],
        compiler_params=pltpu.CompilerParams(collective_id=call_id, has_side_effects=True),
    )(piece)


def gather_rows(piece, call_id):
    upper = lax.axis_index("zh") == 1
    other = exchange(piece, call_id)
    pair = jnp.stack([jnp.where(upper, other, piece), jnp.where(upper, piece, other)])
    return lax.all_gather(pair, "y", axis=0, tiled=True).reshape((-1,) + piece.shape[1:])


def scatter_rows(full, call_id):
    y_size = lax.axis_size("y")
    zh_size = lax.axis_size("zh")
    split = full.reshape((y_size * zh_size, full.shape[0] // (y_size * zh_size)) + full.shape[1:])
    part = lax.psum_scatter(split, "y", scatter_dimension=0, tiled=True)
    me = lax.axis_index("zh")
    mine = lax.dynamic_index_in_dim(part, me, 0, keepdims=False)
    outgoing = lax.dynamic_index_in_dim(part, 1 - me, 0, keepdims=False)
    return mine.astype(jnp.float32) + exchange(outgoing, call_id).astype(jnp.float32)


def prompt_for_requests(prompt_keys, prompt_values, prompt_group):
    dp_size = lax.axis_size("dp")
    wanted = lax.all_to_all(
        jnp.broadcast_to(prompt_group[None], (dp_size,) + prompt_group.shape), "dp", 0, 0, tiled=False
    )
    both = jnp.stack([prompt_keys, prompt_values], axis=1)
    outgoing = jnp.take(both, wanted, axis=0)
    return lax.all_to_all(outgoing, "dp", 0, 0, tiled=False)


def body(
    tokens,
    cached_len,
    prompt_group,
    attn_gain,
    w_query,
    key_matrix,
    value_matrix,
    w_out,
    window_cache_keys,
    window_cache_values,
    prompt_keys,
    prompt_values,
    mlp_gain,
    w_gate,
    w_up,
    w_down,
):
    local_rows = tokens.shape[0]
    local_reqs = tokens.shape[1]
    query_cols = w_query.shape[1]
    key_cols = key_matrix.shape[1]
    hidden_cols = w_gate.shape[1]
    key_heads = key_cols // HEAD_SIZE
    query_group_width = query_cols // key_cols
    score_scale = 1.0 / math.sqrt(HEAD_SIZE)
    source = norm_rows(tokens, attn_gain).reshape(local_rows * local_reqs, MODEL_WIDTH)
    offset = 0
    flattened_rows = gather_rows(source, 0)
    row_count = flattened_rows.shape[0] // local_reqs
    y_size = lax.axis_size("y")
    zh_size = lax.axis_size("zh")
    gathered_row = jnp.arange(row_count, dtype=jnp.int32)
    token_of_row = (
        (gathered_row // (zh_size * local_rows) + y_size * ((gathered_row // local_rows) % zh_size))
        * local_rows
        + gathered_row % local_rows
    )
    positions = PROMPT_TOKENS + cached_len[None, :] + token_of_row[:, None]
    project_queries = jnp.dot(flattened_rows, w_query, preferred_element_type=jnp.float32).reshape(
        row_count, local_reqs, query_cols // HEAD_SIZE, HEAD_SIZE
    )
    fresh_keys = jnp.dot(flattened_rows, key_matrix, preferred_element_type=jnp.float32).reshape(
        row_count, local_reqs, key_heads, HEAD_SIZE
    )
    fresh_values = (
        jnp.dot(flattened_rows, value_matrix, preferred_element_type=jnp.float32)
        .astype(jnp.bfloat16)
        .reshape(row_count, local_reqs, key_cols)
    )
    project_queries = (
        rotate(project_queries, positions)
        .astype(jnp.bfloat16)
        .reshape(row_count, local_reqs, query_cols)
    )
    fresh_keys = (
        rotate(fresh_keys, positions).astype(jnp.bfloat16).reshape(row_count, local_reqs, key_cols)
    )
    query_heads = query_cols // HEAD_SIZE
    grid_rows = (y_size, zh_size, local_rows, local_reqs)
    queries = (
        project_queries.reshape(grid_rows + (query_heads, HEAD_SIZE))
        .transpose(3, 4, 1, 0, 2, 5)
        .reshape(local_reqs, query_heads * row_count, HEAD_SIZE)
    )
    own_keys = (
        fresh_keys.reshape(grid_rows + (HEAD_SIZE,))
        .transpose(3, 1, 0, 2, 4)
        .reshape(local_reqs, row_count, HEAD_SIZE)
    )
    own_values = (
        fresh_values.reshape(grid_rows + (HEAD_SIZE,))
        .transpose(3, 1, 0, 2, 4)
        .reshape(local_reqs, row_count, HEAD_SIZE)
    )
    prompt_kv = prompt_for_requests(prompt_keys, prompt_values, prompt_group)
    attended = attention(
        cached_len, queries, prompt_kv, window_cache_keys, window_cache_values, own_keys, own_values
    )
    attended = (
        attended.reshape(local_reqs, query_heads, zh_size, y_size, local_rows, HEAD_SIZE)
        .transpose(3, 2, 4, 0, 1, 5)
        .reshape(row_count, local_reqs, query_cols)
    )
    picked = attended
    attn_part = scatter_rows(
        jnp.dot(
            picked.reshape(FRESH_TOKENS * local_reqs, query_cols),
            w_out,
            preferred_element_type=jnp.float32,
        ).astype(jnp.bfloat16),
        1,
    ).reshape(tokens.shape)
    residual = (tokens.astype(jnp.float32) + attn_part).astype(jnp.bfloat16)
    flattened_rows = gather_rows(
        norm_rows(residual, mlp_gain).reshape(local_rows * local_reqs, MODEL_WIDTH), 2
    )
    gate_part = jnp.dot(flattened_rows, w_gate, preferred_element_type=jnp.float32)
    up_part = jnp.dot(flattened_rows, w_up, preferred_element_type=jnp.float32)
    hidden = (jax.nn.silu(gate_part) * up_part).astype(jnp.bfloat16)
    mlp_part = scatter_rows(
        jnp.dot(hidden, w_down, preferred_element_type=jnp.float32).astype(jnp.bfloat16),
        3,
    ).reshape(tokens.shape)
    return (residual.astype(jnp.float32) + mlp_part).astype(jnp.bfloat16)


def solution(mesh):
    zh_size = 2
    split_mesh = jax.sharding.Mesh(
        mesh.devices.reshape(mesh.devices.shape[0], zh_size, -1), ("dp", "zh", "y")
    )
    rows = ("zh", "y")
    in_specs = (
        P(rows, "dp", None),
        P("dp"),
        P("dp"),
        P(),
        P(None, rows),
        P(None, rows),
        P(None, rows),
        P(rows, None),
        P("dp", None, rows),
        P("dp", None, rows),
        P(None, "dp", rows),
        P(None, "dp", rows),
        P(),
        P(None, rows),
        P(None, rows),
        P(rows, None),
    )
    out_specs = P(rows, "dp", None)
    return jax.shard_map(
        body, mesh=split_mesh, in_specs=in_specs, out_specs=out_specs, check_vma=False
    )
```

```python
import math

import jax
import jax.numpy as jnp
from jax import lax
from jax.sharding import PartitionSpec as P
from jax.experimental import pallas as pl
from jax.experimental.pallas import tpu as pltpu

MODEL_WIDTH = 1536
HEAD_SIZE = 96
FRESH_TOKENS = 512
WINDOW_SPAN = 4096
SINKS = 4
PROMPT_TOKENS = 4096


rope_base = 10000.0
epsilon = 1e-05
far_below = -1e30


def norm_rows(values, gain_vec):
    widened = values.astype(jnp.float32)
    factor = lax.rsqrt(jnp.mean(widened * widened, axis=-1, keepdims=True) + epsilon)
    return (widened * factor * gain_vec).astype(jnp.bfloat16)


def rotate(values, positions):
    half_dim = values.shape[-1] // 2
    frequency = rope_base ** (-2.0 * jnp.arange(half_dim, dtype=jnp.float32) / values.shape[-1])
    angles = positions.astype(jnp.float32)[..., None, None] * frequency
    cosine = jnp.cos(angles)
    sine_part = jnp.sin(angles)
    first_half = values[..., :half_dim]
    second_half = values[..., half_dim:]
    return jnp.concatenate(
        [
            first_half * cosine - second_half * sine_part,
            second_half * cosine + first_half * sine_part,
        ],
        axis=-1,
    )


KEY_BLOCK = 512


def absorber(q_ref, peak, total, acc):
    score_scale = 1.0 / math.sqrt(HEAD_SIZE)

    def absorb(keys, values, visible):
        scores = (
            lax.dot_general(
                q_ref[0],
                keys,
                (((1,), (1,)), ((), ())),
                preferred_element_type=jnp.float32,
            )
            * score_scale
        )
        if visible is not None:
            scores = jnp.where(visible, scores, -jnp.inf)
        old_peak = peak[0]
        new_peak = jnp.maximum(old_peak, jnp.max(scores, axis=-1, keepdims=True))
        factor = jnp.exp(old_peak - new_peak)
        weights = jnp.exp(scores - new_peak)
        total[0] = total[0] * factor + jnp.sum(weights, axis=-1, keepdims=True)
        acc[0] = acc[0] * factor + jnp.dot(
            weights.astype(jnp.bfloat16), values, preferred_element_type=jnp.float32
        )
        peak[0] = new_peak

    return absorb


def recent_kernel(length_ref, q_ref, wk_ref, wv_ref, nk_ref, nv_ref, acc, peak, total):
    request = pl.program_id(0)
    block = pl.program_id(1)
    length = length_ref[request]
    window_blocks = WINDOW_SPAN // KEY_BLOCK
    row_count = q_ref.shape[1]
    absorb = absorber(q_ref, peak, total, acc)

    @pl.when(block == 0)
    def _():
        peak[...] = jnp.full(peak.shape, far_below, jnp.float32)
        total[...] = jnp.zeros(total.shape, jnp.float32)
        acc[...] = jnp.zeros(acc.shape, jnp.float32)

    rows = lax.rem(lax.broadcasted_iota(jnp.int32, (row_count, KEY_BLOCK), 0), FRESH_TOKENS)
    cols = lax.broadcasted_iota(jnp.int32, (row_count, KEY_BLOCK), 1)
    window_start = block * KEY_BLOCK

    whole = (window_start >= WINDOW_SPAN - length) & (window_start >= FRESH_TOKENS)

    @pl.when(
        (block < window_blocks)
        & (window_start + KEY_BLOCK - 1 >= WINDOW_SPAN - length)
        & jnp.logical_not(whole)
    )
    def _():
        slot = window_start + cols
        absorb(wk_ref[0], wv_ref[0], (slot >= WINDOW_SPAN - length) & (slot > rows))

    @pl.when((block < window_blocks) & whole)
    def _():
        absorb(wk_ref[0], wv_ref[0], None)

    @pl.when(block == window_blocks)
    def _():
        absorb(nk_ref[0], nv_ref[0], cols <= rows)


def prompt_kernel(
    length_ref, q_ref, pk_ref, pv_ref, acc_in, peak_in, total_in, o_ref, acc, peak, total
):
    request = pl.program_id(0)
    block = pl.program_id(1)
    length = length_ref[request]
    prompt_blocks = PROMPT_TOKENS // KEY_BLOCK
    row_count = q_ref.shape[1]
    absorb = absorber(q_ref, peak, total, acc)

    @pl.when(block == 0)
    def _():
        peak[...] = peak_in[...]
        total[...] = total_in[...]
        acc[...] = acc_in[...]

    rows = lax.rem(lax.broadcasted_iota(jnp.int32, (row_count, KEY_BLOCK), 0), FRESH_TOKENS)
    cols = lax.broadcasted_iota(jnp.int32, (row_count, KEY_BLOCK), 1)
    prompt_start = block * KEY_BLOCK

    whole = prompt_start > length + FRESH_TOKENS - 1

    @pl.when(((block == 0) | (prompt_start + KEY_BLOCK - 1 > length)) & jnp.logical_not(whole))
    def _():
        spot = prompt_start + cols
        absorb(
            pk_ref[:, 0, 0].reshape(KEY_BLOCK, HEAD_SIZE),
            pv_ref[:, 0, 0].reshape(KEY_BLOCK, HEAD_SIZE),
            (spot < SINKS) | (spot > length + rows),
        )

    @pl.when(whole)
    def _():
        absorb(
            pk_ref[:, 0, 0].reshape(KEY_BLOCK, HEAD_SIZE),
            pv_ref[:, 0, 0].reshape(KEY_BLOCK, HEAD_SIZE),
            None,
        )

    @pl.when(block == prompt_blocks - 1)
    def _():
        o_ref[0] = (acc[0] / total[0]).astype(o_ref.dtype)


def attention(lengths, queries, prompt_kv, window_k, window_v, new_k, new_v):
    local_reqs, row_count, width = queries.shape
    prompt_blocks = PROMPT_TOKENS // KEY_BLOCK
    window_blocks = WINDOW_SPAN // KEY_BLOCK
    key_spec = lambda pick: pl.BlockSpec((1, KEY_BLOCK, width), pick)
    window_pick = lambda r, b, lens: (r, jnp.minimum(b, window_blocks - 1), 0)
    fixed_pick = lambda r, b, lens: (r, 0, 0)
    state_specs = [
        pl.BlockSpec((1, row_count, width), fixed_pick),
        pl.BlockSpec((1, row_count, 1), fixed_pick),
        pl.BlockSpec((1, row_count, 1), fixed_pick),
    ]
    state_shapes = [
        jax.ShapeDtypeStruct((local_reqs, row_count, width), jnp.float32),
        jax.ShapeDtypeStruct((local_reqs, row_count, 1), jnp.float32),
        jax.ShapeDtypeStruct((local_reqs, row_count, 1), jnp.float32),
    ]
    recent_keys = WINDOW_SPAN + FRESH_TOKENS
    state = pl.pallas_call(
        recent_kernel,
        grid_spec=pltpu.PrefetchScalarGridSpec(
            num_scalar_prefetch=1,
            grid=(local_reqs, window_blocks + 1),
            in_specs=[
                pl.BlockSpec((1, row_count, width), fixed_pick),
                key_spec(window_pick),
                key_spec(window_pick),
                key_spec(fixed_pick),
                key_spec(fixed_pick),
            ],
            out_specs=state_specs,
        ),
        out_shape=state_shapes,
        cost_estimate=pl.CostEstimate(
            flops=4 * local_reqs * row_count * recent_keys * width,
            transcendentals=local_reqs * row_count * recent_keys,
            bytes_accessed=4 * local_reqs * recent_keys * width,
        ),
    )(lengths, queries, window_k, window_v, new_k, new_v)

    source_rows = prompt_kv.shape[3]
    if source_rows <= KEY_BLOCK:
        prompt_spec = lambda half: pl.BlockSpec(
            (KEY_BLOCK // source_rows, 1, 1, source_rows, width),
            lambda r, b, lens: (b, r, half, 0, 0),
        )
    else:
        per_source = source_rows // KEY_BLOCK
        prompt_spec = lambda half: pl.BlockSpec(
            (1, 1, 1, KEY_BLOCK, width),
            lambda r, b, lens: (b // per_source, r, half, b % per_source, 0),
        )
    return pl.pallas_call(
        prompt_kernel,
        grid_spec=pltpu.PrefetchScalarGridSpec(
            num_scalar_prefetch=1,
            grid=(local_reqs, prompt_blocks),
            in_specs=[
                pl.BlockSpec((1, row_count, width), fixed_pick),
                prompt_spec(0),
                prompt_spec(1),
            ]
            + state_specs,
            out_specs=pl.BlockSpec((1, row_count, width), fixed_pick),
            scratch_shapes=[
                pltpu.VMEM((1, row_count, width), jnp.float32),
                pltpu.VMEM((1, row_count, 1), jnp.float32),
                pltpu.VMEM((1, row_count, 1), jnp.float32),
            ],
        ),
        out_shape=jax.ShapeDtypeStruct(queries.shape, jnp.bfloat16),
        cost_estimate=pl.CostEstimate(
            flops=4 * local_reqs * row_count * PROMPT_TOKENS * width,
            transcendentals=local_reqs * row_count * PROMPT_TOKENS,
            bytes_accessed=4 * local_reqs * PROMPT_TOKENS * width,
        ),
    )(lengths, queries, prompt_kv, prompt_kv, *state)


def exchange_kernel(piece_ref, other_ref, send_sem, recv_sem):
    partner = (
        lax.axis_index("dp"),
        1 - lax.axis_index("zh"),
        lax.axis_index("y"),
    )
    barrier = pltpu.get_barrier_semaphore()
    pl.semaphore_signal(
        barrier, 1, device_id=partner, device_id_type=pl.DeviceIdType.MESH
    )
    pl.semaphore_wait(barrier, 1)
    copy = pltpu.make_async_remote_copy(
        src_ref=piece_ref,
        dst_ref=other_ref,
        send_sem=send_sem,
        recv_sem=recv_sem,
        device_id=partner,
        device_id_type=pl.DeviceIdType.MESH,
    )
    copy.start()
    copy.wait()


def exchange(piece, call_id):
    return pl.pallas_call(
        exchange_kernel,
        out_shape=jax.ShapeDtypeStruct(piece.shape, piece.dtype),
        in_specs=[pl.BlockSpec(memory_space=pl.ANY)],
        out_specs=pl.BlockSpec(memory_space=pl.ANY),
        scratch_shapes=[pltpu.SemaphoreType.DMA, pltpu.SemaphoreType.DMA],
        compiler_params=pltpu.CompilerParams(collective_id=call_id, has_side_effects=True),
    )(piece)


def gather_rows(piece, call_id):
    upper = lax.axis_index("zh") == 1
    other = exchange(piece, call_id)
    pair = jnp.stack([jnp.where(upper, other, piece), jnp.where(upper, piece, other)])
    return lax.all_gather(pair, "y", axis=0, tiled=True).reshape((-1,) + piece.shape[1:])


def scatter_rows(full, call_id):
    y_size = lax.axis_size("y")
    zh_size = lax.axis_size("zh")
    split = full.reshape((y_size * zh_size, full.shape[0] // (y_size * zh_size)) + full.shape[1:])
    part = lax.psum_scatter(split, "y", scatter_dimension=0, tiled=True)
    me = lax.axis_index("zh")
    mine = lax.dynamic_index_in_dim(part, me, 0, keepdims=False)
    outgoing = lax.dynamic_index_in_dim(part, 1 - me, 0, keepdims=False)
    return mine.astype(jnp.float32) + exchange(outgoing, call_id).astype(jnp.float32)


def prompt_for_requests(prompt_keys, prompt_values, prompt_group):
    dp_size = lax.axis_size("dp")
    wanted = lax.all_to_all(
        jnp.broadcast_to(prompt_group[None], (dp_size,) + prompt_group.shape), "dp", 0, 0, tiled=False
    )
    both = jnp.stack([prompt_keys, prompt_values], axis=1)
    outgoing = jnp.take(both, wanted, axis=0)
    return lax.all_to_all(outgoing, "dp", 0, 0, tiled=False)


def body(
    tokens,
    cached_len,
    prompt_group,
    attn_gain,
    w_query,
    key_matrix,
    value_matrix,
    w_out,
    window_cache_keys,
    window_cache_values,
    prompt_keys,
    prompt_values,
    mlp_gain,
    w_gate,
    w_up,
    w_down,
):
    local_rows = tokens.shape[0]
    local_reqs = tokens.shape[1]
    query_cols = w_query.shape[1]
    key_cols = key_matrix.shape[1]
    hidden_cols = w_gate.shape[1]
    key_heads = key_cols // HEAD_SIZE
    query_group_width = query_cols // key_cols
    score_scale = 1.0 / math.sqrt(HEAD_SIZE)
    source = norm_rows(tokens, attn_gain).reshape(local_rows * local_reqs, MODEL_WIDTH)
    offset = 0
    flattened_rows = gather_rows(source, 0)
    row_count = flattened_rows.shape[0] // local_reqs
    y_size = lax.axis_size("y")
    zh_size = lax.axis_size("zh")
    gathered_row = jnp.arange(row_count, dtype=jnp.int32)
    token_of_row = (
        (gathered_row // (zh_size * local_rows) + y_size * ((gathered_row // local_rows) % zh_size))
        * local_rows
        + gathered_row % local_rows
    )
    positions = PROMPT_TOKENS + cached_len[None, :] + token_of_row[:, None]
    project_queries = jnp.dot(flattened_rows, w_query, preferred_element_type=jnp.float32).reshape(
        row_count, local_reqs, query_cols // HEAD_SIZE, HEAD_SIZE
    )
    fresh_keys = jnp.dot(flattened_rows, key_matrix, preferred_element_type=jnp.float32).reshape(
        row_count, local_reqs, key_heads, HEAD_SIZE
    )
    fresh_values = (
        jnp.dot(flattened_rows, value_matrix, preferred_element_type=jnp.float32)
        .astype(jnp.bfloat16)
        .reshape(row_count, local_reqs, key_cols)
    )
    project_queries = (
        rotate(project_queries, positions)
        .astype(jnp.bfloat16)
        .reshape(row_count, local_reqs, query_cols)
    )
    fresh_keys = (
        rotate(fresh_keys, positions).astype(jnp.bfloat16).reshape(row_count, local_reqs, key_cols)
    )
    query_heads = query_cols // HEAD_SIZE
    grid_rows = (y_size, zh_size, local_rows, local_reqs)
    queries = (
        project_queries.reshape(grid_rows + (query_heads, HEAD_SIZE))
        .transpose(3, 4, 1, 0, 2, 5)
        .reshape(local_reqs, query_heads * row_count, HEAD_SIZE)
    )
    own_keys = (
        fresh_keys.reshape(grid_rows + (HEAD_SIZE,))
        .transpose(3, 1, 0, 2, 4)
        .reshape(local_reqs, row_count, HEAD_SIZE)
    )
    own_values = (
        fresh_values.reshape(grid_rows + (HEAD_SIZE,))
        .transpose(3, 1, 0, 2, 4)
        .reshape(local_reqs, row_count, HEAD_SIZE)
    )
    prompt_kv = prompt_for_requests(prompt_keys, prompt_values, prompt_group)
    attended = attention(
        cached_len, queries, prompt_kv, window_cache_keys, window_cache_values, own_keys, own_values
    )
    attended = (
        attended.reshape(local_reqs, query_heads, zh_size, y_size, local_rows, HEAD_SIZE)
        .transpose(3, 2, 4, 0, 1, 5)
        .reshape(row_count, local_reqs, query_cols)
    )
    picked = attended
    attn_part = scatter_rows(
        jnp.dot(
            picked.reshape(FRESH_TOKENS * local_reqs, query_cols),
            w_out,
            preferred_element_type=jnp.float32,
        ).astype(jnp.bfloat16),
        1,
    ).reshape(tokens.shape)
    residual = (tokens.astype(jnp.float32) + attn_part).astype(jnp.bfloat16)
    flattened_rows = gather_rows(
        norm_rows(residual, mlp_gain).reshape(local_rows * local_reqs, MODEL_WIDTH), 2
    )
    gate_part = jnp.dot(flattened_rows, w_gate, preferred_element_type=jnp.float32)
    up_part = jnp.dot(flattened_rows, w_up, preferred_element_type=jnp.float32)
    hidden = (jax.nn.silu(gate_part) * up_part).astype(jnp.bfloat16)
    mlp_part = scatter_rows(
        jnp.dot(hidden, w_down, preferred_element_type=jnp.float32).astype(jnp.bfloat16),
        3,
    ).reshape(tokens.shape)
    return (residual.astype(jnp.float32) + mlp_part).astype(jnp.bfloat16)


def solution(mesh):
    zh_size = 2
    split_mesh = jax.sharding.Mesh(
        mesh.devices.reshape(mesh.devices.shape[0], zh_size, -1), ("dp", "zh", "y")
    )
    rows = ("zh", "y")
    in_specs = (
        P(rows, "dp", None),
        P("dp"),
        P("dp"),
        P(),
        P(None, rows),
        P(None, rows),
        P(None, rows),
        P(rows, None),
        P("dp", None, rows),
        P("dp", None, rows),
        P(None, "dp", rows),
        P(None, "dp", rows),
        P(),
        P(None, rows),
        P(None, rows),
        P(rows, None),
    )
    out_specs = P(rows, "dp", None)
    return jax.shard_map(
        body, mesh=split_mesh, in_specs=in_specs, out_specs=out_specs, check_vma=False
    )
```

```python
import math

import jax
import jax.numpy as jnp
from jax import lax
from jax.sharding import PartitionSpec as P
from jax.experimental import pallas as pl
from jax.experimental.pallas import tpu as pltpu

MODEL_WIDTH = 1536
HEAD_SIZE = 96
FRESH_TOKENS = 512
WINDOW_SPAN = 4096
SINKS = 4
PROMPT_TOKENS = 4096


rope_base = 10000.0
epsilon = 1e-05
far_below = -1e30


def norm_rows(values, gain_vec):
    widened = values.astype(jnp.float32)
    factor = lax.rsqrt(jnp.mean(widened * widened, axis=-1, keepdims=True) + epsilon)
    return (widened * factor * gain_vec).astype(jnp.bfloat16)


def rotate(values, positions):
    half_dim = values.shape[-1] // 2
    frequency = rope_base ** (-2.0 * jnp.arange(half_dim, dtype=jnp.float32) / values.shape[-1])
    angles = positions.astype(jnp.float32)[..., None, None] * frequency
    cosine = jnp.cos(angles)
    sine_part = jnp.sin(angles)
    first_half = values[..., :half_dim]
    second_half = values[..., half_dim:]
    return jnp.concatenate(
        [
            first_half * cosine - second_half * sine_part,
            second_half * cosine + first_half * sine_part,
        ],
        axis=-1,
    )


KEY_BLOCK = 512


def absorber(q_ref, peak, total, acc):
    score_scale = 1.0 / math.sqrt(HEAD_SIZE)

    def absorb(keys, values, visible):
        scores = (
            lax.dot_general(
                q_ref[0],
                keys,
                (((1,), (1,)), ((), ())),
                preferred_element_type=jnp.float32,
            )
            * score_scale
        )
        if visible is not None:
            scores = jnp.where(visible, scores, -jnp.inf)
        old_peak = peak[0]
        new_peak = jnp.maximum(old_peak, jnp.max(scores, axis=-1, keepdims=True))
        factor = jnp.exp(old_peak - new_peak)
        weights = jnp.exp(scores - new_peak)
        total[0] = total[0] * factor + jnp.sum(weights, axis=-1, keepdims=True)
        acc[0] = acc[0] * factor + jnp.dot(
            weights.astype(jnp.bfloat16), values, preferred_element_type=jnp.float32
        )
        peak[0] = new_peak

    return absorb


def recent_kernel(length_ref, q_ref, wk_ref, wv_ref, nk_ref, nv_ref, acc, peak, total):
    request = pl.program_id(0)
    block = pl.program_id(1)
    length = length_ref[request]
    window_blocks = WINDOW_SPAN // KEY_BLOCK
    row_count = q_ref.shape[1]
    absorb = absorber(q_ref, peak, total, acc)

    @pl.when(block == 0)
    def _():
        peak[...] = jnp.full(peak.shape, far_below, jnp.float32)
        total[...] = jnp.zeros(total.shape, jnp.float32)
        acc[...] = jnp.zeros(acc.shape, jnp.float32)

    rows = lax.rem(lax.broadcasted_iota(jnp.int32, (row_count, KEY_BLOCK), 0), FRESH_TOKENS)
    cols = lax.broadcasted_iota(jnp.int32, (row_count, KEY_BLOCK), 1)
    window_start = block * KEY_BLOCK

    whole = (window_start >= WINDOW_SPAN - length) & (window_start >= FRESH_TOKENS)

    @pl.when(
        (block < window_blocks)
        & (window_start + KEY_BLOCK - 1 >= WINDOW_SPAN - length)
        & jnp.logical_not(whole)
    )
    def _():
        slot = window_start + cols
        absorb(wk_ref[0], wv_ref[0], (slot >= WINDOW_SPAN - length) & (slot > rows))

    @pl.when((block < window_blocks) & whole)
    def _():
        absorb(wk_ref[0], wv_ref[0], None)

    @pl.when(block == window_blocks)
    def _():
        absorb(nk_ref[0], nv_ref[0], cols <= rows)


def prompt_kernel(
    length_ref, q_ref, pk_ref, pv_ref, acc_in, peak_in, total_in, o_ref, acc, peak, total
):
    request = pl.program_id(0)
    block = pl.program_id(1)
    length = length_ref[request]
    prompt_blocks = PROMPT_TOKENS // KEY_BLOCK
    row_count = q_ref.shape[1]
    absorb = absorber(q_ref, peak, total, acc)

    @pl.when(block == 0)
    def _():
        peak[...] = peak_in[...]
        total[...] = total_in[...]
        acc[...] = acc_in[...]

    rows = lax.rem(lax.broadcasted_iota(jnp.int32, (row_count, KEY_BLOCK), 0), FRESH_TOKENS)
    cols = lax.broadcasted_iota(jnp.int32, (row_count, KEY_BLOCK), 1)
    prompt_start = block * KEY_BLOCK

    whole = prompt_start > length + FRESH_TOKENS - 1

    @pl.when(((block == 0) | (prompt_start + KEY_BLOCK - 1 > length)) & jnp.logical_not(whole))
    def _():
        spot = prompt_start + cols
        absorb(
            pk_ref[:, 0, 0].reshape(KEY_BLOCK, HEAD_SIZE),
            pv_ref[:, 0, 0].reshape(KEY_BLOCK, HEAD_SIZE),
            (spot < SINKS) | (spot > length + rows),
        )

    @pl.when(whole)
    def _():
        absorb(
            pk_ref[:, 0, 0].reshape(KEY_BLOCK, HEAD_SIZE),
            pv_ref[:, 0, 0].reshape(KEY_BLOCK, HEAD_SIZE),
            None,
        )

    @pl.when(block == prompt_blocks - 1)
    def _():
        o_ref[0] = (acc[0] / total[0]).astype(o_ref.dtype)


def attention(lengths, queries, prompt_kv, window_k, window_v, new_k, new_v):
    local_reqs, row_count, width = queries.shape
    prompt_blocks = PROMPT_TOKENS // KEY_BLOCK
    window_blocks = WINDOW_SPAN // KEY_BLOCK
    key_spec = lambda pick: pl.BlockSpec((1, KEY_BLOCK, width), pick)
    window_pick = lambda r, b, lens: (r, jnp.minimum(b, window_blocks - 1), 0)
    fixed_pick = lambda r, b, lens: (r, 0, 0)
    state_specs = [
        pl.BlockSpec((1, row_count, width), fixed_pick),
        pl.BlockSpec((1, row_count, 1), fixed_pick),
        pl.BlockSpec((1, row_count, 1), fixed_pick),
    ]
    state_shapes = [
        jax.ShapeDtypeStruct((local_reqs, row_count, width), jnp.float32),
        jax.ShapeDtypeStruct((local_reqs, row_count, 1), jnp.float32),
        jax.ShapeDtypeStruct((local_reqs, row_count, 1), jnp.float32),
    ]
    recent_keys = WINDOW_SPAN + FRESH_TOKENS
    state = pl.pallas_call(
        recent_kernel,
        grid_spec=pltpu.PrefetchScalarGridSpec(
            num_scalar_prefetch=1,
            grid=(local_reqs, window_blocks + 1),
            in_specs=[
                pl.BlockSpec((1, row_count, width), fixed_pick),
                key_spec(window_pick),
                key_spec(window_pick),
                key_spec(fixed_pick),
                key_spec(fixed_pick),
            ],
            out_specs=state_specs,
        ),
        out_shape=state_shapes,
        cost_estimate=pl.CostEstimate(
            flops=4 * local_reqs * row_count * recent_keys * width,
            transcendentals=local_reqs * row_count * recent_keys,
            bytes_accessed=4 * local_reqs * recent_keys * width,
        ),
    )(lengths, queries, window_k, window_v, new_k, new_v)

    source_rows = prompt_kv.shape[3]
    if source_rows <= KEY_BLOCK:
        prompt_spec = lambda half: pl.BlockSpec(
            (KEY_BLOCK // source_rows, 1, 1, source_rows, width),
            lambda r, b, lens: (b, r, half, 0, 0),
        )
    else:
        per_source = source_rows // KEY_BLOCK
        prompt_spec = lambda half: pl.BlockSpec(
            (1, 1, 1, KEY_BLOCK, width),
            lambda r, b, lens: (b // per_source, r, half, b % per_source, 0),
        )
    return pl.pallas_call(
        prompt_kernel,
        grid_spec=pltpu.PrefetchScalarGridSpec(
            num_scalar_prefetch=1,
            grid=(local_reqs, prompt_blocks),
            in_specs=[
                pl.BlockSpec((1, row_count, width), fixed_pick),
                prompt_spec(0),
                prompt_spec(1),
            ]
            + state_specs,
            out_specs=pl.BlockSpec((1, row_count, width), fixed_pick),
            scratch_shapes=[
                pltpu.VMEM((1, row_count, width), jnp.float32),
                pltpu.VMEM((1, row_count, 1), jnp.float32),
                pltpu.VMEM((1, row_count, 1), jnp.float32),
            ],
        ),
        out_shape=jax.ShapeDtypeStruct(queries.shape, jnp.bfloat16),
        cost_estimate=pl.CostEstimate(
            flops=4 * local_reqs * row_count * PROMPT_TOKENS * width,
            transcendentals=local_reqs * row_count * PROMPT_TOKENS,
            bytes_accessed=4 * local_reqs * PROMPT_TOKENS * width,
        ),
    )(lengths, queries, prompt_kv, prompt_kv, *state)


def exchange_kernel(piece_ref, other_ref, send_sem, recv_sem):
    partner = (
        lax.axis_index("dp"),
        1 - lax.axis_index("zh"),
        lax.axis_index("y"),
    )
    barrier = pltpu.get_barrier_semaphore()
    pl.semaphore_signal(
        barrier, 1, device_id=partner, device_id_type=pl.DeviceIdType.MESH
    )
    pl.semaphore_wait(barrier, 1)
    copy = pltpu.make_async_remote_copy(
        src_ref=piece_ref,
        dst_ref=other_ref,
        send_sem=send_sem,
        recv_sem=recv_sem,
        device_id=partner,
        device_id_type=pl.DeviceIdType.MESH,
    )
    copy.start()
    copy.wait()


def exchange(piece, call_id):
    return pl.pallas_call(
        exchange_kernel,
        out_shape=jax.ShapeDtypeStruct(piece.shape, piece.dtype),
        in_specs=[pl.BlockSpec(memory_space=pl.ANY)],
        out_specs=pl.BlockSpec(memory_space=pl.ANY),
        scratch_shapes=[pltpu.SemaphoreType.DMA, pltpu.SemaphoreType.DMA],
        compiler_params=pltpu.CompilerParams(collective_id=call_id, has_side_effects=True),
    )(piece)


def pair_rows(piece, call_id):
    upper = lax.axis_index("zh") == 1
    other = exchange(piece, call_id)
    return jnp.stack([jnp.where(upper, other, piece), jnp.where(upper, piece, other)])


def gather_rows(pair):
    return lax.all_gather(pair, "y", axis=0, tiled=True).reshape((-1,) + pair.shape[2:])


def reduce_rows(full, call_id):
    y_size = lax.axis_size("y")
    zh_size = lax.axis_size("zh")
    split = full.reshape((y_size * zh_size, full.shape[0] // (y_size * zh_size)) + full.shape[1:])
    part = lax.psum_scatter(split, "y", scatter_dimension=0, tiled=True)
    return part.astype(jnp.float32) + exchange(part, call_id).astype(jnp.float32)


def scatter_rows(full, call_id):
    y_size = lax.axis_size("y")
    zh_size = lax.axis_size("zh")
    split = full.reshape((y_size * zh_size, full.shape[0] // (y_size * zh_size)) + full.shape[1:])
    part = lax.psum_scatter(split, "y", scatter_dimension=0, tiled=True)
    me = lax.axis_index("zh")
    mine = lax.dynamic_index_in_dim(part, me, 0, keepdims=False)
    outgoing = lax.dynamic_index_in_dim(part, 1 - me, 0, keepdims=False)
    return mine.astype(jnp.float32) + exchange(outgoing, call_id).astype(jnp.float32)


def prompt_for_requests(prompt_keys, prompt_values, prompt_group):
    dp_size = lax.axis_size("dp")
    wanted = lax.all_to_all(
        jnp.broadcast_to(prompt_group[None], (dp_size,) + prompt_group.shape), "dp", 0, 0, tiled=False
    )
    both = jnp.stack([prompt_keys, prompt_values], axis=1)
    outgoing = jnp.take(both, wanted, axis=0)
    return lax.all_to_all(outgoing, "dp", 0, 0, tiled=False)


def body(
    tokens,
    cached_len,
    prompt_group,
    attn_gain,
    w_query,
    key_matrix,
    value_matrix,
    w_out,
    window_cache_keys,
    window_cache_values,
    prompt_keys,
    prompt_values,
    mlp_gain,
    w_gate,
    w_up,
    w_down,
):
    local_rows = tokens.shape[0]
    local_reqs = tokens.shape[1]
    query_cols = w_query.shape[1]
    key_cols = key_matrix.shape[1]
    hidden_cols = w_gate.shape[1]
    key_heads = key_cols // HEAD_SIZE
    query_group_width = query_cols // key_cols
    score_scale = 1.0 / math.sqrt(HEAD_SIZE)
    token_pair = pair_rows(tokens.reshape(local_rows * local_reqs, MODEL_WIDTH), 0)
    source = norm_rows(token_pair, attn_gain)
    offset = 0
    flattened_rows = gather_rows(source)
    row_count = flattened_rows.shape[0] // local_reqs
    y_size = lax.axis_size("y")
    zh_size = lax.axis_size("zh")
    gathered_row = jnp.arange(row_count, dtype=jnp.int32)
    token_of_row = (
        (gathered_row // (zh_size * local_rows) + y_size * ((gathered_row // local_rows) % zh_size))
        * local_rows
        + gathered_row % local_rows
    )
    positions = PROMPT_TOKENS + cached_len[None, :] + token_of_row[:, None]
    project_queries = jnp.dot(flattened_rows, w_query, preferred_element_type=jnp.float32).reshape(
        row_count, local_reqs, query_cols // HEAD_SIZE, HEAD_SIZE
    )
    fresh_keys = jnp.dot(flattened_rows, key_matrix, preferred_element_type=jnp.float32).reshape(
        row_count, local_reqs, key_heads, HEAD_SIZE
    )
    fresh_values = (
        jnp.dot(flattened_rows, value_matrix, preferred_element_type=jnp.float32)
        .astype(jnp.bfloat16)
        .reshape(row_count, local_reqs, key_cols)
    )
    project_queries = (
        rotate(project_queries, positions)
        .astype(jnp.bfloat16)
        .reshape(row_count, local_reqs, query_cols)
    )
    fresh_keys = (
        rotate(fresh_keys, positions).astype(jnp.bfloat16).reshape(row_count, local_reqs, key_cols)
    )
    query_heads = query_cols // HEAD_SIZE
    grid_rows = (y_size, zh_size, local_rows, local_reqs)
    queries = (
        project_queries.reshape(grid_rows + (query_heads, HEAD_SIZE))
        .transpose(3, 4, 1, 0, 2, 5)
        .reshape(local_reqs, query_heads * row_count, HEAD_SIZE)
    )
    own_keys = (
        fresh_keys.reshape(grid_rows + (HEAD_SIZE,))
        .transpose(3, 1, 0, 2, 4)
        .reshape(local_reqs, row_count, HEAD_SIZE)
    )
    own_values = (
        fresh_values.reshape(grid_rows + (HEAD_SIZE,))
        .transpose(3, 1, 0, 2, 4)
        .reshape(local_reqs, row_count, HEAD_SIZE)
    )
    prompt_kv = prompt_for_requests(prompt_keys, prompt_values, prompt_group)
    attended = attention(
        cached_len, queries, prompt_kv, window_cache_keys, window_cache_values, own_keys, own_values
    )
    attended = (
        attended.reshape(local_reqs, query_heads, zh_size, y_size, local_rows, HEAD_SIZE)
        .transpose(3, 2, 4, 0, 1, 5)
        .reshape(row_count, local_reqs, query_cols)
    )
    picked = attended
    attn_pair = reduce_rows(
        jnp.dot(
            picked.reshape(FRESH_TOKENS * local_reqs, query_cols),
            w_out,
            preferred_element_type=jnp.float32,
        ).astype(jnp.bfloat16),
        1,
    )
    residual_pair = (token_pair.astype(jnp.float32) + attn_pair).astype(jnp.bfloat16)
    residual = lax.dynamic_index_in_dim(
        residual_pair, lax.axis_index("zh"), 0, keepdims=False
    ).reshape(tokens.shape)
    flattened_rows = gather_rows(norm_rows(residual_pair, mlp_gain))
    gate_part = jnp.dot(flattened_rows, w_gate, preferred_element_type=jnp.float32)
    up_part = jnp.dot(flattened_rows, w_up, preferred_element_type=jnp.float32)
    hidden = (jax.nn.silu(gate_part) * up_part).astype(jnp.bfloat16)
    mlp_part = scatter_rows(
        jnp.dot(hidden, w_down, preferred_element_type=jnp.float32).astype(jnp.bfloat16),
        3,
    ).reshape(tokens.shape)
    return (residual.astype(jnp.float32) + mlp_part).astype(jnp.bfloat16)


def solution(mesh):
    zh_size = 2
    split_mesh = jax.sharding.Mesh(
        mesh.devices.reshape(mesh.devices.shape[0], zh_size, -1), ("dp", "zh", "y")
    )
    rows = ("zh", "y")
    in_specs = (
        P(rows, "dp", None),
        P("dp"),
        P("dp"),
        P(),
        P(None, rows),
        P(None, rows),
        P(None, rows),
        P(rows, None),
        P("dp", None, rows),
        P("dp", None, rows),
        P(None, "dp", rows),
        P(None, "dp", rows),
        P(),
        P(None, rows),
        P(None, rows),
        P(rows, None),
    )
    out_specs = P(rows, "dp", None)
    return jax.shard_map(
        body, mesh=split_mesh, in_specs=in_specs, out_specs=out_specs, check_vma=False
    )
```

```python
import math

import jax
import jax.numpy as jnp
from jax import lax
from jax.sharding import PartitionSpec as P
from jax.experimental import pallas as pl
from jax.experimental.pallas import tpu as pltpu

MODEL_WIDTH = 1536
HEAD_SIZE = 96
FRESH_TOKENS = 512
WINDOW_SPAN = 4096
SINKS = 4
PROMPT_TOKENS = 4096


rope_base = 10000.0
epsilon = 1e-05
far_below = -1e30


def norm_rows(values, gain_vec):
    widened = values.astype(jnp.float32)
    factor = lax.rsqrt(jnp.mean(widened * widened, axis=-1, keepdims=True) + epsilon)
    return (widened * factor * gain_vec).astype(jnp.bfloat16)


def rotate(values, positions):
    half_dim = values.shape[-1] // 2
    frequency = rope_base ** (-2.0 * jnp.arange(half_dim, dtype=jnp.float32) / values.shape[-1])
    angles = positions.astype(jnp.float32)[..., None, None] * frequency
    cosine = jnp.cos(angles)
    sine_part = jnp.sin(angles)
    first_half = values[..., :half_dim]
    second_half = values[..., half_dim:]
    return jnp.concatenate(
        [
            first_half * cosine - second_half * sine_part,
            second_half * cosine + first_half * sine_part,
        ],
        axis=-1,
    )


KEY_BLOCK = 512


def absorber(q_ref, peak, total, acc):
    score_scale = 1.0 / math.sqrt(HEAD_SIZE)

    def absorb(keys, values, visible):
        scores = (
            lax.dot_general(
                q_ref[0],
                keys,
                (((1,), (1,)), ((), ())),
                preferred_element_type=jnp.float32,
            )
            * score_scale
        )
        if visible is not None:
            scores = jnp.where(visible, scores, -jnp.inf)
        old_peak = peak[0]
        new_peak = jnp.maximum(old_peak, jnp.max(scores, axis=-1, keepdims=True))
        factor = jnp.exp(old_peak - new_peak)
        weights = jnp.exp(scores - new_peak)
        total[0] = total[0] * factor + jnp.sum(weights, axis=-1, keepdims=True)
        acc[0] = acc[0] * factor + jnp.dot(
            weights.astype(jnp.bfloat16), values, preferred_element_type=jnp.float32
        )
        peak[0] = new_peak

    return absorb


def recent_kernel(length_ref, q_ref, wk_ref, wv_ref, nk_ref, nv_ref, acc, peak, total):
    request = pl.program_id(0)
    block = pl.program_id(1)
    length = length_ref[request]
    window_blocks = WINDOW_SPAN // KEY_BLOCK
    row_count = q_ref.shape[1]
    absorb = absorber(q_ref, peak, total, acc)

    @pl.when(block == 0)
    def _():
        peak[...] = jnp.full(peak.shape, far_below, jnp.float32)
        total[...] = jnp.zeros(total.shape, jnp.float32)
        acc[...] = jnp.zeros(acc.shape, jnp.float32)

    rows = lax.rem(lax.broadcasted_iota(jnp.int32, (row_count, KEY_BLOCK), 0), FRESH_TOKENS)
    cols = lax.broadcasted_iota(jnp.int32, (row_count, KEY_BLOCK), 1)
    window_start = block * KEY_BLOCK

    whole = (window_start >= WINDOW_SPAN - length) & (window_start >= FRESH_TOKENS)

    @pl.when(
        (block < window_blocks)
        & (window_start + KEY_BLOCK - 1 >= WINDOW_SPAN - length)
        & jnp.logical_not(whole)
    )
    def _():
        slot = window_start + cols
        absorb(wk_ref[0], wv_ref[0], (slot >= WINDOW_SPAN - length) & (slot > rows))

    @pl.when((block < window_blocks) & whole)
    def _():
        absorb(wk_ref[0], wv_ref[0], None)

    @pl.when(block == window_blocks)
    def _():
        absorb(nk_ref[0], nv_ref[0], cols <= rows)


def prompt_kernel(
    length_ref, q_ref, pk_ref, pv_ref, acc_in, peak_in, total_in, o_ref, acc, peak, total
):
    request = pl.program_id(0)
    block = pl.program_id(1)
    length = length_ref[request]
    prompt_blocks = PROMPT_TOKENS // KEY_BLOCK
    row_count = q_ref.shape[1]
    absorb = absorber(q_ref, peak, total, acc)

    @pl.when(block == 0)
    def _():
        peak[...] = peak_in[...]
        total[...] = total_in[...]
        acc[...] = acc_in[...]

    rows = lax.rem(lax.broadcasted_iota(jnp.int32, (row_count, KEY_BLOCK), 0), FRESH_TOKENS)
    cols = lax.broadcasted_iota(jnp.int32, (row_count, KEY_BLOCK), 1)
    prompt_start = block * KEY_BLOCK

    whole = prompt_start > length + FRESH_TOKENS - 1

    @pl.when(((block == 0) | (prompt_start + KEY_BLOCK - 1 > length)) & jnp.logical_not(whole))
    def _():
        spot = prompt_start + cols
        absorb(
            pk_ref[:, 0, 0].reshape(KEY_BLOCK, HEAD_SIZE),
            pv_ref[:, 0, 0].reshape(KEY_BLOCK, HEAD_SIZE),
            (spot < SINKS) | (spot > length + rows),
        )

    @pl.when(whole)
    def _():
        absorb(
            pk_ref[:, 0, 0].reshape(KEY_BLOCK, HEAD_SIZE),
            pv_ref[:, 0, 0].reshape(KEY_BLOCK, HEAD_SIZE),
            None,
        )

    @pl.when(block == prompt_blocks - 1)
    def _():
        o_ref[0] = (acc[0] / total[0]).astype(o_ref.dtype)


def attention(lengths, queries, prompt_kv, window_k, window_v, new_k, new_v):
    local_reqs, row_count, width = queries.shape
    prompt_blocks = PROMPT_TOKENS // KEY_BLOCK
    window_blocks = WINDOW_SPAN // KEY_BLOCK
    key_spec = lambda pick: pl.BlockSpec((1, KEY_BLOCK, width), pick)
    window_pick = lambda r, b, lens: (r, jnp.minimum(b, window_blocks - 1), 0)
    fixed_pick = lambda r, b, lens: (r, 0, 0)
    state_specs = [
        pl.BlockSpec((1, row_count, width), fixed_pick),
        pl.BlockSpec((1, row_count, 1), fixed_pick),
        pl.BlockSpec((1, row_count, 1), fixed_pick),
    ]
    state_shapes = [
        jax.ShapeDtypeStruct((local_reqs, row_count, width), jnp.float32),
        jax.ShapeDtypeStruct((local_reqs, row_count, 1), jnp.float32),
        jax.ShapeDtypeStruct((local_reqs, row_count, 1), jnp.float32),
    ]
    recent_keys = WINDOW_SPAN + FRESH_TOKENS
    state = pl.pallas_call(
        recent_kernel,
        grid_spec=pltpu.PrefetchScalarGridSpec(
            num_scalar_prefetch=1,
            grid=(local_reqs, window_blocks + 1),
            in_specs=[
                pl.BlockSpec((1, row_count, width), fixed_pick),
                key_spec(window_pick),
                key_spec(window_pick),
                key_spec(fixed_pick),
                key_spec(fixed_pick),
            ],
            out_specs=state_specs,
        ),
        out_shape=state_shapes,
        cost_estimate=pl.CostEstimate(
            flops=4 * local_reqs * row_count * recent_keys * width,
            transcendentals=local_reqs * row_count * recent_keys,
            bytes_accessed=4 * local_reqs * recent_keys * width,
        ),
    )(lengths, queries, window_k, window_v, new_k, new_v)

    source_rows = prompt_kv.shape[3]
    if source_rows <= KEY_BLOCK:
        prompt_spec = lambda half: pl.BlockSpec(
            (KEY_BLOCK // source_rows, 1, 1, source_rows, width),
            lambda r, b, lens: (b, r, half, 0, 0),
        )
    else:
        per_source = source_rows // KEY_BLOCK
        prompt_spec = lambda half: pl.BlockSpec(
            (1, 1, 1, KEY_BLOCK, width),
            lambda r, b, lens: (b // per_source, r, half, b % per_source, 0),
        )
    return pl.pallas_call(
        prompt_kernel,
        grid_spec=pltpu.PrefetchScalarGridSpec(
            num_scalar_prefetch=1,
            grid=(local_reqs, prompt_blocks),
            in_specs=[
                pl.BlockSpec((1, row_count, width), fixed_pick),
                prompt_spec(0),
                prompt_spec(1),
            ]
            + state_specs,
            out_specs=pl.BlockSpec((1, row_count, width), fixed_pick),
            scratch_shapes=[
                pltpu.VMEM((1, row_count, width), jnp.float32),
                pltpu.VMEM((1, row_count, 1), jnp.float32),
                pltpu.VMEM((1, row_count, 1), jnp.float32),
            ],
        ),
        out_shape=jax.ShapeDtypeStruct(queries.shape, jnp.bfloat16),
        cost_estimate=pl.CostEstimate(
            flops=4 * local_reqs * row_count * PROMPT_TOKENS * width,
            transcendentals=local_reqs * row_count * PROMPT_TOKENS,
            bytes_accessed=4 * local_reqs * PROMPT_TOKENS * width,
        ),
    )(lengths, queries, prompt_kv, prompt_kv, *state)


def exchange_kernel(piece_ref, other_ref, send_sem, recv_sem):
    partner = (
        lax.axis_index("dp"),
        1 - lax.axis_index("zh"),
        lax.axis_index("y"),
    )
    barrier = pltpu.get_barrier_semaphore()
    pl.semaphore_signal(
        barrier, 1, device_id=partner, device_id_type=pl.DeviceIdType.MESH
    )
    pl.semaphore_wait(barrier, 1)
    copy = pltpu.make_async_remote_copy(
        src_ref=piece_ref,
        dst_ref=other_ref,
        send_sem=send_sem,
        recv_sem=recv_sem,
        device_id=partner,
        device_id_type=pl.DeviceIdType.MESH,
    )
    copy.start()
    copy.wait()


def exchange(piece, call_id):
    return pl.pallas_call(
        exchange_kernel,
        out_shape=jax.ShapeDtypeStruct(piece.shape, piece.dtype),
        in_specs=[pl.BlockSpec(memory_space=pl.ANY)],
        out_specs=pl.BlockSpec(memory_space=pl.ANY),
        scratch_shapes=[pltpu.SemaphoreType.DMA, pltpu.SemaphoreType.DMA],
        compiler_params=pltpu.CompilerParams(collective_id=call_id, has_side_effects=True),
    )(piece)


def pair_rows(piece, call_id):
    upper = lax.axis_index("zh") == 1
    other = exchange(piece, call_id)
    return jnp.stack([jnp.where(upper, other, piece), jnp.where(upper, piece, other)])


def gather_rows(pair):
    return lax.all_gather(pair, "y", axis=0, tiled=True).reshape((-1,) + pair.shape[2:])


def reduce_rows(full, call_id):
    y_size = lax.axis_size("y")
    zh_size = lax.axis_size("zh")
    split = full.reshape((y_size * zh_size, full.shape[0] // (y_size * zh_size)) + full.shape[1:])
    part = lax.psum_scatter(split, "y", scatter_dimension=0, tiled=True)
    return part.astype(jnp.float32) + exchange(part, call_id).astype(jnp.float32)


def scatter_rows(full, call_id):
    y_size = lax.axis_size("y")
    zh_size = lax.axis_size("zh")
    split = full.reshape((y_size * zh_size, full.shape[0] // (y_size * zh_size)) + full.shape[1:])
    part = lax.psum_scatter(split, "y", scatter_dimension=0, tiled=True)
    me = lax.axis_index("zh")
    mine = lax.dynamic_index_in_dim(part, me, 0, keepdims=False)
    outgoing = lax.dynamic_index_in_dim(part, 1 - me, 0, keepdims=False)
    return mine.astype(jnp.float32) + exchange(outgoing, call_id).astype(jnp.float32)


def prompt_for_requests(prompt_keys, prompt_values, prompt_group):
    dp_size = lax.axis_size("dp")
    wanted = lax.all_to_all(
        jnp.broadcast_to(prompt_group[None], (dp_size,) + prompt_group.shape), "dp", 0, 0, tiled=False
    )
    both = jnp.stack([prompt_keys, prompt_values], axis=1)
    outgoing = jnp.take(both, wanted, axis=0)
    return lax.all_to_all(outgoing, "dp", 0, 0, tiled=False)


def body(
    tokens,
    cached_len,
    prompt_group,
    attn_gain,
    w_query,
    key_matrix,
    value_matrix,
    w_out,
    window_cache_keys,
    window_cache_values,
    prompt_keys,
    prompt_values,
    mlp_gain,
    w_gate,
    w_up,
    w_down,
):
    local_rows = tokens.shape[0]
    local_reqs = tokens.shape[1]
    query_cols = w_query.shape[1]
    key_cols = key_matrix.shape[1]
    hidden_cols = w_gate.shape[1]
    key_heads = key_cols // HEAD_SIZE
    query_group_width = query_cols // key_cols
    score_scale = 1.0 / math.sqrt(HEAD_SIZE)
    token_pair = pair_rows(tokens.reshape(local_rows * local_reqs, MODEL_WIDTH), 0)
    source = norm_rows(token_pair, attn_gain)
    offset = 0
    flattened_rows = gather_rows(source)
    row_count = flattened_rows.shape[0] // local_reqs
    y_size = lax.axis_size("y")
    zh_size = lax.axis_size("zh")
    gathered_row = jnp.arange(row_count, dtype=jnp.int32)
    token_of_row = (
        (gathered_row // (zh_size * local_rows) + y_size * ((gathered_row // local_rows) % zh_size))
        * local_rows
        + gathered_row % local_rows
    )
    positions = PROMPT_TOKENS + cached_len[None, :] + token_of_row[:, None]
    project_queries = jnp.dot(flattened_rows, w_query, preferred_element_type=jnp.float32).reshape(
        row_count, local_reqs, query_cols // HEAD_SIZE, HEAD_SIZE
    )
    fresh_keys = jnp.dot(flattened_rows, key_matrix, preferred_element_type=jnp.float32).reshape(
        row_count, local_reqs, key_heads, HEAD_SIZE
    )
    fresh_values = (
        jnp.dot(flattened_rows, value_matrix, preferred_element_type=jnp.float32)
        .astype(jnp.bfloat16)
        .reshape(row_count, local_reqs, key_cols)
    )
    project_queries = (
        rotate(project_queries, positions)
        .astype(jnp.bfloat16)
        .reshape(row_count, local_reqs, query_cols)
    )
    fresh_keys = (
        rotate(fresh_keys, positions).astype(jnp.bfloat16).reshape(row_count, local_reqs, key_cols)
    )
    query_heads = query_cols // HEAD_SIZE
    grid_rows = (y_size, zh_size, local_rows, local_reqs)
    queries = (
        project_queries.reshape(grid_rows + (query_heads, HEAD_SIZE))
        .transpose(3, 4, 1, 0, 2, 5)
        .reshape(local_reqs, query_heads * row_count, HEAD_SIZE)
    )
    own_keys = (
        fresh_keys.reshape(grid_rows + (HEAD_SIZE,))
        .transpose(3, 1, 0, 2, 4)
        .reshape(local_reqs, row_count, HEAD_SIZE)
    )
    own_values = (
        fresh_values.reshape(grid_rows + (HEAD_SIZE,))
        .transpose(3, 1, 0, 2, 4)
        .reshape(local_reqs, row_count, HEAD_SIZE)
    )
    prompt_kv = prompt_for_requests(prompt_keys, prompt_values, prompt_group)
    attended = attention(
        cached_len, queries, prompt_kv, window_cache_keys, window_cache_values, own_keys, own_values
    )
    attended = (
        attended.reshape(local_reqs, query_heads, zh_size, y_size, local_rows, HEAD_SIZE)
        .transpose(3, 2, 4, 0, 1, 5)
        .reshape(row_count, local_reqs, query_cols)
    )
    blocks = lax.axis_size("y") * lax.axis_size("zh")
    block_rows = local_rows * local_reqs
    chunks = 2
    chunk_rows = block_rows // chunks
    rows_by_block = attended.reshape(blocks, block_rows, query_cols)
    residual_parts = []
    mlp_parts = []
    for chunk in range(chunks):
        picked = rows_by_block[:, chunk * chunk_rows : (chunk + 1) * chunk_rows].reshape(
            blocks * chunk_rows, query_cols
        )
        attn_pair = reduce_rows(
            jnp.dot(picked, w_out, preferred_element_type=jnp.float32).astype(jnp.bfloat16),
            1 + chunk,
        )
        token_chunk = token_pair[:, chunk * chunk_rows : (chunk + 1) * chunk_rows]
        residual_pair = (token_chunk.astype(jnp.float32) + attn_pair).astype(jnp.bfloat16)
        residual_parts.append(
            lax.dynamic_index_in_dim(residual_pair, lax.axis_index("zh"), 0, keepdims=False)
        )
        flattened_rows = gather_rows(norm_rows(residual_pair, mlp_gain))
        gate_part = jnp.dot(flattened_rows, w_gate, preferred_element_type=jnp.float32)
        up_part = jnp.dot(flattened_rows, w_up, preferred_element_type=jnp.float32)
        hidden = (jax.nn.silu(gate_part) * up_part).astype(jnp.bfloat16)
        mlp_parts.append(
            scatter_rows(
                jnp.dot(hidden, w_down, preferred_element_type=jnp.float32).astype(jnp.bfloat16),
                1 + chunks + chunk,
            )
        )
    residual = jnp.concatenate(residual_parts, axis=0).reshape(tokens.shape)
    mlp_part = jnp.concatenate(mlp_parts, axis=0).reshape(tokens.shape)
    return (residual.astype(jnp.float32) + mlp_part).astype(jnp.bfloat16)


def solution(mesh):
    zh_size = 2
    split_mesh = jax.sharding.Mesh(
        mesh.devices.reshape(mesh.devices.shape[0], zh_size, -1), ("dp", "zh", "y")
    )
    rows = ("zh", "y")
    in_specs = (
        P(rows, "dp", None),
        P("dp"),
        P("dp"),
        P(),
        P(None, rows),
        P(None, rows),
        P(None, rows),
        P(rows, None),
        P("dp", None, rows),
        P("dp", None, rows),
        P(None, "dp", rows),
        P(None, "dp", rows),
        P(),
        P(None, rows),
        P(None, rows),
        P(rows, None),
    )
    out_specs = P(rows, "dp", None)
    return jax.shard_map(
        body, mesh=split_mesh, in_specs=in_specs, out_specs=out_specs, check_vma=False
    )
```

```python
import math

import jax
import jax.numpy as jnp
from jax import lax
from jax.sharding import PartitionSpec as P
from jax.experimental import pallas as pl
from jax.experimental.pallas import tpu as pltpu

MODEL_WIDTH = 1536
HEAD_SIZE = 96
FRESH_TOKENS = 512
WINDOW_SPAN = 4096
SINKS = 4
PROMPT_TOKENS = 4096


rope_base = 10000.0
epsilon = 1e-05
far_below = -1e30


def norm_rows(values, gain_vec):
    widened = values.astype(jnp.float32)
    factor = lax.rsqrt(jnp.mean(widened * widened, axis=-1, keepdims=True) + epsilon)
    return (widened * factor * gain_vec).astype(jnp.bfloat16)


def rotate(values, positions):
    half_dim = values.shape[-1] // 2
    frequency = rope_base ** (-2.0 * jnp.arange(half_dim, dtype=jnp.float32) / values.shape[-1])
    angles = positions.astype(jnp.float32)[..., None, None] * frequency
    cosine = jnp.cos(angles)
    sine_part = jnp.sin(angles)
    first_half = values[..., :half_dim]
    second_half = values[..., half_dim:]
    return jnp.concatenate(
        [
            first_half * cosine - second_half * sine_part,
            second_half * cosine + first_half * sine_part,
        ],
        axis=-1,
    )


KEY_BLOCK = 512


def absorber(q_ref, peak, total, acc):
    score_scale = 1.0 / math.sqrt(HEAD_SIZE)

    def absorb(keys, values, visible, flipped=False):
        scores = (
            lax.dot_general(
                q_ref[0],
                keys,
                (((1,), (0 if flipped else 1,)), ((), ())),
                preferred_element_type=jnp.float32,
            )
            * score_scale
        )
        if visible is not None:
            scores = jnp.where(visible, scores, -jnp.inf)
        old_peak = peak[0]
        new_peak = jnp.maximum(old_peak, jnp.max(scores, axis=-1, keepdims=True))
        factor = jnp.exp(old_peak - new_peak)
        weights = jnp.exp(scores - new_peak)
        total[0] = total[0] * factor + jnp.sum(weights, axis=-1, keepdims=True)
        acc[0] = acc[0] * factor + lax.dot_general(
            weights.astype(jnp.bfloat16),
            values,
            (((1,), (1 if flipped else 0,)), ((), ())),
            preferred_element_type=jnp.float32,
        )
        peak[0] = new_peak

    return absorb


def recent_kernel(length_ref, q_ref, wk_ref, wv_ref, nk_ref, nv_ref, acc, peak, total):
    request = pl.program_id(0)
    block = pl.program_id(1)
    length = length_ref[request]
    window_blocks = WINDOW_SPAN // KEY_BLOCK
    row_count = q_ref.shape[1]
    absorb = absorber(q_ref, peak, total, acc)

    @pl.when(block == 0)
    def _():
        peak[...] = jnp.full(peak.shape, far_below, jnp.float32)
        total[...] = jnp.zeros(total.shape, jnp.float32)
        acc[...] = jnp.zeros(acc.shape, jnp.float32)

    rows = lax.rem(lax.broadcasted_iota(jnp.int32, (row_count, KEY_BLOCK), 0), FRESH_TOKENS)
    cols = lax.broadcasted_iota(jnp.int32, (row_count, KEY_BLOCK), 1)
    window_start = block * KEY_BLOCK

    whole = (window_start >= WINDOW_SPAN - length) & (window_start >= FRESH_TOKENS)

    @pl.when(
        (block < window_blocks)
        & (window_start + KEY_BLOCK - 1 >= WINDOW_SPAN - length)
        & jnp.logical_not(whole)
    )
    def _():
        slot = window_start + cols
        absorb(wk_ref[0], wv_ref[0], (slot >= WINDOW_SPAN - length) & (slot > rows))

    @pl.when((block < window_blocks) & whole)
    def _():
        absorb(wk_ref[0], wv_ref[0], None)

    @pl.when(block == window_blocks)
    def _():
        absorb(nk_ref[0], nv_ref[0], cols <= rows)


def flip(block_ref):
    pieces = block_ref.shape[0]
    if pieces == 1:
        return block_ref[0, 0, 0]
    return jnp.concatenate([block_ref[piece, 0, 0] for piece in range(pieces)], axis=1)


def prompt_kernel(
    length_ref, q_ref, pk_ref, pv_ref, acc_in, peak_in, total_in, o_ref, acc, peak, total
):
    request = pl.program_id(0)
    block = pl.program_id(1)
    length = length_ref[request]
    prompt_blocks = PROMPT_TOKENS // KEY_BLOCK
    row_count = q_ref.shape[1]
    absorb = absorber(q_ref, peak, total, acc)

    @pl.when(block == 0)
    def _():
        peak[...] = peak_in[...]
        total[...] = total_in[...]
        acc[...] = acc_in[...]

    rows = lax.rem(lax.broadcasted_iota(jnp.int32, (row_count, KEY_BLOCK), 0), FRESH_TOKENS)
    cols = lax.broadcasted_iota(jnp.int32, (row_count, KEY_BLOCK), 1)
    prompt_start = block * KEY_BLOCK

    whole = prompt_start > length + FRESH_TOKENS - 1

    @pl.when(((block == 0) | (prompt_start + KEY_BLOCK - 1 > length)) & jnp.logical_not(whole))
    def _():
        spot = prompt_start + cols
        absorb(flip(pk_ref), flip(pv_ref), (spot < SINKS) | (spot > length + rows), True)

    @pl.when(whole)
    def _():
        absorb(flip(pk_ref), flip(pv_ref), None, True)

    @pl.when(block == prompt_blocks - 1)
    def _():
        o_ref[0] = (acc[0] / total[0]).astype(o_ref.dtype)


def attention(lengths, queries, prompt_kv, window_k, window_v, new_k, new_v):
    local_reqs, row_count, width = queries.shape
    prompt_blocks = PROMPT_TOKENS // KEY_BLOCK
    window_blocks = WINDOW_SPAN // KEY_BLOCK
    key_spec = lambda pick: pl.BlockSpec((1, KEY_BLOCK, width), pick)
    window_pick = lambda r, b, lens: (r, jnp.minimum(b, window_blocks - 1), 0)
    fixed_pick = lambda r, b, lens: (r, 0, 0)
    state_specs = [
        pl.BlockSpec((1, row_count, width), fixed_pick),
        pl.BlockSpec((1, row_count, 1), fixed_pick),
        pl.BlockSpec((1, row_count, 1), fixed_pick),
    ]
    state_shapes = [
        jax.ShapeDtypeStruct((local_reqs, row_count, width), jnp.float32),
        jax.ShapeDtypeStruct((local_reqs, row_count, 1), jnp.float32),
        jax.ShapeDtypeStruct((local_reqs, row_count, 1), jnp.float32),
    ]
    recent_keys = WINDOW_SPAN + FRESH_TOKENS
    state = pl.pallas_call(
        recent_kernel,
        grid_spec=pltpu.PrefetchScalarGridSpec(
            num_scalar_prefetch=1,
            grid=(local_reqs, window_blocks + 1),
            in_specs=[
                pl.BlockSpec((1, row_count, width), fixed_pick),
                key_spec(window_pick),
                key_spec(window_pick),
                key_spec(fixed_pick),
                key_spec(fixed_pick),
            ],
            out_specs=state_specs,
        ),
        out_shape=state_shapes,
        cost_estimate=pl.CostEstimate(
            flops=4 * local_reqs * row_count * recent_keys * width,
            transcendentals=local_reqs * row_count * recent_keys,
            bytes_accessed=4 * local_reqs * recent_keys * width,
        ),
    )(lengths, queries, window_k, window_v, new_k, new_v)

    prompt_kv = jnp.swapaxes(prompt_kv, 3, 4)
    source_rows = prompt_kv.shape[4]
    if source_rows <= KEY_BLOCK:
        prompt_spec = lambda half: pl.BlockSpec(
            (KEY_BLOCK // source_rows, 1, 1, width, source_rows),
            lambda r, b, lens: (b, r, half, 0, 0),
        )
    else:
        per_source = source_rows // KEY_BLOCK
        prompt_spec = lambda half: pl.BlockSpec(
            (1, 1, 1, width, KEY_BLOCK),
            lambda r, b, lens: (b // per_source, r, half, 0, b % per_source),
        )
    return pl.pallas_call(
        prompt_kernel,
        grid_spec=pltpu.PrefetchScalarGridSpec(
            num_scalar_prefetch=1,
            grid=(local_reqs, prompt_blocks),
            in_specs=[
                pl.BlockSpec((1, row_count, width), fixed_pick),
                prompt_spec(0),
                prompt_spec(1),
            ]
            + state_specs,
            out_specs=pl.BlockSpec((1, row_count, width), fixed_pick),
            scratch_shapes=[
                pltpu.VMEM((1, row_count, width), jnp.float32),
                pltpu.VMEM((1, row_count, 1), jnp.float32),
                pltpu.VMEM((1, row_count, 1), jnp.float32),
            ],
        ),
        out_shape=jax.ShapeDtypeStruct(queries.shape, jnp.bfloat16),
        cost_estimate=pl.CostEstimate(
            flops=4 * local_reqs * row_count * PROMPT_TOKENS * width,
            transcendentals=local_reqs * row_count * PROMPT_TOKENS,
            bytes_accessed=4 * local_reqs * PROMPT_TOKENS * width,
        ),
    )(lengths, queries, prompt_kv, prompt_kv, *state)


def exchange_kernel(piece_ref, other_ref, send_sem, recv_sem):
    partner = (
        lax.axis_index("dp"),
        1 - lax.axis_index("zh"),
        lax.axis_index("y"),
    )
    barrier = pltpu.get_barrier_semaphore()
    pl.semaphore_signal(
        barrier, 1, device_id=partner, device_id_type=pl.DeviceIdType.MESH
    )
    pl.semaphore_wait(barrier, 1)
    copy = pltpu.make_async_remote_copy(
        src_ref=piece_ref,
        dst_ref=other_ref,
        send_sem=send_sem,
        recv_sem=recv_sem,
        device_id=partner,
        device_id_type=pl.DeviceIdType.MESH,
    )
    copy.start()
    copy.wait()


def exchange(piece, call_id):
    return pl.pallas_call(
        exchange_kernel,
        out_shape=jax.ShapeDtypeStruct(piece.shape, piece.dtype),
        in_specs=[pl.BlockSpec(memory_space=pl.ANY)],
        out_specs=pl.BlockSpec(memory_space=pl.ANY),
        scratch_shapes=[pltpu.SemaphoreType.DMA, pltpu.SemaphoreType.DMA],
        compiler_params=pltpu.CompilerParams(collective_id=call_id, has_side_effects=True),
    )(piece)


def pair_rows(piece, call_id):
    upper = lax.axis_index("zh") == 1
    other = exchange(piece, call_id)
    return jnp.stack([jnp.where(upper, other, piece), jnp.where(upper, piece, other)])


def gather_rows(pair):
    return lax.all_gather(pair, "y", axis=0, tiled=True).reshape((-1,) + pair.shape[2:])


def reduce_rows(full, call_id):
    y_size = lax.axis_size("y")
    zh_size = lax.axis_size("zh")
    split = full.reshape((y_size * zh_size, full.shape[0] // (y_size * zh_size)) + full.shape[1:])
    part = lax.psum_scatter(split, "y", scatter_dimension=0, tiled=True)
    return part.astype(jnp.float32) + exchange(part, call_id).astype(jnp.float32)


def scatter_rows(full, call_id):
    y_size = lax.axis_size("y")
    zh_size = lax.axis_size("zh")
    split = full.reshape((y_size * zh_size, full.shape[0] // (y_size * zh_size)) + full.shape[1:])
    part = lax.psum_scatter(split, "y", scatter_dimension=0, tiled=True)
    me = lax.axis_index("zh")
    mine = lax.dynamic_index_in_dim(part, me, 0, keepdims=False)
    outgoing = lax.dynamic_index_in_dim(part, 1 - me, 0, keepdims=False)
    return mine.astype(jnp.float32) + exchange(outgoing, call_id).astype(jnp.float32)


def prompt_for_requests(prompt_keys, prompt_values, prompt_group):
    dp_size = lax.axis_size("dp")
    wanted = lax.all_to_all(
        jnp.broadcast_to(prompt_group[None], (dp_size,) + prompt_group.shape), "dp", 0, 0, tiled=False
    )
    both = jnp.stack([prompt_keys, prompt_values], axis=1)
    outgoing = jnp.take(both, wanted, axis=0)
    return lax.all_to_all(outgoing, "dp", 0, 0, tiled=False)


def body(
    tokens,
    cached_len,
    prompt_group,
    attn_gain,
    w_query,
    key_matrix,
    value_matrix,
    w_out,
    window_cache_keys,
    window_cache_values,
    prompt_keys,
    prompt_values,
    mlp_gain,
    w_gate,
    w_up,
    w_down,
):
    local_rows = tokens.shape[0]
    local_reqs = tokens.shape[1]
    query_cols = w_query.shape[1]
    key_cols = key_matrix.shape[1]
    hidden_cols = w_gate.shape[1]
    key_heads = key_cols // HEAD_SIZE
    query_group_width = query_cols // key_cols
    score_scale = 1.0 / math.sqrt(HEAD_SIZE)
    token_pair = pair_rows(tokens.reshape(local_rows * local_reqs, MODEL_WIDTH), 0)
    source = norm_rows(token_pair, attn_gain)
    offset = 0
    flattened_rows = gather_rows(source)
    row_count = flattened_rows.shape[0] // local_reqs
    y_size = lax.axis_size("y")
    zh_size = lax.axis_size("zh")
    gathered_row = jnp.arange(row_count, dtype=jnp.int32)
    token_of_row = (
        (gathered_row // (zh_size * local_rows) + y_size * ((gathered_row // local_rows) % zh_size))
        * local_rows
        + gathered_row % local_rows
    )
    positions = PROMPT_TOKENS + cached_len[None, :] + token_of_row[:, None]
    project_queries = jnp.dot(flattened_rows, w_query, preferred_element_type=jnp.float32).reshape(
        row_count, local_reqs, query_cols // HEAD_SIZE, HEAD_SIZE
    )
    fresh_keys = jnp.dot(flattened_rows, key_matrix, preferred_element_type=jnp.float32).reshape(
        row_count, local_reqs, key_heads, HEAD_SIZE
    )
    fresh_values = (
        jnp.dot(flattened_rows, value_matrix, preferred_element_type=jnp.float32)
        .astype(jnp.bfloat16)
        .reshape(row_count, local_reqs, key_cols)
    )
    project_queries = (
        rotate(project_queries, positions)
        .astype(jnp.bfloat16)
        .reshape(row_count, local_reqs, query_cols)
    )
    fresh_keys = (
        rotate(fresh_keys, positions).astype(jnp.bfloat16).reshape(row_count, local_reqs, key_cols)
    )
    query_heads = query_cols // HEAD_SIZE
    grid_rows = (y_size, zh_size, local_rows, local_reqs)
    queries = (
        project_queries.reshape(grid_rows + (query_heads, HEAD_SIZE))
        .transpose(3, 4, 1, 0, 2, 5)
        .reshape(local_reqs, query_heads * row_count, HEAD_SIZE)
    )
    own_keys = (
        fresh_keys.reshape(grid_rows + (HEAD_SIZE,))
        .transpose(3, 1, 0, 2, 4)
        .reshape(local_reqs, row_count, HEAD_SIZE)
    )
    own_values = (
        fresh_values.reshape(grid_rows + (HEAD_SIZE,))
        .transpose(3, 1, 0, 2, 4)
        .reshape(local_reqs, row_count, HEAD_SIZE)
    )
    prompt_kv = prompt_for_requests(prompt_keys, prompt_values, prompt_group)
    attended = attention(
        cached_len, queries, prompt_kv, window_cache_keys, window_cache_values, own_keys, own_values
    )
    attended = (
        attended.reshape(local_reqs, query_heads, zh_size, y_size, local_rows, HEAD_SIZE)
        .transpose(3, 2, 4, 0, 1, 5)
        .reshape(row_count, local_reqs, query_cols)
    )
    picked = attended
    attn_pair = reduce_rows(
        jnp.dot(
            picked.reshape(FRESH_TOKENS * local_reqs, query_cols),
            w_out,
            preferred_element_type=jnp.float32,
        ).astype(jnp.bfloat16),
        1,
    )
    residual_pair = (token_pair.astype(jnp.float32) + attn_pair).astype(jnp.bfloat16)
    residual = lax.dynamic_index_in_dim(
        residual_pair, lax.axis_index("zh"), 0, keepdims=False
    ).reshape(tokens.shape)
    flattened_rows = gather_rows(norm_rows(residual_pair, mlp_gain))
    gate_part = jnp.dot(flattened_rows, w_gate, preferred_element_type=jnp.float32)
    up_part = jnp.dot(flattened_rows, w_up, preferred_element_type=jnp.float32)
    hidden = (jax.nn.silu(gate_part) * up_part).astype(jnp.bfloat16)
    mlp_part = scatter_rows(
        jnp.dot(hidden, w_down, preferred_element_type=jnp.float32).astype(jnp.bfloat16),
        3,
    ).reshape(tokens.shape)
    return (residual.astype(jnp.float32) + mlp_part).astype(jnp.bfloat16)


def solution(mesh):
    zh_size = 2
    split_mesh = jax.sharding.Mesh(
        mesh.devices.reshape(mesh.devices.shape[0], zh_size, -1), ("dp", "zh", "y")
    )
    rows = ("zh", "y")
    in_specs = (
        P(rows, "dp", None),
        P("dp"),
        P("dp"),
        P(),
        P(None, rows),
        P(None, rows),
        P(None, rows),
        P(rows, None),
        P("dp", None, rows),
        P("dp", None, rows),
        P(None, "dp", rows),
        P(None, "dp", rows),
        P(),
        P(None, rows),
        P(None, rows),
        P(rows, None),
    )
    out_specs = P(rows, "dp", None)
    return jax.shard_map(
        body, mesh=split_mesh, in_specs=in_specs, out_specs=out_specs, check_vma=False
    )
```

```python
import math

import jax
import jax.numpy as jnp
from jax import lax
from jax.sharding import PartitionSpec as P
from jax.experimental import pallas as pl
from jax.experimental.pallas import tpu as pltpu

MODEL_WIDTH = 1536
HEAD_SIZE = 96
FRESH_TOKENS = 512
WINDOW_SPAN = 4096
SINKS = 4
PROMPT_TOKENS = 4096


rope_base = 10000.0
epsilon = 1e-05
far_below = -1e30


def norm_rows(values, gain_vec):
    widened = values.astype(jnp.float32)
    factor = lax.rsqrt(jnp.mean(widened * widened, axis=-1, keepdims=True) + epsilon)
    return (widened * factor * gain_vec).astype(jnp.bfloat16)


def rotate(values, positions):
    half_dim = values.shape[-1] // 2
    frequency = rope_base ** (-2.0 * jnp.arange(half_dim, dtype=jnp.float32) / values.shape[-1])
    angles = positions.astype(jnp.float32)[..., None, None] * frequency
    cosine = jnp.cos(angles)
    sine_part = jnp.sin(angles)
    first_half = values[..., :half_dim]
    second_half = values[..., half_dim:]
    return jnp.concatenate(
        [
            first_half * cosine - second_half * sine_part,
            second_half * cosine + first_half * sine_part,
        ],
        axis=-1,
    )


KEY_BLOCK = 512


def absorber(q_ref, peak, total, acc):
    score_scale = 1.0 / math.sqrt(HEAD_SIZE)

    def absorb(keys, values, visible, flipped=False):
        scores = (
            lax.dot_general(
                q_ref[0],
                keys,
                (((1,), (0 if flipped else 1,)), ((), ())),
                preferred_element_type=jnp.float32,
            )
            * score_scale
        )
        if visible is not None:
            scores = jnp.where(visible, scores, -jnp.inf)
        old_peak = peak[0]
        new_peak = jnp.maximum(old_peak, jnp.max(scores, axis=-1, keepdims=True))
        factor = jnp.exp(old_peak - new_peak)
        weights = jnp.exp(scores - new_peak)
        total[0] = total[0] * factor + jnp.sum(weights, axis=-1, keepdims=True)
        acc[0] = acc[0] * factor + lax.dot_general(
            weights.astype(jnp.bfloat16),
            values,
            (((1,), (1 if flipped else 0,)), ((), ())),
            preferred_element_type=jnp.float32,
        )
        peak[0] = new_peak

    return absorb


def recent_kernel(length_ref, q_ref, wk_ref, wv_ref, nk_ref, nv_ref, acc, peak, total):
    request = pl.program_id(0)
    block = pl.program_id(1)
    length = length_ref[request]
    window_blocks = WINDOW_SPAN // KEY_BLOCK
    row_count = q_ref.shape[1]
    absorb = absorber(q_ref, peak, total, acc)

    @pl.when(block == 0)
    def _():
        peak[...] = jnp.full(peak.shape, far_below, jnp.float32)
        total[...] = jnp.zeros(total.shape, jnp.float32)
        acc[...] = jnp.zeros(acc.shape, jnp.float32)

    rows = lax.rem(lax.broadcasted_iota(jnp.int32, (row_count, KEY_BLOCK), 0), FRESH_TOKENS)
    cols = lax.broadcasted_iota(jnp.int32, (row_count, KEY_BLOCK), 1)
    window_start = block * KEY_BLOCK

    whole = (window_start >= WINDOW_SPAN - length) & (window_start >= FRESH_TOKENS)

    @pl.when(
        (block < window_blocks)
        & (window_start + KEY_BLOCK - 1 >= WINDOW_SPAN - length)
        & jnp.logical_not(whole)
    )
    def _():
        slot = window_start + cols
        absorb(wk_ref[0], wv_ref[0], (slot >= WINDOW_SPAN - length) & (slot > rows))

    @pl.when((block < window_blocks) & whole)
    def _():
        absorb(wk_ref[0], wv_ref[0], None)

    @pl.when(block == window_blocks)
    def _():
        absorb(nk_ref[0], nv_ref[0], cols <= rows)


def flip(block_ref):
    pieces = block_ref.shape[0]
    if pieces == 1:
        return block_ref[0, 0, 0]
    return jnp.concatenate([block_ref[piece, 0, 0] for piece in range(pieces)], axis=1)


def prompt_kernel(
    length_ref, q_ref, pk_ref, pv_ref, acc_in, peak_in, total_in, o_ref, acc, peak, total
):
    request = pl.program_id(0)
    block = pl.program_id(1)
    length = length_ref[request]
    prompt_blocks = PROMPT_TOKENS // KEY_BLOCK
    row_count = q_ref.shape[1]
    absorb = absorber(q_ref, peak, total, acc)

    @pl.when(block == 0)
    def _():
        peak[...] = peak_in[...]
        total[...] = total_in[...]
        acc[...] = acc_in[...]

    rows = lax.rem(lax.broadcasted_iota(jnp.int32, (row_count, KEY_BLOCK), 0), FRESH_TOKENS)
    cols = lax.broadcasted_iota(jnp.int32, (row_count, KEY_BLOCK), 1)
    prompt_start = block * KEY_BLOCK

    whole = prompt_start > length + FRESH_TOKENS - 1

    @pl.when(((block == 0) | (prompt_start + KEY_BLOCK - 1 > length)) & jnp.logical_not(whole))
    def _():
        spot = prompt_start + cols
        absorb(flip(pk_ref), flip(pv_ref), (spot < SINKS) | (spot > length + rows), True)

    @pl.when(whole)
    def _():
        absorb(flip(pk_ref), flip(pv_ref), None, True)

    @pl.when(block == prompt_blocks - 1)
    def _():
        o_ref[0] = (acc[0] / total[0]).astype(o_ref.dtype)


def attention(lengths, queries, prompt_kv, window_k, window_v, new_k, new_v):
    local_reqs, row_count, width = queries.shape
    prompt_blocks = PROMPT_TOKENS // KEY_BLOCK
    window_blocks = WINDOW_SPAN // KEY_BLOCK
    key_spec = lambda pick: pl.BlockSpec((1, KEY_BLOCK, width), pick)
    window_pick = lambda r, b, lens: (r, jnp.minimum(b, window_blocks - 1), 0)
    fixed_pick = lambda r, b, lens: (r, 0, 0)
    state_specs = [
        pl.BlockSpec((1, row_count, width), fixed_pick),
        pl.BlockSpec((1, row_count, 1), fixed_pick),
        pl.BlockSpec((1, row_count, 1), fixed_pick),
    ]
    state_shapes = [
        jax.ShapeDtypeStruct((local_reqs, row_count, width), jnp.float32),
        jax.ShapeDtypeStruct((local_reqs, row_count, 1), jnp.float32),
        jax.ShapeDtypeStruct((local_reqs, row_count, 1), jnp.float32),
    ]
    recent_keys = WINDOW_SPAN + FRESH_TOKENS
    state = pl.pallas_call(
        recent_kernel,
        grid_spec=pltpu.PrefetchScalarGridSpec(
            num_scalar_prefetch=1,
            grid=(local_reqs, window_blocks + 1),
            in_specs=[
                pl.BlockSpec((1, row_count, width), fixed_pick),
                key_spec(window_pick),
                key_spec(window_pick),
                key_spec(fixed_pick),
                key_spec(fixed_pick),
            ],
            out_specs=state_specs,
        ),
        out_shape=state_shapes,
        cost_estimate=pl.CostEstimate(
            flops=4 * local_reqs * row_count * recent_keys * width,
            transcendentals=local_reqs * row_count * recent_keys,
            bytes_accessed=4 * local_reqs * recent_keys * width,
        ),
    )(lengths, queries, window_k, window_v, new_k, new_v)

    prompt_kv = jnp.swapaxes(prompt_kv, 3, 4)
    source_rows = prompt_kv.shape[4]
    if source_rows <= KEY_BLOCK:
        prompt_spec = lambda half: pl.BlockSpec(
            (KEY_BLOCK // source_rows, 1, 1, width, source_rows),
            lambda r, b, lens: (b, r, half, 0, 0),
        )
    else:
        per_source = source_rows // KEY_BLOCK
        prompt_spec = lambda half: pl.BlockSpec(
            (1, 1, 1, width, KEY_BLOCK),
            lambda r, b, lens: (b // per_source, r, half, 0, b % per_source),
        )
    return pl.pallas_call(
        prompt_kernel,
        grid_spec=pltpu.PrefetchScalarGridSpec(
            num_scalar_prefetch=1,
            grid=(local_reqs, prompt_blocks),
            in_specs=[
                pl.BlockSpec((1, row_count, width), fixed_pick),
                prompt_spec(0),
                prompt_spec(1),
            ]
            + state_specs,
            out_specs=pl.BlockSpec((1, row_count, width), fixed_pick),
            scratch_shapes=[
                pltpu.VMEM((1, row_count, width), jnp.float32),
                pltpu.VMEM((1, row_count, 1), jnp.float32),
                pltpu.VMEM((1, row_count, 1), jnp.float32),
            ],
        ),
        out_shape=jax.ShapeDtypeStruct(queries.shape, jnp.bfloat16),
        cost_estimate=pl.CostEstimate(
            flops=4 * local_reqs * row_count * PROMPT_TOKENS * width,
            transcendentals=local_reqs * row_count * PROMPT_TOKENS,
            bytes_accessed=4 * local_reqs * PROMPT_TOKENS * width,
        ),
    )(lengths, queries, prompt_kv, prompt_kv, *state)


def exchange_kernel(piece_ref, other_ref, send_sem, recv_sem):
    partner = (
        lax.axis_index("dp"),
        1 - lax.axis_index("zh"),
        lax.axis_index("y"),
    )
    barrier = pltpu.get_barrier_semaphore()
    pl.semaphore_signal(
        barrier, 1, device_id=partner, device_id_type=pl.DeviceIdType.MESH
    )
    pl.semaphore_wait(barrier, 1)
    copy = pltpu.make_async_remote_copy(
        src_ref=piece_ref,
        dst_ref=other_ref,
        send_sem=send_sem,
        recv_sem=recv_sem,
        device_id=partner,
        device_id_type=pl.DeviceIdType.MESH,
    )
    copy.start()
    copy.wait()


def exchange(piece, call_id):
    return pl.pallas_call(
        exchange_kernel,
        out_shape=jax.ShapeDtypeStruct(piece.shape, piece.dtype),
        in_specs=[pl.BlockSpec(memory_space=pl.ANY)],
        out_specs=pl.BlockSpec(memory_space=pl.ANY),
        scratch_shapes=[pltpu.SemaphoreType.DMA, pltpu.SemaphoreType.DMA],
        compiler_params=pltpu.CompilerParams(collective_id=call_id, has_side_effects=True),
    )(piece)


def pair_rows(piece, call_id):
    upper = lax.axis_index("zh") == 1
    other = exchange(piece, call_id)
    return jnp.stack([jnp.where(upper, other, piece), jnp.where(upper, piece, other)])


def gather_rows(pair):
    return lax.all_gather(pair, "y", axis=0, tiled=True).reshape((-1,) + pair.shape[2:])


def reduce_rows(full, call_id):
    y_size = lax.axis_size("y")
    zh_size = lax.axis_size("zh")
    split = full.reshape((y_size * zh_size, full.shape[0] // (y_size * zh_size)) + full.shape[1:])
    part = lax.psum_scatter(split, "y", scatter_dimension=0, tiled=True)
    return part.astype(jnp.float32) + exchange(part, call_id).astype(jnp.float32)


def scatter_rows(full, call_id):
    y_size = lax.axis_size("y")
    zh_size = lax.axis_size("zh")
    split = full.reshape((y_size * zh_size, full.shape[0] // (y_size * zh_size)) + full.shape[1:])
    part = lax.psum_scatter(split, "y", scatter_dimension=0, tiled=True)
    me = lax.axis_index("zh")
    mine = lax.dynamic_index_in_dim(part, me, 0, keepdims=False)
    outgoing = lax.dynamic_index_in_dim(part, 1 - me, 0, keepdims=False)
    return mine.astype(jnp.float32) + exchange(outgoing, call_id).astype(jnp.float32)


def prompt_for_requests(prompt_keys, prompt_values, prompt_group):
    dp_size = lax.axis_size("dp")
    wanted = lax.all_to_all(
        jnp.broadcast_to(prompt_group[None], (dp_size,) + prompt_group.shape), "dp", 0, 0, tiled=False
    )
    both = jnp.stack([prompt_keys, prompt_values], axis=1)
    outgoing = jnp.take(both, wanted, axis=0)
    return lax.all_to_all(outgoing, "dp", 0, 0, tiled=False)


def body(
    tokens,
    cached_len,
    prompt_group,
    attn_gain,
    w_query,
    key_matrix,
    value_matrix,
    w_out,
    window_cache_keys,
    window_cache_values,
    prompt_keys,
    prompt_values,
    mlp_gain,
    w_gate,
    w_up,
    w_down,
):
    local_rows = tokens.shape[0]
    local_reqs = tokens.shape[1]
    query_cols = w_query.shape[1]
    key_cols = key_matrix.shape[1]
    hidden_cols = w_gate.shape[1]
    key_heads = key_cols // HEAD_SIZE
    query_group_width = query_cols // key_cols
    score_scale = 1.0 / math.sqrt(HEAD_SIZE)
    token_pair = pair_rows(tokens.reshape(local_rows * local_reqs, MODEL_WIDTH), 0)
    source = norm_rows(token_pair, attn_gain)
    offset = 0
    flattened_rows = gather_rows(source)
    row_count = flattened_rows.shape[0] // local_reqs
    y_size = lax.axis_size("y")
    zh_size = lax.axis_size("zh")
    block_rows = local_rows * local_reqs
    flat_row = jnp.arange(row_count * local_reqs, dtype=jnp.int32)
    block_of_row = flat_row // block_rows
    token_of_row = (
        (block_of_row % zh_size) * y_size + block_of_row // zh_size
    ) * local_rows + (flat_row % block_rows) // local_reqs
    positions = PROMPT_TOKENS + jnp.take(cached_len, flat_row % local_reqs) + token_of_row
    query_heads = query_cols // HEAD_SIZE
    project_queries = jnp.dot(flattened_rows, w_query, preferred_element_type=jnp.float32).reshape(
        row_count * local_reqs, query_heads, HEAD_SIZE
    )
    fresh_keys = jnp.dot(flattened_rows, key_matrix, preferred_element_type=jnp.float32).reshape(
        row_count * local_reqs, key_heads, HEAD_SIZE
    )
    fresh_values = jnp.dot(flattened_rows, value_matrix, preferred_element_type=jnp.float32).astype(
        jnp.bfloat16
    )
    project_queries = rotate(project_queries, positions).astype(jnp.bfloat16)
    fresh_keys = rotate(fresh_keys, positions).astype(jnp.bfloat16)
    grid_rows = (y_size, zh_size, local_rows, local_reqs)
    queries = (
        project_queries.reshape(grid_rows + (query_heads, HEAD_SIZE))
        .transpose(3, 4, 1, 0, 2, 5)
        .reshape(local_reqs, query_heads * row_count, HEAD_SIZE)
    )
    own_keys = (
        fresh_keys.reshape(grid_rows + (HEAD_SIZE,))
        .transpose(3, 1, 0, 2, 4)
        .reshape(local_reqs, row_count, HEAD_SIZE)
    )
    own_values = (
        fresh_values.reshape(grid_rows + (HEAD_SIZE,))
        .transpose(3, 1, 0, 2, 4)
        .reshape(local_reqs, row_count, HEAD_SIZE)
    )
    prompt_kv = prompt_for_requests(prompt_keys, prompt_values, prompt_group)
    attended = attention(
        cached_len, queries, prompt_kv, window_cache_keys, window_cache_values, own_keys, own_values
    )
    attended = (
        attended.reshape(local_reqs, query_heads, zh_size, y_size, local_rows, HEAD_SIZE)
        .transpose(3, 2, 4, 0, 1, 5)
        .reshape(row_count, local_reqs, query_cols)
    )
    picked = attended
    attn_pair = reduce_rows(
        jnp.dot(
            picked.reshape(FRESH_TOKENS * local_reqs, query_cols),
            w_out,
            preferred_element_type=jnp.float32,
        ).astype(jnp.bfloat16),
        1,
    )
    residual_pair = (token_pair.astype(jnp.float32) + attn_pair).astype(jnp.bfloat16)
    residual = lax.dynamic_index_in_dim(
        residual_pair, lax.axis_index("zh"), 0, keepdims=False
    ).reshape(tokens.shape)
    flattened_rows = gather_rows(norm_rows(residual_pair, mlp_gain))
    gate_part = jnp.dot(flattened_rows, w_gate, preferred_element_type=jnp.float32)
    up_part = jnp.dot(flattened_rows, w_up, preferred_element_type=jnp.float32)
    hidden = (jax.nn.silu(gate_part) * up_part).astype(jnp.bfloat16)
    mlp_part = scatter_rows(
        jnp.dot(hidden, w_down, preferred_element_type=jnp.float32).astype(jnp.bfloat16),
        3,
    ).reshape(tokens.shape)
    return (residual.astype(jnp.float32) + mlp_part).astype(jnp.bfloat16)


def solution(mesh):
    zh_size = 2
    split_mesh = jax.sharding.Mesh(
        mesh.devices.reshape(mesh.devices.shape[0], zh_size, -1), ("dp", "zh", "y")
    )
    rows = ("zh", "y")
    in_specs = (
        P(rows, "dp", None),
        P("dp"),
        P("dp"),
        P(),
        P(None, rows),
        P(None, rows),
        P(None, rows),
        P(rows, None),
        P("dp", None, rows),
        P("dp", None, rows),
        P(None, "dp", rows),
        P(None, "dp", rows),
        P(),
        P(None, rows),
        P(None, rows),
        P(rows, None),
    )
    out_specs = P(rows, "dp", None)
    return jax.shard_map(
        body, mesh=split_mesh, in_specs=in_specs, out_specs=out_specs, check_vma=False
    )
```

```python
import math

import jax
import jax.numpy as jnp
from jax import lax
from jax.sharding import PartitionSpec as P
from jax.experimental import pallas as pl
from jax.experimental.pallas import tpu as pltpu

MODEL_WIDTH = 1536
HEAD_SIZE = 96
FRESH_TOKENS = 512
WINDOW_SPAN = 4096
SINKS = 4
PROMPT_TOKENS = 4096


rope_base = 10000.0
epsilon = 1e-05
far_below = -1e30


def norm_rows(values, gain_vec):
    widened = values.astype(jnp.float32)
    factor = lax.rsqrt(jnp.mean(widened * widened, axis=-1, keepdims=True) + epsilon)
    return (widened * factor * gain_vec).astype(jnp.bfloat16)


def rotate(values, positions):
    half_dim = values.shape[-1] // 2
    frequency = rope_base ** (-2.0 * jnp.arange(half_dim, dtype=jnp.float32) / values.shape[-1])
    angles = positions.astype(jnp.float32)[..., None, None] * frequency
    cosine = jnp.cos(angles)
    sine_part = jnp.sin(angles)
    first_half = values[..., :half_dim]
    second_half = values[..., half_dim:]
    return jnp.concatenate(
        [
            first_half * cosine - second_half * sine_part,
            second_half * cosine + first_half * sine_part,
        ],
        axis=-1,
    )


KEY_BLOCK = 512


def absorber(q_ref, peak, total, acc):
    score_scale = 1.0 / math.sqrt(HEAD_SIZE)

    def absorb(keys, values, visible, flipped=False):
        scores = (
            lax.dot_general(
                q_ref[0],
                keys,
                (((1,), (0 if flipped else 1,)), ((), ())),
                preferred_element_type=jnp.float32,
            )
            * score_scale
        )
        if visible is not None:
            scores = jnp.where(visible, scores, -jnp.inf)
        old_peak = peak[0]
        new_peak = jnp.maximum(old_peak, jnp.max(scores, axis=-1, keepdims=True))
        factor = jnp.exp(old_peak - new_peak)
        weights = jnp.exp(scores - new_peak)
        total[0] = total[0] * factor + jnp.sum(weights, axis=-1, keepdims=True)
        acc[0] = acc[0] * factor + lax.dot_general(
            weights.astype(jnp.bfloat16),
            values,
            (((1,), (1 if flipped else 0,)), ((), ())),
            preferred_element_type=jnp.float32,
        )
        peak[0] = new_peak

    return absorb


def recent_kernel(length_ref, q_ref, wk_ref, wv_ref, nk_ref, nv_ref, acc, peak, total):
    request = pl.program_id(0)
    block = pl.program_id(1)
    length = length_ref[request]
    window_blocks = WINDOW_SPAN // KEY_BLOCK
    row_count = q_ref.shape[1]
    absorb = absorber(q_ref, peak, total, acc)

    @pl.when(block == 0)
    def _():
        peak[...] = jnp.full(peak.shape, far_below, jnp.float32)
        total[...] = jnp.zeros(total.shape, jnp.float32)
        acc[...] = jnp.zeros(acc.shape, jnp.float32)

    rows = lax.rem(lax.broadcasted_iota(jnp.int32, (row_count, KEY_BLOCK), 0), FRESH_TOKENS)
    cols = lax.broadcasted_iota(jnp.int32, (row_count, KEY_BLOCK), 1)
    window_start = block * KEY_BLOCK

    whole = (window_start >= WINDOW_SPAN - length) & (window_start >= FRESH_TOKENS)

    @pl.when(
        (block < window_blocks)
        & (window_start + KEY_BLOCK - 1 >= WINDOW_SPAN - length)
        & jnp.logical_not(whole)
    )
    def _():
        slot = window_start + cols
        absorb(wk_ref[0], wv_ref[0], (slot >= WINDOW_SPAN - length) & (slot > rows))

    @pl.when((block < window_blocks) & whole)
    def _():
        absorb(wk_ref[0], wv_ref[0], None)

    @pl.when(block == window_blocks)
    def _():
        absorb(nk_ref[0], nv_ref[0], cols <= rows)


def flip(block_ref):
    pieces = block_ref.shape[0]
    if pieces == 1:
        return block_ref[0, 0, 0]
    return jnp.concatenate([block_ref[piece, 0, 0] for piece in range(pieces)], axis=1)


def prompt_kernel(
    length_ref, q_ref, pk_ref, pv_ref, acc_in, peak_in, total_in, o_ref, acc, peak, total
):
    request = pl.program_id(0)
    block = pl.program_id(1)
    length = length_ref[request]
    prompt_blocks = PROMPT_TOKENS // KEY_BLOCK
    row_count = q_ref.shape[1]
    absorb = absorber(q_ref, peak, total, acc)

    @pl.when(block == 0)
    def _():
        peak[...] = peak_in[...]
        total[...] = total_in[...]
        acc[...] = acc_in[...]

    rows = lax.rem(lax.broadcasted_iota(jnp.int32, (row_count, KEY_BLOCK), 0), FRESH_TOKENS)
    cols = lax.broadcasted_iota(jnp.int32, (row_count, KEY_BLOCK), 1)
    prompt_start = block * KEY_BLOCK

    whole = prompt_start > length + FRESH_TOKENS - 1

    @pl.when(((block == 0) | (prompt_start + KEY_BLOCK - 1 > length)) & jnp.logical_not(whole))
    def _():
        spot = prompt_start + cols
        absorb(flip(pk_ref), flip(pv_ref), (spot < SINKS) | (spot > length + rows), True)

    @pl.when(whole)
    def _():
        absorb(flip(pk_ref), flip(pv_ref), None, True)

    @pl.when(block == prompt_blocks - 1)
    def _():
        o_ref[0] = (acc[0] / total[0]).astype(o_ref.dtype)


def attention(lengths, queries, prompt_kv, window_k, window_v, new_k, new_v):
    local_reqs, row_count, width = queries.shape
    prompt_blocks = PROMPT_TOKENS // KEY_BLOCK
    window_blocks = WINDOW_SPAN // KEY_BLOCK
    key_spec = lambda pick: pl.BlockSpec((1, KEY_BLOCK, width), pick)
    window_pick = lambda r, b, lens: (r, jnp.minimum(b, window_blocks - 1), 0)
    fixed_pick = lambda r, b, lens: (r, 0, 0)
    state_specs = [
        pl.BlockSpec((1, row_count, width), fixed_pick),
        pl.BlockSpec((1, row_count, 1), fixed_pick),
        pl.BlockSpec((1, row_count, 1), fixed_pick),
    ]
    state_shapes = [
        jax.ShapeDtypeStruct((local_reqs, row_count, width), jnp.float32),
        jax.ShapeDtypeStruct((local_reqs, row_count, 1), jnp.float32),
        jax.ShapeDtypeStruct((local_reqs, row_count, 1), jnp.float32),
    ]
    recent_keys = WINDOW_SPAN + FRESH_TOKENS
    state = pl.pallas_call(
        recent_kernel,
        grid_spec=pltpu.PrefetchScalarGridSpec(
            num_scalar_prefetch=1,
            grid=(local_reqs, window_blocks + 1),
            in_specs=[
                pl.BlockSpec((1, row_count, width), fixed_pick),
                key_spec(window_pick),
                key_spec(window_pick),
                key_spec(fixed_pick),
                key_spec(fixed_pick),
            ],
            out_specs=state_specs,
        ),
        out_shape=state_shapes,
        cost_estimate=pl.CostEstimate(
            flops=4 * local_reqs * row_count * recent_keys * width,
            transcendentals=local_reqs * row_count * recent_keys,
            bytes_accessed=4 * local_reqs * recent_keys * width,
        ),
    )(lengths, queries, window_k, window_v, new_k, new_v)

    prompt_kv = jnp.swapaxes(prompt_kv, 3, 4)
    source_rows = prompt_kv.shape[4]
    if source_rows <= KEY_BLOCK:
        prompt_spec = lambda half: pl.BlockSpec(
            (KEY_BLOCK // source_rows, 1, 1, width, source_rows),
            lambda r, b, lens: (b, r, half, 0, 0),
        )
    else:
        per_source = source_rows // KEY_BLOCK
        prompt_spec = lambda half: pl.BlockSpec(
            (1, 1, 1, width, KEY_BLOCK),
            lambda r, b, lens: (b // per_source, r, half, 0, b % per_source),
        )
    return pl.pallas_call(
        prompt_kernel,
        grid_spec=pltpu.PrefetchScalarGridSpec(
            num_scalar_prefetch=1,
            grid=(local_reqs, prompt_blocks),
            in_specs=[
                pl.BlockSpec((1, row_count, width), fixed_pick),
                prompt_spec(0),
                prompt_spec(1),
            ]
            + state_specs,
            out_specs=pl.BlockSpec((1, row_count, width), fixed_pick),
            scratch_shapes=[
                pltpu.VMEM((1, row_count, width), jnp.float32),
                pltpu.VMEM((1, row_count, 1), jnp.float32),
                pltpu.VMEM((1, row_count, 1), jnp.float32),
            ],
        ),
        out_shape=jax.ShapeDtypeStruct(queries.shape, jnp.bfloat16),
        cost_estimate=pl.CostEstimate(
            flops=4 * local_reqs * row_count * PROMPT_TOKENS * width,
            transcendentals=local_reqs * row_count * PROMPT_TOKENS,
            bytes_accessed=4 * local_reqs * PROMPT_TOKENS * width,
        ),
    )(lengths, queries, prompt_kv, prompt_kv, *state)


def exchange_kernel(piece_ref, other_ref, send_sem, recv_sem):
    partner = (
        lax.axis_index("dp"),
        1 - lax.axis_index("zh"),
        lax.axis_index("y"),
    )
    barrier = pltpu.get_barrier_semaphore()
    pl.semaphore_signal(
        barrier, 1, device_id=partner, device_id_type=pl.DeviceIdType.MESH
    )
    pl.semaphore_wait(barrier, 1)
    copy = pltpu.make_async_remote_copy(
        src_ref=piece_ref,
        dst_ref=other_ref,
        send_sem=send_sem,
        recv_sem=recv_sem,
        device_id=partner,
        device_id_type=pl.DeviceIdType.MESH,
    )
    copy.start()
    copy.wait()


def exchange(piece, call_id):
    return pl.pallas_call(
        exchange_kernel,
        out_shape=jax.ShapeDtypeStruct(piece.shape, piece.dtype),
        in_specs=[pl.BlockSpec(memory_space=pl.ANY)],
        out_specs=pl.BlockSpec(memory_space=pl.ANY),
        scratch_shapes=[pltpu.SemaphoreType.DMA, pltpu.SemaphoreType.DMA],
        compiler_params=pltpu.CompilerParams(collective_id=call_id, has_side_effects=True),
    )(piece)


def pair_rows(piece):
    upper = lax.axis_index("zh") == 1
    other = lax.ppermute(piece, "zh", perm=[(0, 1), (1, 0)])
    return jnp.stack([jnp.where(upper, other, piece), jnp.where(upper, piece, other)])


def gather_rows(pair):
    return lax.all_gather(pair, "y", axis=0, tiled=True).reshape((-1,) + pair.shape[2:])


def reduce_rows(full, call_id):
    y_size = lax.axis_size("y")
    zh_size = lax.axis_size("zh")
    split = full.reshape((y_size * zh_size, full.shape[0] // (y_size * zh_size)) + full.shape[1:])
    part = lax.psum_scatter(split, "y", scatter_dimension=0, tiled=True)
    return part.astype(jnp.float32) + exchange(part, call_id).astype(jnp.float32)


def scatter_rows(full, call_id):
    y_size = lax.axis_size("y")
    zh_size = lax.axis_size("zh")
    split = full.reshape((y_size * zh_size, full.shape[0] // (y_size * zh_size)) + full.shape[1:])
    part = lax.psum_scatter(split, "y", scatter_dimension=0, tiled=True)
    me = lax.axis_index("zh")
    mine = lax.dynamic_index_in_dim(part, me, 0, keepdims=False)
    outgoing = lax.dynamic_index_in_dim(part, 1 - me, 0, keepdims=False)
    return mine.astype(jnp.float32) + exchange(outgoing, call_id).astype(jnp.float32)


def prompt_for_requests(prompt_keys, prompt_values, prompt_group):
    dp_size = lax.axis_size("dp")
    wanted = lax.all_to_all(
        jnp.broadcast_to(prompt_group[None], (dp_size,) + prompt_group.shape), "dp", 0, 0, tiled=False
    )
    both = jnp.stack([prompt_keys, prompt_values], axis=1)
    outgoing = jnp.take(both, wanted, axis=0)
    return lax.all_to_all(outgoing, "dp", 0, 0, tiled=False)


def body(
    tokens,
    cached_len,
    prompt_group,
    attn_gain,
    w_query,
    key_matrix,
    value_matrix,
    w_out,
    window_cache_keys,
    window_cache_values,
    prompt_keys,
    prompt_values,
    mlp_gain,
    w_gate,
    w_up,
    w_down,
):
    local_rows = tokens.shape[0]
    local_reqs = tokens.shape[1]
    query_cols = w_query.shape[1]
    key_cols = key_matrix.shape[1]
    hidden_cols = w_gate.shape[1]
    key_heads = key_cols // HEAD_SIZE
    query_group_width = query_cols // key_cols
    score_scale = 1.0 / math.sqrt(HEAD_SIZE)
    token_pair = pair_rows(tokens.reshape(local_rows * local_reqs, MODEL_WIDTH))
    source = norm_rows(token_pair, attn_gain)
    offset = 0
    flattened_rows = gather_rows(source)
    row_count = flattened_rows.shape[0] // local_reqs
    y_size = lax.axis_size("y")
    zh_size = lax.axis_size("zh")
    block_rows = local_rows * local_reqs
    flat_row = jnp.arange(row_count * local_reqs, dtype=jnp.int32)
    block_of_row = flat_row // block_rows
    token_of_row = (
        (block_of_row % zh_size) * y_size + block_of_row // zh_size
    ) * local_rows + (flat_row % block_rows) // local_reqs
    positions = PROMPT_TOKENS + jnp.take(cached_len, flat_row % local_reqs) + token_of_row
    query_heads = query_cols // HEAD_SIZE
    project_queries = jnp.dot(flattened_rows, w_query, preferred_element_type=jnp.float32).reshape(
        row_count * local_reqs, query_heads, HEAD_SIZE
    )
    fresh_keys = jnp.dot(flattened_rows, key_matrix, preferred_element_type=jnp.float32).reshape(
        row_count * local_reqs, key_heads, HEAD_SIZE
    )
    fresh_values = jnp.dot(flattened_rows, value_matrix, preferred_element_type=jnp.float32).astype(
        jnp.bfloat16
    )
    project_queries = rotate(project_queries, positions).astype(jnp.bfloat16)
    fresh_keys = rotate(fresh_keys, positions).astype(jnp.bfloat16)
    grid_rows = (y_size, zh_size, local_rows, local_reqs)
    queries = (
        project_queries.reshape(grid_rows + (query_heads, HEAD_SIZE))
        .transpose(3, 4, 1, 0, 2, 5)
        .reshape(local_reqs, query_heads * row_count, HEAD_SIZE)
    )
    own_keys = (
        fresh_keys.reshape(grid_rows + (HEAD_SIZE,))
        .transpose(3, 1, 0, 2, 4)
        .reshape(local_reqs, row_count, HEAD_SIZE)
    )
    own_values = (
        fresh_values.reshape(grid_rows + (HEAD_SIZE,))
        .transpose(3, 1, 0, 2, 4)
        .reshape(local_reqs, row_count, HEAD_SIZE)
    )
    prompt_kv = prompt_for_requests(prompt_keys, prompt_values, prompt_group)
    attended = attention(
        cached_len, queries, prompt_kv, window_cache_keys, window_cache_values, own_keys, own_values
    )
    attended = (
        attended.reshape(local_reqs, query_heads, zh_size, y_size, local_rows, HEAD_SIZE)
        .transpose(3, 2, 4, 0, 1, 5)
        .reshape(row_count, local_reqs, query_cols)
    )
    picked = attended
    attn_pair = reduce_rows(
        jnp.dot(
            picked.reshape(FRESH_TOKENS * local_reqs, query_cols),
            w_out,
            preferred_element_type=jnp.float32,
        ).astype(jnp.bfloat16),
        1,
    )
    residual_pair = (token_pair.astype(jnp.float32) + attn_pair).astype(jnp.bfloat16)
    residual = lax.dynamic_index_in_dim(
        residual_pair, lax.axis_index("zh"), 0, keepdims=False
    ).reshape(tokens.shape)
    flattened_rows = gather_rows(norm_rows(residual_pair, mlp_gain))
    gate_part = jnp.dot(flattened_rows, w_gate, preferred_element_type=jnp.float32)
    up_part = jnp.dot(flattened_rows, w_up, preferred_element_type=jnp.float32)
    hidden = (jax.nn.silu(gate_part) * up_part).astype(jnp.bfloat16)
    mlp_part = scatter_rows(
        jnp.dot(hidden, w_down, preferred_element_type=jnp.float32).astype(jnp.bfloat16),
        3,
    ).reshape(tokens.shape)
    return (residual.astype(jnp.float32) + mlp_part).astype(jnp.bfloat16)


def solution(mesh):
    zh_size = 2
    split_mesh = jax.sharding.Mesh(
        mesh.devices.reshape(mesh.devices.shape[0], zh_size, -1), ("dp", "zh", "y")
    )
    rows = ("zh", "y")
    in_specs = (
        P(rows, "dp", None),
        P("dp"),
        P("dp"),
        P(),
        P(None, rows),
        P(None, rows),
        P(None, rows),
        P(rows, None),
        P("dp", None, rows),
        P("dp", None, rows),
        P(None, "dp", rows),
        P(None, "dp", rows),
        P(),
        P(None, rows),
        P(None, rows),
        P(rows, None),
    )
    out_specs = P(rows, "dp", None)
    return jax.shard_map(
        body, mesh=split_mesh, in_specs=in_specs, out_specs=out_specs, check_vma=False
    )
```

```python
import math

import jax
import jax.numpy as jnp
from jax import lax
from jax.sharding import PartitionSpec as P
from jax.experimental import pallas as pl
from jax.experimental.pallas import tpu as pltpu

MODEL_WIDTH = 1536
HEAD_SIZE = 96
FRESH_TOKENS = 512
WINDOW_SPAN = 4096
SINKS = 4
PROMPT_TOKENS = 4096


rope_base = 10000.0
epsilon = 1e-05
far_below = -1e30


def norm_rows(values, gain_vec):
    widened = values.astype(jnp.float32)
    factor = lax.rsqrt(jnp.mean(widened * widened, axis=-1, keepdims=True) + epsilon)
    return (widened * factor * gain_vec).astype(jnp.bfloat16)


def rotate(values, positions):
    half_dim = values.shape[-1] // 2
    frequency = rope_base ** (-2.0 * jnp.arange(half_dim, dtype=jnp.float32) / values.shape[-1])
    angles = positions.astype(jnp.float32)[..., None, None] * frequency
    cosine = jnp.cos(angles)
    sine_part = jnp.sin(angles)
    first_half = values[..., :half_dim]
    second_half = values[..., half_dim:]
    return jnp.concatenate(
        [
            first_half * cosine - second_half * sine_part,
            second_half * cosine + first_half * sine_part,
        ],
        axis=-1,
    )


KEY_BLOCK = 512


def absorber(q_ref, peak, total, acc):
    score_scale = 1.0 / math.sqrt(HEAD_SIZE)

    def absorb(keys, values, visible, flipped=False):
        scores = (
            lax.dot_general(
                q_ref[0],
                keys,
                (((1,), (0 if flipped else 1,)), ((), ())),
                preferred_element_type=jnp.float32,
            )
            * score_scale
        )
        if visible is not None:
            scores = jnp.where(visible, scores, -jnp.inf)
        old_peak = peak[0]
        new_peak = jnp.maximum(old_peak, jnp.max(scores, axis=-1, keepdims=True))
        factor = jnp.exp(old_peak - new_peak)
        weights = jnp.exp(scores - new_peak)
        total[0] = total[0] * factor + jnp.sum(weights, axis=-1, keepdims=True)
        acc[0] = acc[0] * factor + lax.dot_general(
            weights.astype(jnp.bfloat16),
            values,
            (((1,), (1 if flipped else 0,)), ((), ())),
            preferred_element_type=jnp.float32,
        )
        peak[0] = new_peak

    return absorb


def recent_kernel(length_ref, q_ref, wk_ref, wv_ref, nk_ref, nv_ref, acc, peak, total):
    request = pl.program_id(0)
    block = pl.program_id(1)
    length = length_ref[request]
    window_blocks = WINDOW_SPAN // KEY_BLOCK
    row_count = q_ref.shape[1]
    absorb = absorber(q_ref, peak, total, acc)

    @pl.when(block == 0)
    def _():
        peak[...] = jnp.full(peak.shape, far_below, jnp.float32)
        total[...] = jnp.zeros(total.shape, jnp.float32)
        acc[...] = jnp.zeros(acc.shape, jnp.float32)

    rows = lax.rem(lax.broadcasted_iota(jnp.int32, (row_count, KEY_BLOCK), 0), FRESH_TOKENS)
    cols = lax.broadcasted_iota(jnp.int32, (row_count, KEY_BLOCK), 1)
    window_start = block * KEY_BLOCK

    whole = (window_start >= WINDOW_SPAN - length) & (window_start >= FRESH_TOKENS)

    @pl.when(
        (block < window_blocks)
        & (window_start + KEY_BLOCK - 1 >= WINDOW_SPAN - length)
        & jnp.logical_not(whole)
    )
    def _():
        slot = window_start + cols
        absorb(wk_ref[0], wv_ref[0], (slot >= WINDOW_SPAN - length) & (slot > rows))

    @pl.when((block < window_blocks) & whole)
    def _():
        absorb(wk_ref[0], wv_ref[0], None)

    @pl.when(block == window_blocks)
    def _():
        absorb(nk_ref[0], nv_ref[0], cols <= rows)


def flip(block_ref):
    pieces = block_ref.shape[0]
    if pieces == 1:
        return block_ref[0, 0, 0]
    return jnp.concatenate([block_ref[piece, 0, 0] for piece in range(pieces)], axis=1)


def prompt_kernel(
    length_ref, q_ref, pk_ref, pv_ref, acc_in, peak_in, total_in, o_ref, acc, peak, total
):
    request = pl.program_id(0)
    block = pl.program_id(1)
    length = length_ref[request]
    prompt_blocks = PROMPT_TOKENS // KEY_BLOCK
    row_count = q_ref.shape[1]
    absorb = absorber(q_ref, peak, total, acc)

    @pl.when(block == 0)
    def _():
        peak[...] = peak_in[...]
        total[...] = total_in[...]
        acc[...] = acc_in[...]

    rows = lax.rem(lax.broadcasted_iota(jnp.int32, (row_count, KEY_BLOCK), 0), FRESH_TOKENS)
    cols = lax.broadcasted_iota(jnp.int32, (row_count, KEY_BLOCK), 1)
    prompt_start = block * KEY_BLOCK

    whole = prompt_start > length + FRESH_TOKENS - 1

    @pl.when(((block == 0) | (prompt_start + KEY_BLOCK - 1 > length)) & jnp.logical_not(whole))
    def _():
        spot = prompt_start + cols
        absorb(flip(pk_ref), flip(pv_ref), (spot < SINKS) | (spot > length + rows), True)

    @pl.when(whole)
    def _():
        absorb(flip(pk_ref), flip(pv_ref), None, True)

    @pl.when(block == prompt_blocks - 1)
    def _():
        o_ref[0] = (acc[0] / total[0]).astype(o_ref.dtype)


def attention(lengths, queries, prompt_kv, window_k, window_v, new_k, new_v):
    local_reqs, row_count, width = queries.shape
    prompt_blocks = PROMPT_TOKENS // KEY_BLOCK
    window_blocks = WINDOW_SPAN // KEY_BLOCK
    key_spec = lambda pick: pl.BlockSpec((1, KEY_BLOCK, width), pick)
    window_pick = lambda r, b, lens: (r, jnp.minimum(b, window_blocks - 1), 0)
    fixed_pick = lambda r, b, lens: (r, 0, 0)
    state_specs = [
        pl.BlockSpec((1, row_count, width), fixed_pick),
        pl.BlockSpec((1, row_count, 1), fixed_pick),
        pl.BlockSpec((1, row_count, 1), fixed_pick),
    ]
    state_shapes = [
        jax.ShapeDtypeStruct((local_reqs, row_count, width), jnp.float32),
        jax.ShapeDtypeStruct((local_reqs, row_count, 1), jnp.float32),
        jax.ShapeDtypeStruct((local_reqs, row_count, 1), jnp.float32),
    ]
    recent_keys = WINDOW_SPAN + FRESH_TOKENS
    state = pl.pallas_call(
        recent_kernel,
        grid_spec=pltpu.PrefetchScalarGridSpec(
            num_scalar_prefetch=1,
            grid=(local_reqs, window_blocks + 1),
            in_specs=[
                pl.BlockSpec((1, row_count, width), fixed_pick),
                key_spec(window_pick),
                key_spec(window_pick),
                key_spec(fixed_pick),
                key_spec(fixed_pick),
            ],
            out_specs=state_specs,
        ),
        out_shape=state_shapes,
        cost_estimate=pl.CostEstimate(
            flops=4 * local_reqs * row_count * recent_keys * width,
            transcendentals=local_reqs * row_count * recent_keys,
            bytes_accessed=4 * local_reqs * recent_keys * width,
        ),
    )(lengths, queries, window_k, window_v, new_k, new_v)

    prompt_kv = jnp.swapaxes(prompt_kv, 3, 4)
    source_rows = prompt_kv.shape[4]
    if source_rows <= KEY_BLOCK:
        prompt_spec = lambda half: pl.BlockSpec(
            (KEY_BLOCK // source_rows, 1, 1, width, source_rows),
            lambda r, b, lens: (b, r, half, 0, 0),
        )
    else:
        per_source = source_rows // KEY_BLOCK
        prompt_spec = lambda half: pl.BlockSpec(
            (1, 1, 1, width, KEY_BLOCK),
            lambda r, b, lens: (b // per_source, r, half, 0, b % per_source),
        )
    return pl.pallas_call(
        prompt_kernel,
        grid_spec=pltpu.PrefetchScalarGridSpec(
            num_scalar_prefetch=1,
            grid=(local_reqs, prompt_blocks),
            in_specs=[
                pl.BlockSpec((1, row_count, width), fixed_pick),
                prompt_spec(0),
                prompt_spec(1),
            ]
            + state_specs,
            out_specs=pl.BlockSpec((1, row_count, width), fixed_pick),
            scratch_shapes=[
                pltpu.VMEM((1, row_count, width), jnp.float32),
                pltpu.VMEM((1, row_count, 1), jnp.float32),
                pltpu.VMEM((1, row_count, 1), jnp.float32),
            ],
        ),
        out_shape=jax.ShapeDtypeStruct(queries.shape, jnp.bfloat16),
        cost_estimate=pl.CostEstimate(
            flops=4 * local_reqs * row_count * PROMPT_TOKENS * width,
            transcendentals=local_reqs * row_count * PROMPT_TOKENS,
            bytes_accessed=4 * local_reqs * PROMPT_TOKENS * width,
        ),
    )(lengths, queries, prompt_kv, prompt_kv, *state)


def exchange_kernel(piece_ref, other_ref, send_sem, recv_sem):
    partner = (
        lax.axis_index("dp"),
        1 - lax.axis_index("zh"),
        lax.axis_index("y"),
    )
    barrier = pltpu.get_barrier_semaphore()
    pl.semaphore_signal(
        barrier, 1, device_id=partner, device_id_type=pl.DeviceIdType.MESH
    )
    pl.semaphore_wait(barrier, 1)
    copy = pltpu.make_async_remote_copy(
        src_ref=piece_ref,
        dst_ref=other_ref,
        send_sem=send_sem,
        recv_sem=recv_sem,
        device_id=partner,
        device_id_type=pl.DeviceIdType.MESH,
    )
    copy.start()
    copy.wait()


def exchange(piece, call_id):
    return pl.pallas_call(
        exchange_kernel,
        out_shape=jax.ShapeDtypeStruct(piece.shape, piece.dtype),
        in_specs=[pl.BlockSpec(memory_space=pl.ANY)],
        out_specs=pl.BlockSpec(memory_space=pl.ANY),
        scratch_shapes=[pltpu.SemaphoreType.DMA, pltpu.SemaphoreType.DMA],
        compiler_params=pltpu.CompilerParams(collective_id=call_id, has_side_effects=True),
    )(piece)


def pair_rows(piece):
    upper = lax.axis_index("zh") == 1
    other = lax.ppermute(piece, "zh", perm=[(0, 1), (1, 0)])
    return jnp.stack([jnp.where(upper, other, piece), jnp.where(upper, piece, other)])


def gather_rows(pair):
    return lax.all_gather(pair, "y", axis=0, tiled=True).reshape((-1,) + pair.shape[2:])


def reduce_rows(full, call_id):
    y_size = lax.axis_size("y")
    zh_size = lax.axis_size("zh")
    split = full.reshape((y_size * zh_size, full.shape[0] // (y_size * zh_size)) + full.shape[1:])
    part = lax.psum_scatter(split, "y", scatter_dimension=0, tiled=True)
    return part.astype(jnp.float32) + lax.ppermute(part, "zh", perm=[(0, 1), (1, 0)]).astype(jnp.float32)


def scatter_rows(full, call_id):
    y_size = lax.axis_size("y")
    zh_size = lax.axis_size("zh")
    split = full.reshape((y_size * zh_size, full.shape[0] // (y_size * zh_size)) + full.shape[1:])
    part = lax.psum_scatter(split, "y", scatter_dimension=0, tiled=True)
    me = lax.axis_index("zh")
    mine = lax.dynamic_index_in_dim(part, me, 0, keepdims=False)
    outgoing = lax.dynamic_index_in_dim(part, 1 - me, 0, keepdims=False)
    return mine.astype(jnp.float32) + lax.ppermute(outgoing, "zh", perm=[(0, 1), (1, 0)]).astype(
        jnp.float32
    )


def prompt_for_requests(prompt_keys, prompt_values, prompt_group):
    dp_size = lax.axis_size("dp")
    wanted = lax.all_to_all(
        jnp.broadcast_to(prompt_group[None], (dp_size,) + prompt_group.shape), "dp", 0, 0, tiled=False
    )
    both = jnp.stack([prompt_keys, prompt_values], axis=1)
    outgoing = jnp.take(both, wanted, axis=0)
    return lax.all_to_all(outgoing, "dp", 0, 0, tiled=False)


def body(
    tokens,
    cached_len,
    prompt_group,
    attn_gain,
    w_query,
    key_matrix,
    value_matrix,
    w_out,
    window_cache_keys,
    window_cache_values,
    prompt_keys,
    prompt_values,
    mlp_gain,
    w_gate,
    w_up,
    w_down,
):
    local_rows = tokens.shape[0]
    local_reqs = tokens.shape[1]
    query_cols = w_query.shape[1]
    key_cols = key_matrix.shape[1]
    hidden_cols = w_gate.shape[1]
    key_heads = key_cols // HEAD_SIZE
    query_group_width = query_cols // key_cols
    score_scale = 1.0 / math.sqrt(HEAD_SIZE)
    token_pair = pair_rows(tokens.reshape(local_rows * local_reqs, MODEL_WIDTH))
    source = norm_rows(token_pair, attn_gain)
    offset = 0
    flattened_rows = gather_rows(source)
    row_count = flattened_rows.shape[0] // local_reqs
    y_size = lax.axis_size("y")
    zh_size = lax.axis_size("zh")
    block_rows = local_rows * local_reqs
    flat_row = jnp.arange(row_count * local_reqs, dtype=jnp.int32)
    block_of_row = flat_row // block_rows
    token_of_row = (
        (block_of_row % zh_size) * y_size + block_of_row // zh_size
    ) * local_rows + (flat_row % block_rows) // local_reqs
    positions = PROMPT_TOKENS + jnp.take(cached_len, flat_row % local_reqs) + token_of_row
    query_heads = query_cols // HEAD_SIZE
    project_queries = jnp.dot(flattened_rows, w_query, preferred_element_type=jnp.float32).reshape(
        row_count * local_reqs, query_heads, HEAD_SIZE
    )
    fresh_keys = jnp.dot(flattened_rows, key_matrix, preferred_element_type=jnp.float32).reshape(
        row_count * local_reqs, key_heads, HEAD_SIZE
    )
    fresh_values = jnp.dot(flattened_rows, value_matrix, preferred_element_type=jnp.float32).astype(
        jnp.bfloat16
    )
    project_queries = rotate(project_queries, positions).astype(jnp.bfloat16)
    fresh_keys = rotate(fresh_keys, positions).astype(jnp.bfloat16)
    grid_rows = (y_size, zh_size, local_rows, local_reqs)
    queries = (
        project_queries.reshape(grid_rows + (query_heads, HEAD_SIZE))
        .transpose(3, 4, 1, 0, 2, 5)
        .reshape(local_reqs, query_heads * row_count, HEAD_SIZE)
    )
    own_keys = (
        fresh_keys.reshape(grid_rows + (HEAD_SIZE,))
        .transpose(3, 1, 0, 2, 4)
        .reshape(local_reqs, row_count, HEAD_SIZE)
    )
    own_values = (
        fresh_values.reshape(grid_rows + (HEAD_SIZE,))
        .transpose(3, 1, 0, 2, 4)
        .reshape(local_reqs, row_count, HEAD_SIZE)
    )
    prompt_kv = prompt_for_requests(prompt_keys, prompt_values, prompt_group)
    attended = attention(
        cached_len, queries, prompt_kv, window_cache_keys, window_cache_values, own_keys, own_values
    )
    attended = (
        attended.reshape(local_reqs, query_heads, zh_size, y_size, local_rows, HEAD_SIZE)
        .transpose(3, 2, 4, 0, 1, 5)
        .reshape(row_count, local_reqs, query_cols)
    )
    picked = attended
    attn_pair = reduce_rows(
        jnp.dot(
            picked.reshape(FRESH_TOKENS * local_reqs, query_cols),
            w_out,
            preferred_element_type=jnp.float32,
        ).astype(jnp.bfloat16),
        1,
    )
    residual_pair = (token_pair.astype(jnp.float32) + attn_pair).astype(jnp.bfloat16)
    residual = lax.dynamic_index_in_dim(
        residual_pair, lax.axis_index("zh"), 0, keepdims=False
    ).reshape(tokens.shape)
    flattened_rows = gather_rows(norm_rows(residual_pair, mlp_gain))
    gate_part = jnp.dot(flattened_rows, w_gate, preferred_element_type=jnp.float32)
    up_part = jnp.dot(flattened_rows, w_up, preferred_element_type=jnp.float32)
    hidden = (jax.nn.silu(gate_part) * up_part).astype(jnp.bfloat16)
    mlp_part = scatter_rows(
        jnp.dot(hidden, w_down, preferred_element_type=jnp.float32).astype(jnp.bfloat16),
        3,
    ).reshape(tokens.shape)
    return (residual.astype(jnp.float32) + mlp_part).astype(jnp.bfloat16)


def solution(mesh):
    zh_size = 2
    split_mesh = jax.sharding.Mesh(
        mesh.devices.reshape(mesh.devices.shape[0], zh_size, -1), ("dp", "zh", "y")
    )
    rows = ("zh", "y")
    in_specs = (
        P(rows, "dp", None),
        P("dp"),
        P("dp"),
        P(),
        P(None, rows),
        P(None, rows),
        P(None, rows),
        P(rows, None),
        P("dp", None, rows),
        P("dp", None, rows),
        P(None, "dp", rows),
        P(None, "dp", rows),
        P(),
        P(None, rows),
        P(None, rows),
        P(rows, None),
    )
    out_specs = P(rows, "dp", None)
    return jax.shard_map(
        body, mesh=split_mesh, in_specs=in_specs, out_specs=out_specs, check_vma=False
    )
```

```python
import math

import jax
import jax.numpy as jnp
from jax import lax
from jax.sharding import PartitionSpec as P
from jax.experimental import pallas as pl
from jax.experimental.pallas import tpu as pltpu

MODEL_WIDTH = 1536
HEAD_SIZE = 96
FRESH_TOKENS = 512
WINDOW_SPAN = 4096
SINKS = 4
PROMPT_TOKENS = 4096


rope_base = 10000.0
epsilon = 1e-05
far_below = -1e30


def norm_rows(values, gain_vec):
    widened = values.astype(jnp.float32)
    factor = lax.rsqrt(jnp.mean(widened * widened, axis=-1, keepdims=True) + epsilon)
    return (widened * factor * gain_vec).astype(jnp.bfloat16)


def rotate(values, positions):
    half_dim = values.shape[-1] // 2
    frequency = rope_base ** (-2.0 * jnp.arange(half_dim, dtype=jnp.float32) / values.shape[-1])
    angles = positions.astype(jnp.float32)[..., None, None] * frequency
    cosine = jnp.cos(angles)
    sine_part = jnp.sin(angles)
    first_half = values[..., :half_dim]
    second_half = values[..., half_dim:]
    return jnp.concatenate(
        [
            first_half * cosine - second_half * sine_part,
            second_half * cosine + first_half * sine_part,
        ],
        axis=-1,
    )


KEY_BLOCK = 1024


def absorber(q_ref, peak, total, acc):
    score_scale = 1.0 / math.sqrt(HEAD_SIZE)

    def absorb(keys, values, visible, flipped=False):
        scores = (
            lax.dot_general(
                q_ref[0],
                keys,
                (((1,), (0 if flipped else 1,)), ((), ())),
                preferred_element_type=jnp.float32,
            )
            * score_scale
        )
        if visible is not None:
            scores = jnp.where(visible, scores, -jnp.inf)
        old_peak = peak[0]
        new_peak = jnp.maximum(old_peak, jnp.max(scores, axis=-1, keepdims=True))
        factor = jnp.exp(old_peak - new_peak)
        weights = jnp.exp(scores - new_peak)
        total[0] = total[0] * factor + jnp.sum(weights, axis=-1, keepdims=True)
        acc[0] = acc[0] * factor + lax.dot_general(
            weights.astype(jnp.bfloat16),
            values,
            (((1,), (1 if flipped else 0,)), ((), ())),
            preferred_element_type=jnp.float32,
        )
        peak[0] = new_peak

    return absorb


def recent_kernel(length_ref, q_ref, wk_ref, wv_ref, nk_ref, nv_ref, acc, peak, total):
    request = pl.program_id(0)
    block = pl.program_id(1)
    length = length_ref[request]
    window_blocks = WINDOW_SPAN // KEY_BLOCK
    row_count = q_ref.shape[1]
    absorb = absorber(q_ref, peak, total, acc)

    @pl.when(block == 0)
    def _():
        peak[...] = jnp.full(peak.shape, far_below, jnp.float32)
        total[...] = jnp.zeros(total.shape, jnp.float32)
        acc[...] = jnp.zeros(acc.shape, jnp.float32)

    rows = lax.rem(lax.broadcasted_iota(jnp.int32, (row_count, KEY_BLOCK), 0), FRESH_TOKENS)
    cols = lax.broadcasted_iota(jnp.int32, (row_count, KEY_BLOCK), 1)
    window_start = block * KEY_BLOCK

    whole = (window_start >= WINDOW_SPAN - length) & (window_start >= FRESH_TOKENS)

    @pl.when(
        (block < window_blocks)
        & (window_start + KEY_BLOCK - 1 >= WINDOW_SPAN - length)
        & jnp.logical_not(whole)
    )
    def _():
        slot = window_start + cols
        absorb(wk_ref[0], wv_ref[0], (slot >= WINDOW_SPAN - length) & (slot > rows))

    @pl.when((block < window_blocks) & whole)
    def _():
        absorb(wk_ref[0], wv_ref[0], None)

    @pl.when(block == window_blocks)
    def _():
        fresh_shape = (row_count, FRESH_TOKENS)
        fresh_rows = lax.rem(lax.broadcasted_iota(jnp.int32, fresh_shape, 0), FRESH_TOKENS)
        absorb(nk_ref[0], nv_ref[0], lax.broadcasted_iota(jnp.int32, fresh_shape, 1) <= fresh_rows)


def flip(block_ref):
    pieces = block_ref.shape[0]
    if pieces == 1:
        return block_ref[0, 0, 0]
    return jnp.concatenate([block_ref[piece, 0, 0] for piece in range(pieces)], axis=1)


def prompt_kernel(
    length_ref, q_ref, pk_ref, pv_ref, acc_in, peak_in, total_in, o_ref, acc, peak, total
):
    request = pl.program_id(0)
    block = pl.program_id(1)
    length = length_ref[request]
    prompt_blocks = PROMPT_TOKENS // KEY_BLOCK
    row_count = q_ref.shape[1]
    absorb = absorber(q_ref, peak, total, acc)

    @pl.when(block == 0)
    def _():
        peak[...] = peak_in[...]
        total[...] = total_in[...]
        acc[...] = acc_in[...]

    rows = lax.rem(lax.broadcasted_iota(jnp.int32, (row_count, KEY_BLOCK), 0), FRESH_TOKENS)
    cols = lax.broadcasted_iota(jnp.int32, (row_count, KEY_BLOCK), 1)
    prompt_start = block * KEY_BLOCK

    whole = prompt_start > length + FRESH_TOKENS - 1

    @pl.when(((block == 0) | (prompt_start + KEY_BLOCK - 1 > length)) & jnp.logical_not(whole))
    def _():
        spot = prompt_start + cols
        absorb(flip(pk_ref), flip(pv_ref), (spot < SINKS) | (spot > length + rows), True)

    @pl.when(whole)
    def _():
        absorb(flip(pk_ref), flip(pv_ref), None, True)

    @pl.when(block == prompt_blocks - 1)
    def _():
        o_ref[0] = (acc[0] / total[0]).astype(o_ref.dtype)


def attention(lengths, queries, prompt_kv, window_k, window_v, new_k, new_v):
    local_reqs, row_count, width = queries.shape
    prompt_blocks = PROMPT_TOKENS // KEY_BLOCK
    window_blocks = WINDOW_SPAN // KEY_BLOCK
    key_spec = lambda pick: pl.BlockSpec((1, KEY_BLOCK, width), pick)
    window_pick = lambda r, b, lens: (r, jnp.minimum(b, window_blocks - 1), 0)
    fixed_pick = lambda r, b, lens: (r, 0, 0)
    state_specs = [
        pl.BlockSpec((1, row_count, width), fixed_pick),
        pl.BlockSpec((1, row_count, 1), fixed_pick),
        pl.BlockSpec((1, row_count, 1), fixed_pick),
    ]
    state_shapes = [
        jax.ShapeDtypeStruct((local_reqs, row_count, width), jnp.float32),
        jax.ShapeDtypeStruct((local_reqs, row_count, 1), jnp.float32),
        jax.ShapeDtypeStruct((local_reqs, row_count, 1), jnp.float32),
    ]
    recent_keys = WINDOW_SPAN + FRESH_TOKENS
    state = pl.pallas_call(
        recent_kernel,
        grid_spec=pltpu.PrefetchScalarGridSpec(
            num_scalar_prefetch=1,
            grid=(local_reqs, window_blocks + 1),
            in_specs=[
                pl.BlockSpec((1, row_count, width), fixed_pick),
                key_spec(window_pick),
                key_spec(window_pick),
                pl.BlockSpec((1, FRESH_TOKENS, width), fixed_pick),
                pl.BlockSpec((1, FRESH_TOKENS, width), fixed_pick),
            ],
            out_specs=state_specs,
        ),
        out_shape=state_shapes,
        cost_estimate=pl.CostEstimate(
            flops=4 * local_reqs * row_count * recent_keys * width,
            transcendentals=local_reqs * row_count * recent_keys,
            bytes_accessed=4 * local_reqs * recent_keys * width,
        ),
    )(lengths, queries, window_k, window_v, new_k, new_v)

    prompt_kv = jnp.swapaxes(prompt_kv, 3, 4)
    source_rows = prompt_kv.shape[4]
    if source_rows <= KEY_BLOCK:
        prompt_spec = lambda half: pl.BlockSpec(
            (KEY_BLOCK // source_rows, 1, 1, width, source_rows),
            lambda r, b, lens: (b, r, half, 0, 0),
        )
    else:
        per_source = source_rows // KEY_BLOCK
        prompt_spec = lambda half: pl.BlockSpec(
            (1, 1, 1, width, KEY_BLOCK),
            lambda r, b, lens: (b // per_source, r, half, 0, b % per_source),
        )
    return pl.pallas_call(
        prompt_kernel,
        grid_spec=pltpu.PrefetchScalarGridSpec(
            num_scalar_prefetch=1,
            grid=(local_reqs, prompt_blocks),
            in_specs=[
                pl.BlockSpec((1, row_count, width), fixed_pick),
                prompt_spec(0),
                prompt_spec(1),
            ]
            + state_specs,
            out_specs=pl.BlockSpec((1, row_count, width), fixed_pick),
            scratch_shapes=[
                pltpu.VMEM((1, row_count, width), jnp.float32),
                pltpu.VMEM((1, row_count, 1), jnp.float32),
                pltpu.VMEM((1, row_count, 1), jnp.float32),
            ],
        ),
        out_shape=jax.ShapeDtypeStruct(queries.shape, jnp.bfloat16),
        cost_estimate=pl.CostEstimate(
            flops=4 * local_reqs * row_count * PROMPT_TOKENS * width,
            transcendentals=local_reqs * row_count * PROMPT_TOKENS,
            bytes_accessed=4 * local_reqs * PROMPT_TOKENS * width,
        ),
    )(lengths, queries, prompt_kv, prompt_kv, *state)


def exchange_kernel(piece_ref, other_ref, send_sem, recv_sem):
    partner = (
        lax.axis_index("dp"),
        1 - lax.axis_index("zh"),
        lax.axis_index("y"),
    )
    barrier = pltpu.get_barrier_semaphore()
    pl.semaphore_signal(
        barrier, 1, device_id=partner, device_id_type=pl.DeviceIdType.MESH
    )
    pl.semaphore_wait(barrier, 1)
    copy = pltpu.make_async_remote_copy(
        src_ref=piece_ref,
        dst_ref=other_ref,
        send_sem=send_sem,
        recv_sem=recv_sem,
        device_id=partner,
        device_id_type=pl.DeviceIdType.MESH,
    )
    copy.start()
    copy.wait()


def exchange(piece, call_id):
    return pl.pallas_call(
        exchange_kernel,
        out_shape=jax.ShapeDtypeStruct(piece.shape, piece.dtype),
        in_specs=[pl.BlockSpec(memory_space=pl.ANY)],
        out_specs=pl.BlockSpec(memory_space=pl.ANY),
        scratch_shapes=[pltpu.SemaphoreType.DMA, pltpu.SemaphoreType.DMA],
        compiler_params=pltpu.CompilerParams(collective_id=call_id, has_side_effects=True),
    )(piece)


def pair_rows(piece):
    upper = lax.axis_index("zh") == 1
    other = lax.ppermute(piece, "zh", perm=[(0, 1), (1, 0)])
    return jnp.stack([jnp.where(upper, other, piece), jnp.where(upper, piece, other)])


def gather_rows(pair):
    return lax.all_gather(pair, "y", axis=0, tiled=True).reshape((-1,) + pair.shape[2:])


def reduce_rows(full, call_id):
    y_size = lax.axis_size("y")
    zh_size = lax.axis_size("zh")
    split = full.reshape((y_size * zh_size, full.shape[0] // (y_size * zh_size)) + full.shape[1:])
    part = lax.psum_scatter(split, "y", scatter_dimension=0, tiled=True)
    return part.astype(jnp.float32) + exchange(part, call_id).astype(jnp.float32)


def scatter_rows(full, call_id):
    y_size = lax.axis_size("y")
    zh_size = lax.axis_size("zh")
    split = full.reshape((y_size * zh_size, full.shape[0] // (y_size * zh_size)) + full.shape[1:])
    part = lax.psum_scatter(split, "y", scatter_dimension=0, tiled=True)
    me = lax.axis_index("zh")
    mine = lax.dynamic_index_in_dim(part, me, 0, keepdims=False)
    outgoing = lax.dynamic_index_in_dim(part, 1 - me, 0, keepdims=False)
    return mine.astype(jnp.float32) + exchange(outgoing, call_id).astype(jnp.float32)


def prompt_for_requests(prompt_keys, prompt_values, prompt_group):
    dp_size = lax.axis_size("dp")
    wanted = lax.all_to_all(
        jnp.broadcast_to(prompt_group[None], (dp_size,) + prompt_group.shape), "dp", 0, 0, tiled=False
    )
    both = jnp.stack([prompt_keys, prompt_values], axis=1)
    outgoing = jnp.take(both, wanted, axis=0)
    return lax.all_to_all(outgoing, "dp", 0, 0, tiled=False)


def body(
    tokens,
    cached_len,
    prompt_group,
    attn_gain,
    w_query,
    key_matrix,
    value_matrix,
    w_out,
    window_cache_keys,
    window_cache_values,
    prompt_keys,
    prompt_values,
    mlp_gain,
    w_gate,
    w_up,
    w_down,
):
    local_rows = tokens.shape[0]
    local_reqs = tokens.shape[1]
    query_cols = w_query.shape[1]
    key_cols = key_matrix.shape[1]
    hidden_cols = w_gate.shape[1]
    key_heads = key_cols // HEAD_SIZE
    query_group_width = query_cols // key_cols
    score_scale = 1.0 / math.sqrt(HEAD_SIZE)
    token_pair = pair_rows(tokens.reshape(local_rows * local_reqs, MODEL_WIDTH))
    source = norm_rows(token_pair, attn_gain)
    offset = 0
    flattened_rows = gather_rows(source)
    row_count = flattened_rows.shape[0] // local_reqs
    y_size = lax.axis_size("y")
    zh_size = lax.axis_size("zh")
    block_rows = local_rows * local_reqs
    flat_row = jnp.arange(row_count * local_reqs, dtype=jnp.int32)
    block_of_row = flat_row // block_rows
    token_of_row = (
        (block_of_row % zh_size) * y_size + block_of_row // zh_size
    ) * local_rows + (flat_row % block_rows) // local_reqs
    positions = PROMPT_TOKENS + jnp.take(cached_len, flat_row % local_reqs) + token_of_row
    query_heads = query_cols // HEAD_SIZE
    project_queries = jnp.dot(flattened_rows, w_query, preferred_element_type=jnp.float32).reshape(
        row_count * local_reqs, query_heads, HEAD_SIZE
    )
    fresh_keys = jnp.dot(flattened_rows, key_matrix, preferred_element_type=jnp.float32).reshape(
        row_count * local_reqs, key_heads, HEAD_SIZE
    )
    fresh_values = jnp.dot(flattened_rows, value_matrix, preferred_element_type=jnp.float32).astype(
        jnp.bfloat16
    )
    project_queries = rotate(project_queries, positions).astype(jnp.bfloat16)
    fresh_keys = rotate(fresh_keys, positions).astype(jnp.bfloat16)
    grid_rows = (y_size, zh_size, local_rows, local_reqs)
    queries = (
        project_queries.reshape(grid_rows + (query_heads, HEAD_SIZE))
        .transpose(3, 4, 1, 0, 2, 5)
        .reshape(local_reqs, query_heads * row_count, HEAD_SIZE)
    )
    own_keys = (
        fresh_keys.reshape(grid_rows + (HEAD_SIZE,))
        .transpose(3, 1, 0, 2, 4)
        .reshape(local_reqs, row_count, HEAD_SIZE)
    )
    own_values = (
        fresh_values.reshape(grid_rows + (HEAD_SIZE,))
        .transpose(3, 1, 0, 2, 4)
        .reshape(local_reqs, row_count, HEAD_SIZE)
    )
    prompt_kv = prompt_for_requests(prompt_keys, prompt_values, prompt_group)
    attended = attention(
        cached_len, queries, prompt_kv, window_cache_keys, window_cache_values, own_keys, own_values
    )
    attended = (
        attended.reshape(local_reqs, query_heads, zh_size, y_size, local_rows, HEAD_SIZE)
        .transpose(3, 2, 4, 0, 1, 5)
        .reshape(row_count, local_reqs, query_cols)
    )
    picked = attended
    attn_pair = reduce_rows(
        jnp.dot(
            picked.reshape(FRESH_TOKENS * local_reqs, query_cols),
            w_out,
            preferred_element_type=jnp.float32,
        ).astype(jnp.bfloat16),
        1,
    )
    residual_pair = (token_pair.astype(jnp.float32) + attn_pair).astype(jnp.bfloat16)
    residual = lax.dynamic_index_in_dim(
        residual_pair, lax.axis_index("zh"), 0, keepdims=False
    ).reshape(tokens.shape)
    flattened_rows = gather_rows(norm_rows(residual_pair, mlp_gain))
    gate_part = jnp.dot(flattened_rows, w_gate, preferred_element_type=jnp.float32)
    up_part = jnp.dot(flattened_rows, w_up, preferred_element_type=jnp.float32)
    hidden = (jax.nn.silu(gate_part) * up_part).astype(jnp.bfloat16)
    mlp_part = scatter_rows(
        jnp.dot(hidden, w_down, preferred_element_type=jnp.float32).astype(jnp.bfloat16),
        3,
    ).reshape(tokens.shape)
    return (residual.astype(jnp.float32) + mlp_part).astype(jnp.bfloat16)


def solution(mesh):
    zh_size = 2
    split_mesh = jax.sharding.Mesh(
        mesh.devices.reshape(mesh.devices.shape[0], zh_size, -1), ("dp", "zh", "y")
    )
    rows = ("zh", "y")
    in_specs = (
        P(rows, "dp", None),
        P("dp"),
        P("dp"),
        P(),
        P(None, rows),
        P(None, rows),
        P(None, rows),
        P(rows, None),
        P("dp", None, rows),
        P("dp", None, rows),
        P(None, "dp", rows),
        P(None, "dp", rows),
        P(),
        P(None, rows),
        P(None, rows),
        P(rows, None),
    )
    out_specs = P(rows, "dp", None)
    return jax.shard_map(
        body, mesh=split_mesh, in_specs=in_specs, out_specs=out_specs, check_vma=False
    )
```
